128 devices in a mesh: ctx: 32 (over x, y, z_lo), tp: 4 (over z_hi, core).
Axes of the slice: x: 4, y: 4, z: 4 (z_hi: 2, z_lo: 2; z = z_hi * 2 + z_lo), core: 2. Of those that a mesh axis runs over, the one named last changes fastest.
Arguments:
- block_input: bfloat16 [4096, 1024], P(('ctx', 'tp')), may hold values from -6 to 6
- block_map: int32 [32], replicated, may hold values from 0 to 31, each once
- attn_gain: float32 [1024], replicated, may hold values from 0.1 to 1.9
- query_weight: bfloat16 [1024, 1024], P(None, 'tp'), may hold values from -0.1875 to 0.1875
- key_weight: bfloat16 [1024, 512], P(None, 'tp'), may hold values from -0.1875 to 0.1875
- value_weight: bfloat16 [1024, 512], P(None, 'tp'), may hold values from -0.1875 to 0.1875
- query_gain: float32 [64], replicated, may hold values from 0.5 to 2
- key_gain: float32 [64], replicated, may hold values from 0.5 to 2
- output_weight: bfloat16 [1024, 1024], P('tp'), may hold values from -3 to 3
- ffn_gain: float32 [1024], replicated, may hold values from 0.1 to 1.9
- gate_weight: bfloat16 [1024, 4608], P(None, 'tp'), may hold values from -0.1875 to 0.1875
- up_weight: bfloat16 [1024, 4608], P(None, 'tp'), may hold values from -0.1875 to 0.1875
- down_weight: bfloat16 [4608, 1024], P('tp'), may hold values from -0.09375 to 0.09375
- cotangent: bfloat16 [4096, 1024], P(('ctx', 'tp')), may hold values from -6 to 6
Outputs:
- block_output: float32 [4096, 1024], P(('ctx', 'tp'))
- input_grad: float32 [4096, 1024], P(('ctx', 'tp'))
- grad_attn_gain: float32 [1024], replicated
- grad_query: float32 [1024, 1024], P(None, 'tp')
- grad_key: float32 [1024, 512], P(None, 'tp')
- grad_value: float32 [1024, 512], P(None, 'tp')
- grad_query_gain: float32 [64], replicated
- grad_key_gain: float32 [64], replicated
- grad_output: float32 [1024, 1024], P('tp')
- grad_ffn_gain: float32 [1024], replicated
- grad_gate: float32 [1024, 4608], P(None, 'tp')
- grad_up: float32 [1024, 4608], P(None, 'tp')
- grad_down: float32 [4608, 1024], P('tp')
The draws below stay inside these ranges and needn't reach their ends.
Inputs may be any that keep to these rules, and one draw needn't show every extreme that they name: Each value appears once; ctx index e holds, for sequence 0 and then sequence 1, the position blocks block_map[e] and 63 - block_map[e] of 32 tokens each, in that order.
All inputs are finite; a program needn't handle non-finite values.
Results may differ from the reference program's by a relative error of at most 0.034.
Values may be sent and summed in bfloat16 or wider, within the bound.
A program may use at most 128 MiB of HBM per device.

```python
import math
import jax
import jax.numpy as jnp
from jax import lax

D = 1024
HEADS = 16
KV_HEADS = 8
HD = 64
FF = 4608
TOK_DEV = 128
BLOCK_LEN = 32
SEQ_LEN = 2048
TOKENS = 4096
N_CTX = 32


def steps_of(own_key, extent, split, low, largest):
    def one(dim, shards_of):
        heights = jax.random.uniform(jax.random.fold_in(jax.random.fold_in(own_key, 6), dim), (shards_of,), jnp.float32, low / len(split), largest / len(split))
        return jnp.repeat(jnp.exp(heights), extent[dim] // shards_of).reshape((-1,) + (1,) * (len(extent) - dim - 1))

    level = one(*split[0])
    for cut in split[1:]:
        level = level * one(*cut)
    return level


def noise(key, extent, deviation, reach, cuts=(), held_as=jnp.bfloat16):
    gain = steps_of(key, extent, cuts, -0.22, 0.18) if cuts else 1.0
    values = jax.random.normal(key, extent, jnp.float32) * deviation * gain
    return jnp.minimum(jnp.maximum(values, -reach), reach).astype(held_as)


def setup_inputs(seed: int = 0) -> dict:
    arg_keys = jax.random.split(jax.random.key(seed), 15)
    return {
        "block_input": noise(arg_keys[0], (TOKENS, D), 1.0, 6.0, ((0, 128),)),
        "block_map": jax.random.permutation(arg_keys[1], N_CTX).astype(jnp.int32),
        "attn_gain": jnp.clip(1.0 + 0.18 * jax.random.normal(arg_keys[2], (D,), jnp.float32), 0.1, 1.9),
        "query_weight": noise(arg_keys[3], (D, HEADS * HD), D ** -0.5, 0.1875, ((1, 4),)),
        "key_weight": noise(arg_keys[4], (D, KV_HEADS * HD), D ** -0.5, 0.1875, ((1, 4),)),
        "value_weight": noise(arg_keys[5], (D, KV_HEADS * HD), D ** -0.5, 0.1875, ((1, 4),)),
        "query_gain": jnp.clip(jnp.exp(jax.random.uniform(arg_keys[6], (HD,), jnp.float32, math.log(0.5), math.log(2.0))), 0.5, 2.0),
        "key_gain": jnp.clip(jnp.exp(jax.random.uniform(arg_keys[7], (HD,), jnp.float32, math.log(0.5), math.log(2.0))), 0.5, 2.0),
        "output_weight": noise(arg_keys[8], (HEADS * HD, D), 4 ** -0.5, 3.0, ((0, 4),)),
        "ffn_gain": jnp.clip(1.0 + 0.18 * jax.random.normal(arg_keys[9], (D,), jnp.float32), 0.1, 1.9),
        "gate_weight": noise(arg_keys[10], (D, FF), D ** -0.5, 0.1875, ((1, 4),)),
        "up_weight": noise(arg_keys[11], (D, FF), D ** -0.5, 0.1875, ((1, 4),)),
        "down_weight": noise(arg_keys[12], (FF, D), FF ** -0.5, 0.09375, ((0, 4),)),
        "cotangent": noise(arg_keys[13], (TOKENS, D), 1.0, 6.0, ((0, 128),)),
    }


EPS = 1e-05
THETA = 1000000.0

def rms_forward(values, norm_gain):
    inverse = lax.rsqrt(lax.optimization_barrier(jnp.mean(values * values, axis=-1, keepdims=True)) + EPS)
    return (values * inverse * norm_gain, inverse)

def rms_backward(values, inverse, norm_gain, upstream):
    scaled = upstream * norm_gain
    inner_mean = lax.optimization_barrier(jnp.mean(scaled * values, axis=-1, keepdims=True))
    through = inverse * (scaled - values * inverse * inverse * inner_mean)
    return (through, upstream * values * inverse)

def rope_tables(positions, head_dim):
    halfway = head_dim // 2
    frequency = THETA ** (-(jnp.arange(halfway, dtype=jnp.float32) * 2.0 / head_dim))
    angles = positions.astype(jnp.float32)[:, None] * frequency[None, :]
    return (jnp.cos(angles)[:, None, :], jnp.sin(angles)[:, None, :])

def rope_apply(values, cosine, sine_table):
    halfway = values.shape[-1] // 2
    first_half = values[..., :halfway]
    second_half = values[..., halfway:]
    return jnp.concatenate([first_half * cosine - second_half * sine_table, second_half * cosine + first_half * sine_table], axis=-1)

def rope_back(upstream, cosine, sine_table):
    halfway = upstream.shape[-1] // 2
    first_half = upstream[..., :halfway]
    second_half = upstream[..., halfway:]
    return jnp.concatenate([first_half * cosine + second_half * sine_table, second_half * cosine - first_half * sine_table], axis=-1)

def natural_rows(block_map):
    row_ids = jnp.arange(TOKENS, dtype=jnp.int32)
    device_ids = row_ids // TOK_DEV
    within = row_ids % TOK_DEV
    sequence = within // (2 * BLOCK_LEN)
    later = within // BLOCK_LEN % 2
    picked = block_map[device_ids]
    piece_index = jnp.where(later == 1, 2 * N_CTX - 1 - picked, picked)
    return sequence * SEQ_LEN + piece_index * BLOCK_LEN + within % BLOCK_LEN

def low_copy(values):
    return lax.optimization_barrier(values.astype(jnp.bfloat16)).astype(jnp.float32)

def attend_block(query_block, keys, values, query_places, key_places):
    score_scale = 1.0 / math.sqrt(HD)
    scores = jnp.einsum('qhgd,khd->hgqk', query_block.astype(jnp.float32), keys.astype(jnp.float32)) * score_scale
    allowed = key_places[None, :] <= query_places[:, None]
    scores = jnp.where(allowed, scores, -jnp.inf)
    row_top = lax.optimization_barrier(jnp.max(scores, axis=-1, keepdims=True))
    weights = jnp.exp(scores - row_top)
    row_total = lax.optimization_barrier(jnp.sum(weights, axis=-1, keepdims=True))
    mixed = jnp.einsum('hgqk,khd->hgqd', low_copy(weights), values.astype(jnp.float32)) / row_total
    log_total = (row_top + jnp.log(row_total))[..., 0]
    return (jnp.transpose(mixed, (2, 0, 1, 3)), jnp.transpose(log_total, (2, 0, 1)))

def attend_back(query_block, keys, values, query_places, key_places, grad_block, delta_block, total_block):
    score_scale = 1.0 / math.sqrt(HD)
    scores = jnp.einsum('qhgd,khd->hgqk', query_block.astype(jnp.float32), keys.astype(jnp.float32)) * score_scale
    allowed = key_places[None, :] <= query_places[:, None]
    total_moved = jnp.transpose(total_block, (1, 2, 0))[..., None]
    delta_moved = jnp.transpose(delta_block, (1, 2, 0))[..., None]
    probs = jnp.where(allowed, jnp.exp(scores - total_moved), 0.0)
    grad_wide = grad_block.astype(jnp.float32)
    grad_values = jnp.einsum('hgqk,qhgd->khd', low_copy(probs), grad_wide)
    grad_probs = jnp.einsum('qhgd,khd->hgqk', grad_wide, values.astype(jnp.float32))
    grad_scores = low_copy(score_scale * probs * (grad_probs - delta_moved))
    grad_query = jnp.einsum('hgqk,khd->qhgd', grad_scores, keys.astype(jnp.float32))
    grad_keys = jnp.einsum('hgqk,qhgd->khd', grad_scores, query_block.astype(jnp.float32))
    return (grad_query, grad_keys, grad_values)

def reference(block_input, block_map, attn_gain, query_weight, key_weight, value_weight, query_gain, key_gain, output_weight, ffn_gain, gate_weight, up_weight, down_weight, cotangent):
    natural = natural_rows(block_map)
    order = jnp.zeros((TOKENS,), jnp.int32).at[natural].set(jnp.arange(TOKENS, dtype=jnp.int32))
    residual_in = block_input[order].astype(jnp.float32)
    grad_rows = cotangent[order]
    group_size = HEADS // KV_HEADS
    block_rows = math.gcd(SEQ_LEN, 512)
    block_count = SEQ_LEN // block_rows
    normed_one, inverse_one = rms_forward(residual_in, attn_gain)
    normed_one = normed_one.astype(jnp.bfloat16)
    query_raw = jnp.dot(normed_one, query_weight, preferred_element_type=jnp.float32).reshape(TOKENS, HEADS, HD)
    key_raw = jnp.dot(normed_one, key_weight, preferred_element_type=jnp.float32).reshape(TOKENS, KV_HEADS, HD)
    value_low = jnp.dot(normed_one, value_weight, preferred_element_type=jnp.float32).astype(jnp.bfloat16)
    query_normed, query_inverse = rms_forward(query_raw, query_gain)
    key_normed, key_inverse = rms_forward(key_raw, key_gain)
    positions = jnp.arange(TOKENS, dtype=jnp.int32) % SEQ_LEN
    cosine, sine_table = rope_tables(positions, HD)
    query_rot = rope_apply(query_normed, cosine, sine_table).astype(jnp.bfloat16)
    key_rot = rope_apply(key_normed, cosine, sine_table).astype(jnp.bfloat16)
    query_seq = query_rot.reshape(2, block_count, block_rows, KV_HEADS, group_size, HD)
    key_seq = key_rot.reshape(2, SEQ_LEN, KV_HEADS, HD)
    value_seq = value_low.reshape(2, SEQ_LEN, KV_HEADS, HD)
    key_places = jnp.arange(SEQ_LEN, dtype=jnp.int32)
    block_starts = jnp.arange(block_count, dtype=jnp.int32) * block_rows

    def forward_sequence(packed):
        query_part, keys, values = packed

        def forward_block(inner):
            query_block, start = inner
            query_places = start + jnp.arange(block_rows, dtype=jnp.int32)
            return attend_block(query_block, keys, values, query_places, key_places)
        return lax.map(forward_block, (query_part, block_starts))
    attn_mix, log_total = lax.map(forward_sequence, (query_seq, key_seq, value_seq))
    attn_flat = attn_mix.reshape(TOKENS, HEADS * HD)
    attn_low = attn_flat.astype(jnp.bfloat16)
    residual_mid = residual_in + jnp.dot(attn_low, output_weight, preferred_element_type=jnp.float32)
    normed_two, inverse_two = rms_forward(residual_mid, ffn_gain)
    normed_two = normed_two.astype(jnp.bfloat16)
    gate_pre = jnp.dot(normed_two, gate_weight, preferred_element_type=jnp.float32)
    up_pre = jnp.dot(normed_two, up_weight, preferred_element_type=jnp.float32)
    gate_sig = jax.nn.sigmoid(gate_pre)
    activated = (gate_pre * gate_sig * up_pre).astype(jnp.bfloat16)
    block_output = residual_mid + jnp.dot(activated, down_weight, preferred_element_type=jnp.float32)
    grad_down = jnp.dot(activated.T, grad_rows, preferred_element_type=jnp.float32)
    grad_act = jnp.dot(grad_rows, down_weight.T, preferred_element_type=jnp.float32)
    grad_gate_pre = (grad_act * up_pre * gate_sig * (1.0 + gate_pre * (1.0 - gate_sig))).astype(jnp.bfloat16)
    grad_up_pre = (grad_act * gate_pre * gate_sig).astype(jnp.bfloat16)
    grad_gate = jnp.dot(normed_two.T, grad_gate_pre, preferred_element_type=jnp.float32)
    grad_up = jnp.dot(normed_two.T, grad_up_pre, preferred_element_type=jnp.float32)
    grad_normed_two = jnp.dot(grad_gate_pre, gate_weight.T, preferred_element_type=jnp.float32) + jnp.dot(grad_up_pre, up_weight.T, preferred_element_type=jnp.float32)
    through_two, ffn_terms = rms_backward(residual_mid, inverse_two, ffn_gain, grad_normed_two)
    grad_ffn_gain = lax.optimization_barrier(jnp.sum(ffn_terms, axis=0))
    grad_mid = grad_rows.astype(jnp.float32) + through_two
    grad_mid_low = grad_mid.astype(jnp.bfloat16)
    grad_output = jnp.dot(attn_low.T, grad_mid_low, preferred_element_type=jnp.float32)
    grad_attn = jnp.dot(grad_mid_low, output_weight.T, preferred_element_type=jnp.float32).astype(jnp.bfloat16)
    grad_attn_seq = grad_attn.reshape(2, block_count, block_rows, KV_HEADS, group_size, HD)
    delta_seq = lax.optimization_barrier(jnp.sum(grad_attn_seq.astype(jnp.float32) * attn_mix, axis=-1))

    def backward_sequence(packed):
        query_part, keys, values, grad_part, delta_part, total_part = packed

        def backward_block(carried, inner):
            key_acc, value_acc = carried
            query_block, grad_block, delta_block, total_block, start = inner
            query_places = start + jnp.arange(block_rows, dtype=jnp.int32)
            grad_query, grad_keys, grad_values = attend_back(query_block, keys, values, query_places, key_places, grad_block, delta_block, total_block)
            return ((key_acc + grad_keys, value_acc + grad_values), grad_query)
        empty_grads = jnp.zeros((SEQ_LEN, KV_HEADS, HD), jnp.float32)
        carried, grad_query = lax.scan(backward_block, (empty_grads, empty_grads), (query_part, grad_part, delta_part, total_part, block_starts))
        return (grad_query, carried[0], carried[1])
    grad_query_seq, grad_key_seq, grad_value_seq = lax.map(backward_sequence, (query_seq, key_seq, value_seq, grad_attn_seq, delta_seq, log_total))
    grad_query_rot = grad_query_seq.reshape(TOKENS, HEADS, HD)
    grad_key_rot = grad_key_seq.reshape(TOKENS, KV_HEADS, HD)
    grad_query_raw, query_terms = rms_backward(query_raw, query_inverse, query_gain, rope_back(grad_query_rot, cosine, sine_table))
    grad_key_raw, key_terms = rms_backward(key_raw, key_inverse, key_gain, rope_back(grad_key_rot, cosine, sine_table))
    grad_query_gain = lax.optimization_barrier(jnp.sum(query_terms, axis=(0, 1)))
    grad_key_gain = lax.optimization_barrier(jnp.sum(key_terms, axis=(0, 1)))
    grad_query_low = grad_query_raw.reshape(TOKENS, HEADS * HD).astype(jnp.bfloat16)
    grad_key_low = grad_key_raw.reshape(TOKENS, KV_HEADS * HD).astype(jnp.bfloat16)
    grad_value_low = grad_value_seq.reshape(TOKENS, KV_HEADS * HD).astype(jnp.bfloat16)
    grad_query = jnp.dot(normed_one.T, grad_query_low, preferred_element_type=jnp.float32)
    grad_key = jnp.dot(normed_one.T, grad_key_low, preferred_element_type=jnp.float32)
    grad_value = jnp.dot(normed_one.T, grad_value_low, preferred_element_type=jnp.float32)
    grad_normed_one = jnp.dot(grad_query_low, query_weight.T, preferred_element_type=jnp.float32) + jnp.dot(grad_key_low, key_weight.T, preferred_element_type=jnp.float32) + jnp.dot(grad_value_low, value_weight.T, preferred_element_type=jnp.float32)
    through_one, attn_terms = rms_backward(residual_in, inverse_one, attn_gain, grad_normed_one)
    grad_attn_gain = lax.optimization_barrier(jnp.sum(attn_terms, axis=0))
    input_grad = grad_mid + through_one
    return (block_output[natural], input_grad[natural], grad_attn_gain, grad_query, grad_key, grad_value, grad_query_gain, grad_key_gain, grad_output, grad_ffn_gain, grad_gate, grad_up, grad_down)
```

```python
import math

import jax
import jax.numpy as jnp
from jax import lax
from jax.sharding import PartitionSpec as P

EPS = 1e-05
THETA = 1000000.0
NEGATIVE = -1e30


def rms_forward(values, norm_gain):
    inverse = lax.rsqrt(jnp.mean(values * values, axis=-1, keepdims=True) + EPS)
    return (values * inverse * norm_gain, inverse)


def rms_backward(values, inverse, norm_gain, upstream):
    scaled = upstream * norm_gain
    inner_mean = jnp.mean(scaled * values, axis=-1, keepdims=True)
    through = inverse * (scaled - values * inverse * inverse * inner_mean)
    return (through, upstream * values * inverse)


def rope_tables(positions, head_dim):
    halfway = head_dim // 2
    frequency = THETA ** (-(jnp.arange(halfway, dtype=jnp.float32) * 2.0 / head_dim))
    angles = positions.astype(jnp.float32)[:, None] * frequency[None, :]
    return (jnp.cos(angles)[:, None, :], jnp.sin(angles)[:, None, :])


def rope_apply(values, cosine, sine_table):
    halfway = values.shape[-1] // 2
    first_half = values[..., :halfway]
    second_half = values[..., halfway:]
    return jnp.concatenate(
        [
            first_half * cosine - second_half * sine_table,
            second_half * cosine + first_half * sine_table,
        ],
        axis=-1,
    )


def rope_back(upstream, cosine, sine_table):
    halfway = upstream.shape[-1] // 2
    first_half = upstream[..., :halfway]
    second_half = upstream[..., halfway:]
    return jnp.concatenate(
        [
            first_half * cosine + second_half * sine_table,
            second_half * cosine - first_half * sine_table,
        ],
        axis=-1,
    )


def row_places(block_map, holder, rows_total, place_count):
    piece_len = rows_total // 4
    within = jnp.arange(rows_total, dtype=jnp.int32)
    picked = jnp.sum(jnp.where(jnp.arange(place_count, dtype=jnp.int32) == holder, block_map, 0))
    later = within // piece_len % 2
    piece_index = jnp.where(later == 1, 2 * place_count - 1 - picked, picked)
    return piece_index * piece_len + within % piece_len


def span_places(block_map, first_anchor, shard_span, seq_rows, place_count):
    piece_len = seq_rows // 2
    anchors = first_anchor + jnp.arange(shard_span, dtype=jnp.int32)
    picked = jnp.sum(
        jnp.where(
            jnp.arange(place_count, dtype=jnp.int32)[None, :] == anchors[:, None],
            block_map[None, :],
            0,
        ),
        axis=1,
    )
    within = jnp.arange(seq_rows, dtype=jnp.int32)
    later = within // piece_len % 2
    piece_index = jnp.where(
        later[None, :] == 1, 2 * place_count - 1 - picked[:, None], picked[:, None]
    )
    return (piece_index * piece_len + (within % piece_len)[None, :]).reshape(shard_span * seq_rows)


def gather_rows(rows_low):
    return lax.all_gather(rows_low, "tp", axis=0, tiled=True)


def reduce_rows(partial_rows):
    return lax.psum_scatter(
        partial_rows.astype(jnp.bfloat16), "tp", scatter_dimension=0, tiled=True
    ).astype(jnp.float32)


def per_device(
    block_input,
    block_map,
    attn_gain,
    query_weight,
    key_weight,
    value_weight,
    query_gain,
    key_gain,
    output_weight,
    ffn_gain,
    gate_weight,
    up_weight,
    down_weight,
    cotangent,
):
    place_count = lax.axis_size("ctx")
    place_index = lax.axis_index("ctx")
    head_dim = query_gain.shape[0]
    query_heads = query_weight.shape[1] // head_dim
    kv_heads = key_weight.shape[1] // head_dim
    group_size = query_heads // kv_heads
    score_scale = 1.0 / math.sqrt(head_dim)
    shard_span = 4
    residual_in = block_input.astype(jnp.float32)
    normed_one, inverse_one = rms_forward(residual_in, attn_gain)
    rows_one = gather_rows(normed_one.astype(jnp.bfloat16))
    rows_total = rows_one.shape[0]
    seq_rows = rows_total // 2
    kv_width = kv_heads * head_dim
    own_places = row_places(block_map, place_index, rows_total, place_count)
    query_raw = jnp.dot(rows_one, query_weight, preferred_element_type=jnp.float32).reshape(
        rows_total, query_heads, head_dim
    )
    key_raw = jnp.dot(rows_one, key_weight, preferred_element_type=jnp.float32).reshape(
        rows_total, kv_heads, head_dim
    )
    values_own = jnp.dot(rows_one, value_weight, preferred_element_type=jnp.float32).astype(
        jnp.bfloat16
    )
    query_normed, query_inverse = rms_forward(query_raw, query_gain)
    key_normed, key_inverse = rms_forward(key_raw, key_gain)
    cosine, sine_table = rope_tables(own_places, head_dim)
    query_rot = rope_apply(query_normed, cosine, sine_table).astype(jnp.bfloat16)
    keys_own = (
        rope_apply(key_normed, cosine, sine_table)
        .astype(jnp.bfloat16)
        .reshape(rows_total, kv_width)
    )
    query_blocks = query_rot.reshape(2, seq_rows, kv_heads, group_size, head_dim)
    query_places = own_places[:seq_rows]

    def span_heads(flat_rows):
        return jnp.transpose(
            flat_rows.reshape(shard_span, 2, seq_rows, kv_heads, head_dim), (1, 0, 2, 3, 4)
        ).reshape(2, shard_span * seq_rows, kv_heads, head_dim)

    def span_flat(head_rows):
        return jnp.transpose(
            head_rows.reshape(2, shard_span, seq_rows, kv_width), (1, 0, 2, 3)
        ).reshape(shard_span * rows_total, kv_width)

    def scores_for(key_heads, key_places):
        scores = (
            jnp.einsum(
                "sqhgd,skhd->shgqk", query_blocks, key_heads, preferred_element_type=jnp.float32
            )
            * score_scale
        )
        allowed = key_places[None, :] <= query_places[:, None]
        return (scores, allowed)

    def forward_step(softmax_state, key_heads, value_heads, key_places):
        running_top, running_total, running_acc = softmax_state
        scores, allowed = scores_for(key_heads, key_places)
        scores = jnp.where(allowed, scores, NEGATIVE)
        new_top = jnp.maximum(running_top, jnp.max(scores, axis=-1))
        weights = jnp.where(allowed, jnp.exp(scores - new_top[..., None]), 0.0)
        fading = jnp.exp(running_top - new_top)
        running_total = running_total * fading + jnp.sum(weights, axis=-1)
        running_acc = running_acc * fading[..., None] + jnp.einsum(
            "shgqk,skhd->shgqd",
            weights.astype(jnp.bfloat16),
            value_heads,
            preferred_element_type=jnp.float32,
        )
        return (new_top, running_total, running_acc)

    start_state = (
        jnp.full((2, kv_heads, group_size, seq_rows), NEGATIVE, jnp.float32),
        jnp.zeros((2, kv_heads, group_size, seq_rows), jnp.float32),
        jnp.zeros((2, kv_heads, group_size, seq_rows, head_dim), jnp.float32),
    )
    span_count = place_count // shard_span
    span_rows = shard_span * rows_total
    whole_kv = lax.all_gather(
        jnp.concatenate([keys_own, values_own], axis=1), "ctx", axis=0, tiled=True
    )
    whole_keys, whole_values = whole_kv[:, :kv_width], whole_kv[:, kv_width:]

    def whole_forward(span_index, softmax_state):
        first_anchor = span_index * shard_span
        keys_flat = lax.dynamic_slice_in_dim(whole_keys, first_anchor * rows_total, span_rows, 0)
        values_flat = lax.dynamic_slice_in_dim(
            whole_values, first_anchor * rows_total, span_rows, 0
        )
        key_places = span_places(block_map, first_anchor, shard_span, seq_rows, place_count)
        return forward_step(
            softmax_state, span_heads(keys_flat), span_heads(values_flat), key_places
        )

    softmax_state = lax.fori_loop(0, span_count, whole_forward, start_state)
    running_top, running_total, running_acc = softmax_state
    log_total = running_top + jnp.log(running_total)
    attn_rows = jnp.transpose(running_acc / running_total[..., None], (0, 3, 1, 2, 4))
    attn_low = attn_rows.reshape(rows_total, query_heads * head_dim).astype(jnp.bfloat16)
    residual_mid = residual_in + reduce_rows(
        jnp.dot(attn_low, output_weight, preferred_element_type=jnp.float32)
    )
    normed_two, inverse_two = rms_forward(residual_mid, ffn_gain)
    rows_two = gather_rows(normed_two.astype(jnp.bfloat16))
    gate_pre = jnp.dot(rows_two, gate_weight, preferred_element_type=jnp.float32)
    up_pre = jnp.dot(rows_two, up_weight, preferred_element_type=jnp.float32)
    gate_sig = jax.nn.sigmoid(gate_pre)
    activated = (gate_pre * gate_sig * up_pre).astype(jnp.bfloat16)
    block_output = residual_mid + reduce_rows(
        jnp.dot(activated, down_weight, preferred_element_type=jnp.float32)
    )
    grad_rows = gather_rows(cotangent)
    grad_down_t = jnp.dot(grad_rows.T, activated, preferred_element_type=jnp.float32)
    grad_act = jnp.dot(grad_rows, down_weight.T, preferred_element_type=jnp.float32)
    grad_gate_pre = (grad_act * up_pre * gate_sig * (1.0 + gate_pre * (1.0 - gate_sig))).astype(
        jnp.bfloat16
    )
    grad_up_pre = (grad_act * gate_pre * gate_sig).astype(jnp.bfloat16)
    grad_gate = jnp.dot(rows_two.T, grad_gate_pre, preferred_element_type=jnp.float32)
    grad_up = jnp.dot(rows_two.T, grad_up_pre, preferred_element_type=jnp.float32)
    grad_normed_two = reduce_rows(
        jnp.dot(grad_gate_pre, gate_weight.T, preferred_element_type=jnp.float32)
        + jnp.dot(grad_up_pre, up_weight.T, preferred_element_type=jnp.float32)
    )
    through_two, ffn_terms = rms_backward(residual_mid, inverse_two, ffn_gain, grad_normed_two)
    grad_mid = cotangent.astype(jnp.float32) + through_two
    grad_mid_rows = gather_rows(grad_mid.astype(jnp.bfloat16))
    grad_output_t = jnp.dot(grad_mid_rows.T, attn_low, preferred_element_type=jnp.float32)
    grad_attn = jnp.dot(grad_mid_rows, output_weight.T, preferred_element_type=jnp.float32).astype(
        jnp.bfloat16
    )
    grad_attn_blocks = grad_attn.reshape(2, seq_rows, kv_heads, group_size, head_dim)
    delta_rows = jnp.sum(grad_attn_blocks.astype(jnp.float32) * attn_rows, axis=-1)
    delta_rows = jnp.transpose(delta_rows, (0, 2, 3, 1))

    def backward_step(key_heads, value_heads, key_places):
        scores, allowed = scores_for(key_heads, key_places)
        probs = jnp.where(allowed, jnp.exp(scores - log_total[..., None]), 0.0)
        grad_value_block = jnp.einsum(
            "shgqk,sqhgd->skhd",
            probs.astype(jnp.bfloat16),
            grad_attn_blocks,
            preferred_element_type=jnp.float32,
        )
        grad_probs = jnp.einsum(
            "sqhgd,skhd->shgqk", grad_attn_blocks, value_heads, preferred_element_type=jnp.float32
        )
        grad_scores = (score_scale * probs * (grad_probs - delta_rows[..., None])).astype(
            jnp.bfloat16
        )
        grad_query_block = jnp.einsum(
            "shgqk,skhd->sqhgd", grad_scores, key_heads, preferred_element_type=jnp.float32
        )
        grad_key_block = jnp.einsum(
            "shgqk,sqhgd->skhd", grad_scores, query_blocks, preferred_element_type=jnp.float32
        )
        return (grad_query_block, grad_key_block, grad_value_block)

    key_grad_whole = jnp.zeros((place_count * rows_total, kv_width), jnp.float32)
    start_grads = (
        jnp.zeros((2, seq_rows, kv_heads, group_size, head_dim), jnp.float32),
        key_grad_whole,
        key_grad_whole,
    )

    def whole_backward(span_index, grad_carry):
        query_acc, key_grad_all, value_grad_all = grad_carry
        first_anchor = span_index * shard_span
        keys_flat = lax.dynamic_slice_in_dim(whole_keys, first_anchor * rows_total, span_rows, 0)
        values_flat = lax.dynamic_slice_in_dim(
            whole_values, first_anchor * rows_total, span_rows, 0
        )
        key_places = span_places(block_map, first_anchor, shard_span, seq_rows, place_count)
        add_query, add_key, add_value = backward_step(
            span_heads(keys_flat), span_heads(values_flat), key_places
        )
        key_grad_all = lax.dynamic_update_slice_in_dim(
            key_grad_all, span_flat(add_key), first_anchor * rows_total, 0
        )
        value_grad_all = lax.dynamic_update_slice_in_dim(
            value_grad_all, span_flat(add_value), first_anchor * rows_total, 0
        )
        return (query_acc + add_query, key_grad_all, value_grad_all)

    query_acc, key_grad_all, value_grad_all = lax.fori_loop(
        0, span_count, whole_backward, start_grads
    )
    grad_kv_flat = lax.psum_scatter(
        jnp.concatenate([key_grad_all, value_grad_all], axis=1).astype(jnp.bfloat16),
        "ctx",
        scatter_dimension=0,
        tiled=True,
    ).astype(jnp.float32)
    grad_keys_flat, grad_values_flat = grad_kv_flat[:, :kv_width], grad_kv_flat[:, kv_width:]
    grad_query_rot = query_acc.reshape(rows_total, query_heads, head_dim)
    grad_key_rot = grad_keys_flat.reshape(rows_total, kv_heads, head_dim)
    grad_query_raw, query_terms = rms_backward(
        query_raw, query_inverse, query_gain, rope_back(grad_query_rot, cosine, sine_table)
    )
    grad_key_raw, key_terms = rms_backward(
        key_raw, key_inverse, key_gain, rope_back(grad_key_rot, cosine, sine_table)
    )
    grad_query_low = grad_query_raw.reshape(rows_total, query_heads * head_dim).astype(jnp.bfloat16)
    grad_key_low = grad_key_raw.reshape(rows_total, kv_width).astype(jnp.bfloat16)
    grad_value_low = grad_values_flat.astype(jnp.bfloat16)
    grad_query = jnp.dot(rows_one.T, grad_query_low, preferred_element_type=jnp.float32)
    grad_key = jnp.dot(rows_one.T, grad_key_low, preferred_element_type=jnp.float32)
    grad_value = jnp.dot(rows_one.T, grad_value_low, preferred_element_type=jnp.float32)
    grad_normed_one = reduce_rows(
        jnp.dot(grad_query_low, query_weight.T, preferred_element_type=jnp.float32)
        + jnp.dot(grad_key_low, key_weight.T, preferred_element_type=jnp.float32)
        + jnp.dot(grad_value_low, value_weight.T, preferred_element_type=jnp.float32)
    )
    through_one, attn_terms = rms_backward(residual_in, inverse_one, attn_gain, grad_normed_one)
    input_grad = grad_mid + through_one
    weight_parts = (grad_query, grad_key, grad_value, grad_output_t, grad_gate, grad_up, grad_down_t)
    widths = [part.shape[1] for part in weight_parts]
    summed = lax.psum(
        jnp.concatenate([part.astype(jnp.bfloat16) for part in weight_parts], axis=1), "ctx"
    ).astype(jnp.float32)
    offsets = [sum(widths[:k]) for k in range(len(widths) + 1)]
    shared_query, shared_key, shared_value, output_t, shared_gate, shared_up, down_t = (
        summed[:, offsets[k] : offsets[k + 1]] for k in range(len(widths))
    )
    shared_output = output_t.T
    shared_down = down_t.T
    gain_parts = (
        jnp.sum(attn_terms, axis=0),
        jnp.sum(query_terms, axis=(0, 1)),
        jnp.sum(key_terms, axis=(0, 1)),
        jnp.sum(ffn_terms, axis=0),
    )
    gain_sizes = [part.shape[0] for part in gain_parts]
    gains = lax.psum(jnp.concatenate(gain_parts), ("ctx", "tp"))
    gain_attn = gains[: gain_sizes[0]]
    gain_query = gains[gain_sizes[0] : gain_sizes[0] + gain_sizes[1]]
    gain_key = gains[gain_sizes[0] + gain_sizes[1] : gain_sizes[0] + gain_sizes[1] + gain_sizes[2]]
    gain_ffn = gains[gain_sizes[0] + gain_sizes[1] + gain_sizes[2] :]
    return (
        block_output,
        input_grad,
        gain_attn,
        shared_query,
        shared_key,
        shared_value,
        gain_query,
        gain_key,
        shared_output,
        gain_ffn,
        shared_gate,
        shared_up,
        shared_down,
    )


def solution(mesh):
    return jax.shard_map(
        per_device,
        mesh=mesh,
        in_specs=(
            P(("ctx", "tp"), None),
            P(),
            P(),
            P(None, "tp"),
            P(None, "tp"),
            P(None, "tp"),
            P(),
            P(),
            P("tp", None),
            P(),
            P(None, "tp"),
            P(None, "tp"),
            P("tp", None),
            P(("ctx", "tp"), None),
        ),
        out_specs=(
            P(("ctx", "tp"), None),
            P(("ctx", "tp"), None),
            P(),
            P(None, "tp"),
            P(None, "tp"),
            P(None, "tp"),
            P(),
            P(),
            P("tp", None),
            P(),
            P(None, "tp"),
            P(None, "tp"),
            P("tp", None),
        ),
        check_vma=False,
    )
```

```python
import functools
import math

import jax
import jax.numpy as jnp
from jax import lax
from jax.experimental import pallas as pl
from jax.experimental.pallas import tpu as pltpu
from jax.sharding import PartitionSpec as P

MESH = pl.DeviceIdType.MESH
VMEM_LIMIT = 60 * 1024 * 1024


def _enter(n, me, peer_axis):
    barrier = pltpu.get_barrier_semaphore()
    for k in range(1, n):
        pl.semaphore_signal(
            barrier, 1, device_id=(lax.rem(me + k, n), peer_axis), device_id_type=MESH
        )
    pl.semaphore_wait(barrier, n - 1)


def _gather_kernel(n, part_ref, out_ref, send_sem, recv_sem):
    me = lax.axis_index("ctx")
    other = lax.axis_index("tp")
    rows = part_ref.shape[0]
    _enter(n, me, other)
    copies = []
    for k in range(1, n):
        copy = pltpu.make_async_remote_copy(
            src_ref=part_ref,
            dst_ref=out_ref.at[pl.ds(pl.multiple_of(me * rows, rows), rows)],
            send_sem=send_sem.at[k],
            recv_sem=recv_sem.at[k],
            device_id=(lax.rem(me + k, n), other),
            device_id_type=MESH,
        )
        copy.start()
        copies.append(copy)
    out_ref[pl.ds(pl.multiple_of(me * rows, rows), rows), :] = part_ref[...]
    for k in range(1, n):
        source = lax.rem(me + n - k, n)
        pltpu.make_async_remote_copy(
            src_ref=part_ref,
            dst_ref=out_ref.at[pl.ds(pl.multiple_of(source * rows, rows), rows)],
            send_sem=send_sem.at[k],
            recv_sem=recv_sem.at[k],
            device_id=(source, other),
            device_id_type=MESH,
        ).wait_recv()
    for copy in copies:
        copy.wait_send()


def ctx_gather(part, n, collective_id):
    rows, cols = part.shape
    return pl.pallas_call(
        functools.partial(_gather_kernel, n),
        out_shape=jax.ShapeDtypeStruct((n * rows, cols), part.dtype),
        in_specs=[pl.BlockSpec(memory_space=pltpu.VMEM)],
        out_specs=pl.BlockSpec(memory_space=pltpu.VMEM),
        scratch_shapes=[pltpu.SemaphoreType.DMA((n,)), pltpu.SemaphoreType.DMA((n,))],
        compiler_params=pltpu.CompilerParams(
            collective_id=collective_id, has_side_effects=True, vmem_limit_bytes=VMEM_LIMIT
        ),
    )(part)


def _scatter_sum(n, me, other, whole_ref, held, send_sem, recv_sem, rows):
    copies = []
    for k in range(1, n):
        target = lax.rem(me + k, n)
        copy = pltpu.make_async_remote_copy(
            src_ref=whole_ref.at[pl.ds(pl.multiple_of(target * rows, rows), rows)],
            dst_ref=held.at[k],
            send_sem=send_sem.at[k],
            recv_sem=recv_sem.at[k],
            device_id=(target, other),
            device_id_type=MESH,
        )
        copy.start()
        copies.append(copy)
    total = whole_ref[pl.ds(pl.multiple_of(me * rows, rows), rows), :].astype(jnp.float32)
    for k in range(1, n):
        source = lax.rem(me + n - k, n)
        pltpu.make_async_remote_copy(
            src_ref=whole_ref.at[pl.ds(0, rows)],
            dst_ref=held.at[k],
            send_sem=send_sem.at[k],
            recv_sem=recv_sem.at[k],
            device_id=(source, other),
            device_id_type=MESH,
        ).wait_recv()
        total = total + held[k].astype(jnp.float32)
    for copy in copies:
        copy.wait_send()
    return total


def _scatter_kernel(n, whole_ref, out_ref, held, send_sem, recv_sem):
    me = lax.axis_index("ctx")
    other = lax.axis_index("tp")
    rows = out_ref.shape[0]
    _enter(n, me, other)
    out_ref[...] = _scatter_sum(n, me, other, whole_ref, held, send_sem, recv_sem, rows)


def ctx_scatter(whole, n, collective_id):
    rows, cols = whole.shape[0] // n, whole.shape[1]
    return pl.pallas_call(
        functools.partial(_scatter_kernel, n),
        out_shape=jax.ShapeDtypeStruct((rows, cols), jnp.float32),
        in_specs=[pl.BlockSpec(memory_space=pltpu.VMEM)],
        out_specs=pl.BlockSpec(memory_space=pltpu.VMEM),
        scratch_shapes=[
            pltpu.VMEM((n, rows, cols), whole.dtype),
            pltpu.SemaphoreType.DMA((n,)),
            pltpu.SemaphoreType.DMA((n,)),
        ],
        compiler_params=pltpu.CompilerParams(
            collective_id=collective_id, has_side_effects=True, vmem_limit_bytes=VMEM_LIMIT
        ),
    )(whole)


def _sum_kernel(n, whole_ref, out_ref, held, mine, send_sem, recv_sem, send_back, recv_back):
    me = lax.axis_index("ctx")
    other = lax.axis_index("tp")
    rows = whole_ref.shape[0] // n
    _enter(n, me, other)
    mine[...] = _scatter_sum(n, me, other, whole_ref, held, send_sem, recv_sem, rows).astype(
        mine.dtype
    )
    copies = []
    for k in range(1, n):
        copy = pltpu.make_async_remote_copy(
            src_ref=mine,
            dst_ref=out_ref.at[pl.ds(pl.multiple_of(me * rows, rows), rows)],
            send_sem=send_back.at[k],
            recv_sem=recv_back.at[k],
            device_id=(lax.rem(me + k, n), other),
            device_id_type=MESH,
        )
        copy.start()
        copies.append(copy)
    out_ref[pl.ds(pl.multiple_of(me * rows, rows), rows), :] = mine[...]
    for k in range(1, n):
        source = lax.rem(me + n - k, n)
        pltpu.make_async_remote_copy(
            src_ref=mine,
            dst_ref=out_ref.at[pl.ds(pl.multiple_of(source * rows, rows), rows)],
            send_sem=send_back.at[k],
            recv_sem=recv_back.at[k],
            device_id=(source, other),
            device_id_type=MESH,
        ).wait_recv()
    for copy in copies:
        copy.wait_send()


def ctx_sum(whole, n, collective_id):
    rows, cols = whole.shape[0] // n, whole.shape[1]
    return pl.pallas_call(
        functools.partial(_sum_kernel, n),
        out_shape=jax.ShapeDtypeStruct(whole.shape, whole.dtype),
        in_specs=[pl.BlockSpec(memory_space=pltpu.VMEM)],
        out_specs=pl.BlockSpec(memory_space=pltpu.VMEM),
        scratch_shapes=[
            pltpu.VMEM((n, rows, cols), whole.dtype),
            pltpu.VMEM((rows, cols), whole.dtype),
            pltpu.SemaphoreType.DMA((n,)),
            pltpu.SemaphoreType.DMA((n,)),
            pltpu.SemaphoreType.DMA((n,)),
            pltpu.SemaphoreType.DMA((n,)),
        ],
        compiler_params=pltpu.CompilerParams(
            collective_id=collective_id, has_side_effects=True, vmem_limit_bytes=VMEM_LIMIT
        ),
    )(whole)


EPS = 1e-05
THETA = 1000000.0
NEGATIVE = -1e30


def rms_forward(values, norm_gain):
    inverse = lax.rsqrt(jnp.mean(values * values, axis=-1, keepdims=True) + EPS)
    return (values * inverse * norm_gain, inverse)


def rms_backward(values, inverse, norm_gain, upstream):
    scaled = upstream * norm_gain
    inner_mean = jnp.mean(scaled * values, axis=-1, keepdims=True)
    through = inverse * (scaled - values * inverse * inverse * inner_mean)
    return (through, upstream * values * inverse)


def rope_tables(positions, head_dim):
    halfway = head_dim // 2
    frequency = THETA ** (-(jnp.arange(halfway, dtype=jnp.float32) * 2.0 / head_dim))
    angles = positions.astype(jnp.float32)[:, None] * frequency[None, :]
    return (jnp.cos(angles)[:, None, :], jnp.sin(angles)[:, None, :])


def rope_apply(values, cosine, sine_table):
    halfway = values.shape[-1] // 2
    first_half = values[..., :halfway]
    second_half = values[..., halfway:]
    return jnp.concatenate(
        [
            first_half * cosine - second_half * sine_table,
            second_half * cosine + first_half * sine_table,
        ],
        axis=-1,
    )


def rope_back(upstream, cosine, sine_table):
    halfway = upstream.shape[-1] // 2
    first_half = upstream[..., :halfway]
    second_half = upstream[..., halfway:]
    return jnp.concatenate(
        [
            first_half * cosine + second_half * sine_table,
            second_half * cosine - first_half * sine_table,
        ],
        axis=-1,
    )


def row_places(block_map, holder, rows_total, place_count):
    piece_len = rows_total // 4
    within = jnp.arange(rows_total, dtype=jnp.int32)
    picked = jnp.sum(jnp.where(jnp.arange(place_count, dtype=jnp.int32) == holder, block_map, 0))
    later = within // piece_len % 2
    piece_index = jnp.where(later == 1, 2 * place_count - 1 - picked, picked)
    return piece_index * piece_len + within % piece_len


def span_places(block_map, first_anchor, shard_span, seq_rows, place_count):
    piece_len = seq_rows // 2
    anchors = first_anchor + jnp.arange(shard_span, dtype=jnp.int32)
    picked = jnp.sum(
        jnp.where(
            jnp.arange(place_count, dtype=jnp.int32)[None, :] == anchors[:, None],
            block_map[None, :],
            0,
        ),
        axis=1,
    )
    within = jnp.arange(seq_rows, dtype=jnp.int32)
    later = within // piece_len % 2
    piece_index = jnp.where(
        later[None, :] == 1, 2 * place_count - 1 - picked[:, None], picked[:, None]
    )
    return (piece_index * piece_len + (within % piece_len)[None, :]).reshape(shard_span * seq_rows)


def gather_rows(rows_low):
    return lax.all_gather(rows_low, "tp", axis=0, tiled=True)


def reduce_rows(partial_rows):
    return lax.psum_scatter(
        partial_rows.astype(jnp.bfloat16), "tp", scatter_dimension=0, tiled=True
    ).astype(jnp.float32)


def per_device(
    block_input,
    block_map,
    attn_gain,
    query_weight,
    key_weight,
    value_weight,
    query_gain,
    key_gain,
    output_weight,
    ffn_gain,
    gate_weight,
    up_weight,
    down_weight,
    cotangent,
):
    place_count = lax.axis_size("ctx")
    place_index = lax.axis_index("ctx")
    head_dim = query_gain.shape[0]
    query_heads = query_weight.shape[1] // head_dim
    kv_heads = key_weight.shape[1] // head_dim
    group_size = query_heads // kv_heads
    score_scale = 1.0 / math.sqrt(head_dim)
    shard_span = 4
    residual_in = block_input.astype(jnp.float32)
    normed_one, inverse_one = rms_forward(residual_in, attn_gain)
    rows_one = gather_rows(normed_one.astype(jnp.bfloat16))
    rows_total = rows_one.shape[0]
    seq_rows = rows_total // 2
    kv_width = kv_heads * head_dim
    own_places = row_places(block_map, place_index, rows_total, place_count)
    query_raw = jnp.dot(rows_one, query_weight, preferred_element_type=jnp.float32).reshape(
        rows_total, query_heads, head_dim
    )
    key_raw = jnp.dot(rows_one, key_weight, preferred_element_type=jnp.float32).reshape(
        rows_total, kv_heads, head_dim
    )
    values_own = jnp.dot(rows_one, value_weight, preferred_element_type=jnp.float32).astype(
        jnp.bfloat16
    )
    query_normed, query_inverse = rms_forward(query_raw, query_gain)
    key_normed, key_inverse = rms_forward(key_raw, key_gain)
    cosine, sine_table = rope_tables(own_places, head_dim)
    query_rot = rope_apply(query_normed, cosine, sine_table).astype(jnp.bfloat16)
    keys_own = (
        rope_apply(key_normed, cosine, sine_table)
        .astype(jnp.bfloat16)
        .reshape(rows_total, kv_width)
    )
    query_blocks = query_rot.reshape(2, seq_rows, kv_heads, group_size, head_dim)
    query_places = own_places[:seq_rows]

    def span_heads(flat_rows):
        return jnp.transpose(
            flat_rows.reshape(shard_span, 2, seq_rows, kv_heads, head_dim), (1, 0, 2, 3, 4)
        ).reshape(2, shard_span * seq_rows, kv_heads, head_dim)

    def span_flat(head_rows):
        return jnp.transpose(
            head_rows.reshape(2, shard_span, seq_rows, kv_width), (1, 0, 2, 3)
        ).reshape(shard_span * rows_total, kv_width)

    def scores_for(key_heads, key_places):
        scores = (
            jnp.einsum(
                "sqhgd,skhd->shgqk", query_blocks, key_heads, preferred_element_type=jnp.float32
            )
            * score_scale
        )
        allowed = key_places[None, :] <= query_places[:, None]
        return (scores, allowed)

    def forward_step(softmax_state, key_heads, value_heads, key_places):
        running_top, running_total, running_acc = softmax_state
        scores, allowed = scores_for(key_heads, key_places)
        scores = jnp.where(allowed, scores, NEGATIVE)
        new_top = jnp.maximum(running_top, jnp.max(scores, axis=-1))
        weights = jnp.where(allowed, jnp.exp(scores - new_top[..., None]), 0.0)
        fading = jnp.exp(running_top - new_top)
        running_total = running_total * fading + jnp.sum(weights, axis=-1)
        running_acc = running_acc * fading[..., None] + jnp.einsum(
            "shgqk,skhd->shgqd",
            weights.astype(jnp.bfloat16),
            value_heads,
            preferred_element_type=jnp.float32,
        )
        return (new_top, running_total, running_acc)

    start_state = (
        jnp.full((2, kv_heads, group_size, seq_rows), NEGATIVE, jnp.float32),
        jnp.zeros((2, kv_heads, group_size, seq_rows), jnp.float32),
        jnp.zeros((2, kv_heads, group_size, seq_rows, head_dim), jnp.float32),
    )
    span_count = place_count // shard_span
    span_rows = shard_span * rows_total
    whole_kv = ctx_gather(jnp.concatenate([keys_own, values_own], axis=1), place_count, 0)
    whole_keys, whole_values = whole_kv[:, :kv_width], whole_kv[:, kv_width:]

    def whole_forward(span_index, softmax_state):
        first_anchor = span_index * shard_span
        keys_flat = lax.dynamic_slice_in_dim(whole_keys, first_anchor * rows_total, span_rows, 0)
        values_flat = lax.dynamic_slice_in_dim(
            whole_values, first_anchor * rows_total, span_rows, 0
        )
        key_places = span_places(block_map, first_anchor, shard_span, seq_rows, place_count)
        return forward_step(
            softmax_state, span_heads(keys_flat), span_heads(values_flat), key_places
        )

    softmax_state = lax.fori_loop(0, span_count, whole_forward, start_state)
    running_top, running_total, running_acc = softmax_state
    log_total = running_top + jnp.log(running_total)
    attn_rows = jnp.transpose(running_acc / running_total[..., None], (0, 3, 1, 2, 4))
    attn_low = attn_rows.reshape(rows_total, query_heads * head_dim).astype(jnp.bfloat16)
    residual_mid = residual_in + reduce_rows(
        jnp.dot(attn_low, output_weight, preferred_element_type=jnp.float32)
    )
    normed_two, inverse_two = rms_forward(residual_mid, ffn_gain)
    rows_two = gather_rows(normed_two.astype(jnp.bfloat16))
    gate_pre = jnp.dot(rows_two, gate_weight, preferred_element_type=jnp.float32)
    up_pre = jnp.dot(rows_two, up_weight, preferred_element_type=jnp.float32)
    gate_sig = jax.nn.sigmoid(gate_pre)
    activated = (gate_pre * gate_sig * up_pre).astype(jnp.bfloat16)
    block_output = residual_mid + reduce_rows(
        jnp.dot(activated, down_weight, preferred_element_type=jnp.float32)
    )
    grad_rows = gather_rows(cotangent)
    grad_down_t = jnp.dot(grad_rows.T, activated, preferred_element_type=jnp.float32)
    grad_act = jnp.dot(grad_rows, down_weight.T, preferred_element_type=jnp.float32)
    grad_gate_pre = (grad_act * up_pre * gate_sig * (1.0 + gate_pre * (1.0 - gate_sig))).astype(
        jnp.bfloat16
    )
    grad_up_pre = (grad_act * gate_pre * gate_sig).astype(jnp.bfloat16)
    grad_gate = jnp.dot(rows_two.T, grad_gate_pre, preferred_element_type=jnp.float32)
    grad_up = jnp.dot(rows_two.T, grad_up_pre, preferred_element_type=jnp.float32)
    grad_normed_two = reduce_rows(
        jnp.dot(grad_gate_pre, gate_weight.T, preferred_element_type=jnp.float32)
        + jnp.dot(grad_up_pre, up_weight.T, preferred_element_type=jnp.float32)
    )
    through_two, ffn_terms = rms_backward(residual_mid, inverse_two, ffn_gain, grad_normed_two)
    grad_mid = cotangent.astype(jnp.float32) + through_two
    grad_mid_rows = gather_rows(grad_mid.astype(jnp.bfloat16))
    grad_output_t = jnp.dot(grad_mid_rows.T, attn_low, preferred_element_type=jnp.float32)
    grad_attn = jnp.dot(grad_mid_rows, output_weight.T, preferred_element_type=jnp.float32).astype(
        jnp.bfloat16
    )
    grad_attn_blocks = grad_attn.reshape(2, seq_rows, kv_heads, group_size, head_dim)
    delta_rows = jnp.sum(grad_attn_blocks.astype(jnp.float32) * attn_rows, axis=-1)
    delta_rows = jnp.transpose(delta_rows, (0, 2, 3, 1))

    def backward_step(key_heads, value_heads, key_places):
        scores, allowed = scores_for(key_heads, key_places)
        probs = jnp.where(allowed, jnp.exp(scores - log_total[..., None]), 0.0)
        grad_value_block = jnp.einsum(
            "shgqk,sqhgd->skhd",
            probs.astype(jnp.bfloat16),
            grad_attn_blocks,
            preferred_element_type=jnp.float32,
        )
        grad_probs = jnp.einsum(
            "sqhgd,skhd->shgqk", grad_attn_blocks, value_heads, preferred_element_type=jnp.float32
        )
        grad_scores = (score_scale * probs * (grad_probs - delta_rows[..., None])).astype(
            jnp.bfloat16
        )
        grad_query_block = jnp.einsum(
            "shgqk,skhd->sqhgd", grad_scores, key_heads, preferred_element_type=jnp.float32
        )
        grad_key_block = jnp.einsum(
            "shgqk,sqhgd->skhd", grad_scores, query_blocks, preferred_element_type=jnp.float32
        )
        return (grad_query_block, grad_key_block, grad_value_block)

    key_grad_whole = jnp.zeros((place_count * rows_total, kv_width), jnp.float32)
    start_grads = (
        jnp.zeros((2, seq_rows, kv_heads, group_size, head_dim), jnp.float32),
        key_grad_whole,
        key_grad_whole,
    )

    def whole_backward(span_index, grad_carry):
        query_acc, key_grad_all, value_grad_all = grad_carry
        first_anchor = span_index * shard_span
        keys_flat = lax.dynamic_slice_in_dim(whole_keys, first_anchor * rows_total, span_rows, 0)
        values_flat = lax.dynamic_slice_in_dim(
            whole_values, first_anchor * rows_total, span_rows, 0
        )
        key_places = span_places(block_map, first_anchor, shard_span, seq_rows, place_count)
        add_query, add_key, add_value = backward_step(
            span_heads(keys_flat), span_heads(values_flat), key_places
        )
        key_grad_all = lax.dynamic_update_slice_in_dim(
            key_grad_all, span_flat(add_key), first_anchor * rows_total, 0
        )
        value_grad_all = lax.dynamic_update_slice_in_dim(
            value_grad_all, span_flat(add_value), first_anchor * rows_total, 0
        )
        return (query_acc + add_query, key_grad_all, value_grad_all)

    query_acc, key_grad_all, value_grad_all = lax.fori_loop(
        0, span_count, whole_backward, start_grads
    )
    grad_kv_flat = ctx_scatter(
        jnp.concatenate([key_grad_all, value_grad_all], axis=1).astype(jnp.bfloat16),
        place_count,
        1,
    )
    grad_keys_flat, grad_values_flat = grad_kv_flat[:, :kv_width], grad_kv_flat[:, kv_width:]
    grad_query_rot = query_acc.reshape(rows_total, query_heads, head_dim)
    grad_key_rot = grad_keys_flat.reshape(rows_total, kv_heads, head_dim)
    grad_query_raw, query_terms = rms_backward(
        query_raw, query_inverse, query_gain, rope_back(grad_query_rot, cosine, sine_table)
    )
    grad_key_raw, key_terms = rms_backward(
        key_raw, key_inverse, key_gain, rope_back(grad_key_rot, cosine, sine_table)
    )
    grad_query_low = grad_query_raw.reshape(rows_total, query_heads * head_dim).astype(jnp.bfloat16)
    grad_key_low = grad_key_raw.reshape(rows_total, kv_width).astype(jnp.bfloat16)
    grad_value_low = grad_values_flat.astype(jnp.bfloat16)
    grad_query = jnp.dot(rows_one.T, grad_query_low, preferred_element_type=jnp.float32)
    grad_key = jnp.dot(rows_one.T, grad_key_low, preferred_element_type=jnp.float32)
    grad_value = jnp.dot(rows_one.T, grad_value_low, preferred_element_type=jnp.float32)
    grad_normed_one = reduce_rows(
        jnp.dot(grad_query_low, query_weight.T, preferred_element_type=jnp.float32)
        + jnp.dot(grad_key_low, key_weight.T, preferred_element_type=jnp.float32)
        + jnp.dot(grad_value_low, value_weight.T, preferred_element_type=jnp.float32)
    )
    through_one, attn_terms = rms_backward(residual_in, inverse_one, attn_gain, grad_normed_one)
    input_grad = grad_mid + through_one
    weight_parts = (grad_query, grad_key, grad_value, grad_output_t, grad_gate, grad_up, grad_down_t)
    widths = [part.shape[1] for part in weight_parts]
    summed = ctx_sum(
        jnp.concatenate([part.astype(jnp.bfloat16) for part in weight_parts], axis=1),
        place_count,
        2,
    ).astype(jnp.float32)
    offsets = [sum(widths[:k]) for k in range(len(widths) + 1)]
    shared_query, shared_key, shared_value, output_t, shared_gate, shared_up, down_t = (
        summed[:, offsets[k] : offsets[k + 1]] for k in range(len(widths))
    )
    shared_output = output_t.T
    shared_down = down_t.T
    gain_parts = (
        jnp.sum(attn_terms, axis=0),
        jnp.sum(query_terms, axis=(0, 1)),
        jnp.sum(key_terms, axis=(0, 1)),
        jnp.sum(ffn_terms, axis=0),
    )
    gain_sizes = [part.shape[0] for part in gain_parts]
    gains = lax.psum(jnp.concatenate(gain_parts), ("ctx", "tp"))
    gain_attn = gains[: gain_sizes[0]]
    gain_query = gains[gain_sizes[0] : gain_sizes[0] + gain_sizes[1]]
    gain_key = gains[gain_sizes[0] + gain_sizes[1] : gain_sizes[0] + gain_sizes[1] + gain_sizes[2]]
    gain_ffn = gains[gain_sizes[0] + gain_sizes[1] + gain_sizes[2] :]
    return (
        block_output,
        input_grad,
        gain_attn,
        shared_query,
        shared_key,
        shared_value,
        gain_query,
        gain_key,
        shared_output,
        gain_ffn,
        shared_gate,
        shared_up,
        shared_down,
    )


def solution(mesh):
    return jax.shard_map(
        per_device,
        mesh=mesh,
        in_specs=(
            P(("ctx", "tp"), None),
            P(),
            P(),
            P(None, "tp"),
            P(None, "tp"),
            P(None, "tp"),
            P(),
            P(),
            P("tp", None),
            P(),
            P(None, "tp"),
            P(None, "tp"),
            P("tp", None),
            P(("ctx", "tp"), None),
        ),
        out_specs=(
            P(("ctx", "tp"), None),
            P(("ctx", "tp"), None),
            P(),
            P(None, "tp"),
            P(None, "tp"),
            P(None, "tp"),
            P(),
            P(),
            P("tp", None),
            P(),
            P(None, "tp"),
            P(None, "tp"),
            P("tp", None),
        ),
        check_vma=False,
    )
```

```python
import functools
import math

import jax
import jax.numpy as jnp
from jax import lax
from jax.experimental import pallas as pl
from jax.experimental.pallas import tpu as pltpu
from jax.sharding import PartitionSpec as P

MESH = pl.DeviceIdType.MESH
VMEM_LIMIT = 60 * 1024 * 1024


def _enter(n, me, peer_axis):
    barrier = pltpu.get_barrier_semaphore()
    for k in range(1, n):
        pl.semaphore_signal(
            barrier, 1, device_id=(lax.rem(me + k, n), peer_axis), device_id_type=MESH
        )
    pl.semaphore_wait(barrier, n - 1)


def _gather_kernel(n, part_ref, out_ref, send_sem, recv_sem):
    me = lax.axis_index("ctx")
    other = lax.axis_index("tp")
    rows = part_ref.shape[0]
    _enter(n, me, other)
    copies = []
    for k in range(1, n):
        copy = pltpu.make_async_remote_copy(
            src_ref=part_ref,
            dst_ref=out_ref.at[pl.ds(pl.multiple_of(me * rows, rows), rows)],
            send_sem=send_sem.at[k],
            recv_sem=recv_sem.at[k],
            device_id=(lax.rem(me + k, n), other),
            device_id_type=MESH,
        )
        copy.start()
        copies.append(copy)
    out_ref[pl.ds(pl.multiple_of(me * rows, rows), rows), :] = part_ref[...]
    for k in range(1, n):
        source = lax.rem(me + n - k, n)
        pltpu.make_async_remote_copy(
            src_ref=part_ref,
            dst_ref=out_ref.at[pl.ds(pl.multiple_of(source * rows, rows), rows)],
            send_sem=send_sem.at[k],
            recv_sem=recv_sem.at[k],
            device_id=(source, other),
            device_id_type=MESH,
        ).wait_recv()
    for copy in copies:
        copy.wait_send()


def ctx_gather(part, n, collective_id):
    rows, cols = part.shape
    return pl.pallas_call(
        functools.partial(_gather_kernel, n),
        out_shape=jax.ShapeDtypeStruct((n * rows, cols), part.dtype),
        in_specs=[pl.BlockSpec(memory_space=pltpu.VMEM)],
        out_specs=pl.BlockSpec(memory_space=pltpu.VMEM),
        scratch_shapes=[pltpu.SemaphoreType.DMA((n,)), pltpu.SemaphoreType.DMA((n,))],
        compiler_params=pltpu.CompilerParams(
            collective_id=collective_id, has_side_effects=True, vmem_limit_bytes=VMEM_LIMIT
        ),
    )(part)


def _scatter_sum(n, me, other, whole_ref, held, send_sem, recv_sem, rows):
    copies = []
    for k in range(1, n):
        target = lax.rem(me + k, n)
        copy = pltpu.make_async_remote_copy(
            src_ref=whole_ref.at[pl.ds(pl.multiple_of(target * rows, rows), rows)],
            dst_ref=held.at[k],
            send_sem=send_sem.at[k],
            recv_sem=recv_sem.at[k],
            device_id=(target, other),
            device_id_type=MESH,
        )
        copy.start()
        copies.append(copy)
    total = whole_ref[pl.ds(pl.multiple_of(me * rows, rows), rows), :].astype(jnp.float32)
    for k in range(1, n):
        source = lax.rem(me + n - k, n)
        pltpu.make_async_remote_copy(
            src_ref=whole_ref.at[pl.ds(0, rows)],
            dst_ref=held.at[k],
            send_sem=send_sem.at[k],
            recv_sem=recv_sem.at[k],
            device_id=(source, other),
            device_id_type=MESH,
        ).wait_recv()
        total = total + held[k].astype(jnp.float32)
    for copy in copies:
        copy.wait_send()
    return total


def _scatter_kernel(n, whole_ref, out_ref, held, send_sem, recv_sem):
    me = lax.axis_index("ctx")
    other = lax.axis_index("tp")
    rows = out_ref.shape[0]
    _enter(n, me, other)
    out_ref[...] = _scatter_sum(n, me, other, whole_ref, held, send_sem, recv_sem, rows)


def ctx_scatter(whole, n, collective_id):
    rows, cols = whole.shape[0] // n, whole.shape[1]
    return pl.pallas_call(
        functools.partial(_scatter_kernel, n),
        out_shape=jax.ShapeDtypeStruct((rows, cols), jnp.float32),
        in_specs=[pl.BlockSpec(memory_space=pltpu.VMEM)],
        out_specs=pl.BlockSpec(memory_space=pltpu.VMEM),
        scratch_shapes=[
            pltpu.VMEM((n, rows, cols), whole.dtype),
            pltpu.SemaphoreType.DMA((n,)),
            pltpu.SemaphoreType.DMA((n,)),
        ],
        compiler_params=pltpu.CompilerParams(
            collective_id=collective_id, has_side_effects=True, vmem_limit_bytes=VMEM_LIMIT
        ),
    )(whole)


def _sum_kernel(n, whole_ref, out_ref, held, mine, send_sem, recv_sem, send_back, recv_back):
    me = lax.axis_index("ctx")
    other = lax.axis_index("tp")
    rows = whole_ref.shape[0] // n
    _enter(n, me, other)
    mine[...] = _scatter_sum(n, me, other, whole_ref, held, send_sem, recv_sem, rows).astype(
        mine.dtype
    )
    copies = []
    for k in range(1, n):
        copy = pltpu.make_async_remote_copy(
            src_ref=mine,
            dst_ref=out_ref.at[pl.ds(pl.multiple_of(me * rows, rows), rows)],
            send_sem=send_back.at[k],
            recv_sem=recv_back.at[k],
            device_id=(lax.rem(me + k, n), other),
            device_id_type=MESH,
        )
        copy.start()
        copies.append(copy)
    out_ref[pl.ds(pl.multiple_of(me * rows, rows), rows), :] = mine[...]
    for k in range(1, n):
        source = lax.rem(me + n - k, n)
        pltpu.make_async_remote_copy(
            src_ref=mine,
            dst_ref=out_ref.at[pl.ds(pl.multiple_of(source * rows, rows), rows)],
            send_sem=send_back.at[k],
            recv_sem=recv_back.at[k],
            device_id=(source, other),
            device_id_type=MESH,
        ).wait_recv()
    for copy in copies:
        copy.wait_send()


def ctx_sum(whole, n, collective_id):
    rows, cols = whole.shape[0] // n, whole.shape[1]
    return pl.pallas_call(
        functools.partial(_sum_kernel, n),
        out_shape=jax.ShapeDtypeStruct(whole.shape, whole.dtype),
        in_specs=[pl.BlockSpec(memory_space=pltpu.VMEM)],
        out_specs=pl.BlockSpec(memory_space=pltpu.VMEM),
        scratch_shapes=[
            pltpu.VMEM((n, rows, cols), whole.dtype),
            pltpu.VMEM((rows, cols), whole.dtype),
            pltpu.SemaphoreType.DMA((n,)),
            pltpu.SemaphoreType.DMA((n,)),
            pltpu.SemaphoreType.DMA((n,)),
            pltpu.SemaphoreType.DMA((n,)),
        ],
        compiler_params=pltpu.CompilerParams(
            collective_id=collective_id, has_side_effects=True, vmem_limit_bytes=VMEM_LIMIT
        ),
    )(whole)


EPS = 1e-05
THETA = 1000000.0
NEGATIVE = -1e30


def rms_forward(values, norm_gain):
    inverse = lax.rsqrt(jnp.mean(values * values, axis=-1, keepdims=True) + EPS)
    return (values * inverse * norm_gain, inverse)


def rms_backward(values, inverse, norm_gain, upstream):
    scaled = upstream * norm_gain
    inner_mean = jnp.mean(scaled * values, axis=-1, keepdims=True)
    through = inverse * (scaled - values * inverse * inverse * inner_mean)
    return (through, upstream * values * inverse)


def rope_tables(positions, head_dim):
    halfway = head_dim // 2
    frequency = THETA ** (-(jnp.arange(halfway, dtype=jnp.float32) * 2.0 / head_dim))
    angles = positions.astype(jnp.float32)[:, None] * frequency[None, :]
    return (jnp.cos(angles)[:, None, :], jnp.sin(angles)[:, None, :])


def rope_apply(values, cosine, sine_table):
    halfway = values.shape[-1] // 2
    first_half = values[..., :halfway]
    second_half = values[..., halfway:]
    return jnp.concatenate(
        [
            first_half * cosine - second_half * sine_table,
            second_half * cosine + first_half * sine_table,
        ],
        axis=-1,
    )


def rope_back(upstream, cosine, sine_table):
    halfway = upstream.shape[-1] // 2
    first_half = upstream[..., :halfway]
    second_half = upstream[..., halfway:]
    return jnp.concatenate(
        [
            first_half * cosine + second_half * sine_table,
            second_half * cosine - first_half * sine_table,
        ],
        axis=-1,
    )


def row_places(block_map, holder, rows_total, place_count):
    piece_len = rows_total // 4
    within = jnp.arange(rows_total, dtype=jnp.int32)
    picked = jnp.sum(jnp.where(jnp.arange(place_count, dtype=jnp.int32) == holder, block_map, 0))
    later = within // piece_len % 2
    piece_index = jnp.where(later == 1, 2 * place_count - 1 - picked, picked)
    return piece_index * piece_len + within % piece_len


def span_places(block_map, first_anchor, shard_span, seq_rows, place_count):
    piece_len = seq_rows // 2
    anchors = first_anchor + jnp.arange(shard_span, dtype=jnp.int32)
    picked = jnp.sum(
        jnp.where(
            jnp.arange(place_count, dtype=jnp.int32)[None, :] == anchors[:, None],
            block_map[None, :],
            0,
        ),
        axis=1,
    )
    within = jnp.arange(seq_rows, dtype=jnp.int32)
    later = within // piece_len % 2
    piece_index = jnp.where(
        later[None, :] == 1, 2 * place_count - 1 - picked[:, None], picked[:, None]
    )
    return (piece_index * piece_len + (within % piece_len)[None, :]).reshape(shard_span * seq_rows)


def gather_rows(rows_low):
    return lax.all_gather(rows_low, "tp", axis=0, tiled=True)


def reduce_rows(partial_rows):
    return lax.psum_scatter(
        partial_rows.astype(jnp.bfloat16), "tp", scatter_dimension=0, tiled=True
    ).astype(jnp.float32)


def per_device(
    block_input,
    block_map,
    attn_gain,
    query_weight,
    key_weight,
    value_weight,
    query_gain,
    key_gain,
    output_weight,
    ffn_gain,
    gate_weight,
    up_weight,
    down_weight,
    cotangent,
):
    place_count = lax.axis_size("ctx")
    place_index = lax.axis_index("ctx")
    head_dim = query_gain.shape[0]
    query_heads = query_weight.shape[1] // head_dim
    kv_heads = key_weight.shape[1] // head_dim
    group_size = query_heads // kv_heads
    score_scale = 1.0 / math.sqrt(head_dim)
    shard_span = 4
    residual_in = block_input.astype(jnp.float32)
    normed_one, inverse_one = rms_forward(residual_in, attn_gain)
    rows_one = gather_rows(normed_one.astype(jnp.bfloat16))
    rows_total = rows_one.shape[0]
    seq_rows = rows_total // 2
    kv_width = kv_heads * head_dim
    own_places = row_places(block_map, place_index, rows_total, place_count)
    query_raw = jnp.dot(rows_one, query_weight, preferred_element_type=jnp.float32).reshape(
        rows_total, query_heads, head_dim
    )
    key_raw = jnp.dot(rows_one, key_weight, preferred_element_type=jnp.float32).reshape(
        rows_total, kv_heads, head_dim
    )
    values_own = jnp.dot(rows_one, value_weight, preferred_element_type=jnp.float32).astype(
        jnp.bfloat16
    )
    query_normed, query_inverse = rms_forward(query_raw, query_gain)
    key_normed, key_inverse = rms_forward(key_raw, key_gain)
    cosine, sine_table = rope_tables(own_places, head_dim)
    query_rot = rope_apply(query_normed, cosine, sine_table).astype(jnp.bfloat16)
    keys_own = (
        rope_apply(key_normed, cosine, sine_table)
        .astype(jnp.bfloat16)
        .reshape(rows_total, kv_width)
    )
    query_blocks = query_rot.reshape(2, seq_rows, kv_heads, group_size, head_dim)
    query_places = own_places[:seq_rows]

    whole_kv = ctx_gather(jnp.concatenate([keys_own, values_own], axis=1), place_count, 0)
    seq_kv = jnp.transpose(
        whole_kv.reshape(place_count, 2, seq_rows, 2 * kv_width), (1, 0, 2, 3)
    ).reshape(2, place_count * seq_rows, 2 * kv_width)
    key_heads = seq_kv[..., :kv_width].reshape(2, place_count * seq_rows, kv_heads, head_dim)
    value_heads = seq_kv[..., kv_width:].reshape(2, place_count * seq_rows, kv_heads, head_dim)
    key_places = span_places(block_map, 0, place_count, seq_rows, place_count)
    allowed = key_places[None, :] <= query_places[:, None]
    scores = (
        jnp.einsum(
            "sqhgd,skhd->shgqk", query_blocks, key_heads, preferred_element_type=jnp.float32
        )
        * score_scale
    )
    top = jnp.max(jnp.where(allowed, scores, NEGATIVE), axis=-1)
    weights = jnp.where(allowed, jnp.exp(scores - top[..., None]), 0.0)
    weight_total = jnp.sum(weights, axis=-1)
    weighted = jnp.einsum(
        "shgqk,skhd->shgqd",
        weights.astype(jnp.bfloat16),
        value_heads,
        preferred_element_type=jnp.float32,
    )
    log_total = top + jnp.log(weight_total)
    attn_rows = jnp.transpose(weighted / weight_total[..., None], (0, 3, 1, 2, 4))
    attn_low = attn_rows.reshape(rows_total, query_heads * head_dim).astype(jnp.bfloat16)
    residual_mid = residual_in + reduce_rows(
        jnp.dot(attn_low, output_weight, preferred_element_type=jnp.float32)
    )
    normed_two, inverse_two = rms_forward(residual_mid, ffn_gain)
    rows_two = gather_rows(normed_two.astype(jnp.bfloat16))
    gate_pre = jnp.dot(rows_two, gate_weight, preferred_element_type=jnp.float32)
    up_pre = jnp.dot(rows_two, up_weight, preferred_element_type=jnp.float32)
    gate_sig = jax.nn.sigmoid(gate_pre)
    activated = (gate_pre * gate_sig * up_pre).astype(jnp.bfloat16)
    block_output = residual_mid + reduce_rows(
        jnp.dot(activated, down_weight, preferred_element_type=jnp.float32)
    )
    grad_rows = gather_rows(cotangent)
    grad_down_t = jnp.dot(grad_rows.T, activated, preferred_element_type=jnp.float32)
    grad_act = jnp.dot(grad_rows, down_weight.T, preferred_element_type=jnp.float32)
    grad_gate_pre = (grad_act * up_pre * gate_sig * (1.0 + gate_pre * (1.0 - gate_sig))).astype(
        jnp.bfloat16
    )
    grad_up_pre = (grad_act * gate_pre * gate_sig).astype(jnp.bfloat16)
    grad_gate = jnp.dot(rows_two.T, grad_gate_pre, preferred_element_type=jnp.float32)
    grad_up = jnp.dot(rows_two.T, grad_up_pre, preferred_element_type=jnp.float32)
    grad_normed_two = reduce_rows(
        jnp.dot(grad_gate_pre, gate_weight.T, preferred_element_type=jnp.float32)
        + jnp.dot(grad_up_pre, up_weight.T, preferred_element_type=jnp.float32)
    )
    through_two, ffn_terms = rms_backward(residual_mid, inverse_two, ffn_gain, grad_normed_two)
    grad_mid = cotangent.astype(jnp.float32) + through_two
    grad_mid_rows = gather_rows(grad_mid.astype(jnp.bfloat16))
    grad_output_t = jnp.dot(grad_mid_rows.T, attn_low, preferred_element_type=jnp.float32)
    grad_attn = jnp.dot(grad_mid_rows, output_weight.T, preferred_element_type=jnp.float32).astype(
        jnp.bfloat16
    )
    grad_attn_blocks = grad_attn.reshape(2, seq_rows, kv_heads, group_size, head_dim)
    delta_rows = jnp.sum(grad_attn_blocks.astype(jnp.float32) * attn_rows, axis=-1)
    delta_rows = jnp.transpose(delta_rows, (0, 2, 3, 1))

    probs = jnp.where(allowed, jnp.exp(scores - log_total[..., None]), 0.0)
    grad_value_seq = jnp.einsum(
        "shgqk,sqhgd->skhd",
        probs.astype(jnp.bfloat16),
        grad_attn_blocks,
        preferred_element_type=jnp.float32,
    )
    grad_probs = jnp.einsum(
        "sqhgd,skhd->shgqk", grad_attn_blocks, value_heads, preferred_element_type=jnp.float32
    )
    grad_scores = (score_scale * probs * (grad_probs - delta_rows[..., None])).astype(jnp.bfloat16)
    query_acc = jnp.einsum(
        "shgqk,skhd->sqhgd", grad_scores, key_heads, preferred_element_type=jnp.float32
    )
    grad_key_seq = jnp.einsum(
        "shgqk,sqhgd->skhd", grad_scores, query_blocks, preferred_element_type=jnp.float32
    )
    grad_kv_seq = jnp.concatenate(
        [
            grad_key_seq.reshape(2, place_count, seq_rows, kv_width),
            grad_value_seq.reshape(2, place_count, seq_rows, kv_width),
        ],
        axis=-1,
    )
    grad_kv_all = jnp.transpose(grad_kv_seq, (1, 0, 2, 3)).reshape(
        place_count * rows_total, 2 * kv_width
    )
    grad_kv_flat = ctx_scatter(
        grad_kv_all.astype(jnp.bfloat16),
        place_count,
        1,
    )
    grad_keys_flat, grad_values_flat = grad_kv_flat[:, :kv_width], grad_kv_flat[:, kv_width:]
    grad_query_rot = query_acc.reshape(rows_total, query_heads, head_dim)
    grad_key_rot = grad_keys_flat.reshape(rows_total, kv_heads, head_dim)
    grad_query_raw, query_terms = rms_backward(
        query_raw, query_inverse, query_gain, rope_back(grad_query_rot, cosine, sine_table)
    )
    grad_key_raw, key_terms = rms_backward(
        key_raw, key_inverse, key_gain, rope_back(grad_key_rot, cosine, sine_table)
    )
    grad_query_low = grad_query_raw.reshape(rows_total, query_heads * head_dim).astype(jnp.bfloat16)
    grad_key_low = grad_key_raw.reshape(rows_total, kv_width).astype(jnp.bfloat16)
    grad_value_low = grad_values_flat.astype(jnp.bfloat16)
    grad_query = jnp.dot(rows_one.T, grad_query_low, preferred_element_type=jnp.float32)
    grad_key = jnp.dot(rows_one.T, grad_key_low, preferred_element_type=jnp.float32)
    grad_value = jnp.dot(rows_one.T, grad_value_low, preferred_element_type=jnp.float32)
    grad_normed_one = reduce_rows(
        jnp.dot(grad_query_low, query_weight.T, preferred_element_type=jnp.float32)
        + jnp.dot(grad_key_low, key_weight.T, preferred_element_type=jnp.float32)
        + jnp.dot(grad_value_low, value_weight.T, preferred_element_type=jnp.float32)
    )
    through_one, attn_terms = rms_backward(residual_in, inverse_one, attn_gain, grad_normed_one)
    input_grad = grad_mid + through_one
    weight_parts = (grad_query, grad_key, grad_value, grad_output_t, grad_gate, grad_up, grad_down_t)
    widths = [part.shape[1] for part in weight_parts]
    summed = ctx_sum(
        jnp.concatenate([part.astype(jnp.bfloat16) for part in weight_parts], axis=1),
        place_count,
        2,
    ).astype(jnp.float32)
    offsets = [sum(widths[:k]) for k in range(len(widths) + 1)]
    shared_query, shared_key, shared_value, output_t, shared_gate, shared_up, down_t = (
        summed[:, offsets[k] : offsets[k + 1]] for k in range(len(widths))
    )
    shared_output = output_t.T
    shared_down = down_t.T
    gain_parts = (
        jnp.sum(attn_terms, axis=0),
        jnp.sum(query_terms, axis=(0, 1)),
        jnp.sum(key_terms, axis=(0, 1)),
        jnp.sum(ffn_terms, axis=0),
    )
    gain_sizes = [part.shape[0] for part in gain_parts]
    gains = lax.psum(jnp.concatenate(gain_parts), ("ctx", "tp"))
    gain_attn = gains[: gain_sizes[0]]
    gain_query = gains[gain_sizes[0] : gain_sizes[0] + gain_sizes[1]]
    gain_key = gains[gain_sizes[0] + gain_sizes[1] : gain_sizes[0] + gain_sizes[1] + gain_sizes[2]]
    gain_ffn = gains[gain_sizes[0] + gain_sizes[1] + gain_sizes[2] :]
    return (
        block_output,
        input_grad,
        gain_attn,
        shared_query,
        shared_key,
        shared_value,
        gain_query,
        gain_key,
        shared_output,
        gain_ffn,
        shared_gate,
        shared_up,
        shared_down,
    )


def solution(mesh):
    return jax.shard_map(
        per_device,
        mesh=mesh,
        in_specs=(
            P(("ctx", "tp"), None),
            P(),
            P(),
            P(None, "tp"),
            P(None, "tp"),
            P(None, "tp"),
            P(),
            P(),
            P("tp", None),
            P(),
            P(None, "tp"),
            P(None, "tp"),
            P("tp", None),
            P(("ctx", "tp"), None),
        ),
        out_specs=(
            P(("ctx", "tp"), None),
            P(("ctx", "tp"), None),
            P(),
            P(None, "tp"),
            P(None, "tp"),
            P(None, "tp"),
            P(),
            P(),
            P("tp", None),
            P(),
            P(None, "tp"),
            P(None, "tp"),
            P("tp", None),
        ),
        check_vma=False,
    )
```

```python
import functools
import math

import jax
import jax.numpy as jnp
from jax import lax
from jax.experimental import pallas as pl
from jax.experimental.pallas import tpu as pltpu
from jax.sharding import PartitionSpec as P

MESH = pl.DeviceIdType.MESH
VMEM_LIMIT = 60 * 1024 * 1024


def _enter(n, me, peer_axis):
    barrier = pltpu.get_barrier_semaphore()
    for k in range(1, n):
        pl.semaphore_signal(
            barrier, 1, device_id=(lax.rem(me + k, n), peer_axis), device_id_type=MESH
        )
    pl.semaphore_wait(barrier, n - 1)


def _gather_kernel(n, part_ref, out_ref, send_sem, recv_sem):
    me = lax.axis_index("ctx")
    other = lax.axis_index("tp")
    rows = part_ref.shape[0]
    _enter(n, me, other)
    copies = []
    for k in range(1, n):
        copy = pltpu.make_async_remote_copy(
            src_ref=part_ref,
            dst_ref=out_ref.at[pl.ds(pl.multiple_of(me * rows, rows), rows)],
            send_sem=send_sem.at[k],
            recv_sem=recv_sem.at[k],
            device_id=(lax.rem(me + k, n), other),
            device_id_type=MESH,
        )
        copy.start()
        copies.append(copy)
    out_ref[pl.ds(pl.multiple_of(me * rows, rows), rows), :] = part_ref[...]
    for k in range(1, n):
        source = lax.rem(me + n - k, n)
        pltpu.make_async_remote_copy(
            src_ref=part_ref,
            dst_ref=out_ref.at[pl.ds(pl.multiple_of(source * rows, rows), rows)],
            send_sem=send_sem.at[k],
            recv_sem=recv_sem.at[k],
            device_id=(source, other),
            device_id_type=MESH,
        ).wait_recv()
    for copy in copies:
        copy.wait_send()


def ctx_gather(part, n, collective_id):
    rows, cols = part.shape
    return pl.pallas_call(
        functools.partial(_gather_kernel, n),
        out_shape=jax.ShapeDtypeStruct((n * rows, cols), part.dtype),
        in_specs=[pl.BlockSpec(memory_space=pltpu.VMEM)],
        out_specs=pl.BlockSpec(memory_space=pltpu.VMEM),
        scratch_shapes=[pltpu.SemaphoreType.DMA((n,)), pltpu.SemaphoreType.DMA((n,))],
        compiler_params=pltpu.CompilerParams(
            collective_id=collective_id, has_side_effects=True, vmem_limit_bytes=VMEM_LIMIT
        ),
    )(part)


def _scatter_sum(n, me, other, whole_ref, held, send_sem, recv_sem, rows):
    copies = []
    for k in range(1, n):
        target = lax.rem(me + k, n)
        copy = pltpu.make_async_remote_copy(
            src_ref=whole_ref.at[pl.ds(pl.multiple_of(target * rows, rows), rows)],
            dst_ref=held.at[k],
            send_sem=send_sem.at[k],
            recv_sem=recv_sem.at[k],
            device_id=(target, other),
            device_id_type=MESH,
        )
        copy.start()
        copies.append(copy)
    total = whole_ref[pl.ds(pl.multiple_of(me * rows, rows), rows), :].astype(jnp.float32)
    for k in range(1, n):
        source = lax.rem(me + n - k, n)
        pltpu.make_async_remote_copy(
            src_ref=whole_ref.at[pl.ds(0, rows)],
            dst_ref=held.at[k],
            send_sem=send_sem.at[k],
            recv_sem=recv_sem.at[k],
            device_id=(source, other),
            device_id_type=MESH,
        ).wait_recv()
        total = total + held[k].astype(jnp.float32)
    for copy in copies:
        copy.wait_send()
    return total


def _scatter_kernel(n, whole_ref, out_ref, held, send_sem, recv_sem):
    me = lax.axis_index("ctx")
    other = lax.axis_index("tp")
    rows = out_ref.shape[0]
    _enter(n, me, other)
    out_ref[...] = _scatter_sum(n, me, other, whole_ref, held, send_sem, recv_sem, rows)


def ctx_scatter(whole, n, collective_id):
    rows, cols = whole.shape[0] // n, whole.shape[1]
    return pl.pallas_call(
        functools.partial(_scatter_kernel, n),
        out_shape=jax.ShapeDtypeStruct((rows, cols), jnp.float32),
        in_specs=[pl.BlockSpec(memory_space=pltpu.VMEM)],
        out_specs=pl.BlockSpec(memory_space=pltpu.VMEM),
        scratch_shapes=[
            pltpu.VMEM((n, rows, cols), whole.dtype),
            pltpu.SemaphoreType.DMA((n,)),
            pltpu.SemaphoreType.DMA((n,)),
        ],
        compiler_params=pltpu.CompilerParams(
            collective_id=collective_id, has_side_effects=True, vmem_limit_bytes=VMEM_LIMIT
        ),
    )(whole)


def _sum_kernel(
    n,
    whole_ref,
    extra_ref,
    out_ref,
    extra_out,
    held,
    mine,
    extra_held,
    send_sem,
    recv_sem,
    send_back,
    recv_back,
    send_extra,
    recv_extra,
):
    me = lax.axis_index("ctx")
    other = lax.axis_index("tp")
    rows = whole_ref.shape[0] // n
    _enter(n, me, other)
    extra_copies = []
    for k in range(1, n):
        copy = pltpu.make_async_remote_copy(
            src_ref=extra_ref,
            dst_ref=extra_held.at[k],
            send_sem=send_extra.at[k],
            recv_sem=recv_extra.at[k],
            device_id=(lax.rem(me + k, n), other),
            device_id_type=MESH,
        )
        copy.start()
        extra_copies.append(copy)
    mine[...] = _scatter_sum(n, me, other, whole_ref, held, send_sem, recv_sem, rows).astype(
        mine.dtype
    )
    copies = []
    for k in range(1, n):
        copy = pltpu.make_async_remote_copy(
            src_ref=mine,
            dst_ref=out_ref.at[pl.ds(pl.multiple_of(me * rows, rows), rows)],
            send_sem=send_back.at[k],
            recv_sem=recv_back.at[k],
            device_id=(lax.rem(me + k, n), other),
            device_id_type=MESH,
        )
        copy.start()
        copies.append(copy)
    out_ref[pl.ds(pl.multiple_of(me * rows, rows), rows), :] = mine[...]
    extra_total = extra_ref[...]
    for k in range(1, n):
        source = lax.rem(me + n - k, n)
        pltpu.make_async_remote_copy(
            src_ref=extra_ref,
            dst_ref=extra_held.at[k],
            send_sem=send_extra.at[k],
            recv_sem=recv_extra.at[k],
            device_id=(source, other),
            device_id_type=MESH,
        ).wait_recv()
        extra_total = extra_total + extra_held[k]
    extra_out[...] = extra_total
    for k in range(1, n):
        source = lax.rem(me + n - k, n)
        pltpu.make_async_remote_copy(
            src_ref=mine,
            dst_ref=out_ref.at[pl.ds(pl.multiple_of(source * rows, rows), rows)],
            send_sem=send_back.at[k],
            recv_sem=recv_back.at[k],
            device_id=(source, other),
            device_id_type=MESH,
        ).wait_recv()
    for copy in copies + extra_copies:
        copy.wait_send()


def ctx_sum(whole, extra, n, collective_id):
    rows, cols = whole.shape[0] // n, whole.shape[1]
    return pl.pallas_call(
        functools.partial(_sum_kernel, n),
        out_shape=(
            jax.ShapeDtypeStruct(whole.shape, whole.dtype),
            jax.ShapeDtypeStruct(extra.shape, extra.dtype),
        ),
        in_specs=[pl.BlockSpec(memory_space=pltpu.VMEM)] * 2,
        out_specs=(pl.BlockSpec(memory_space=pltpu.VMEM),) * 2,
        scratch_shapes=[
            pltpu.VMEM((n, rows, cols), whole.dtype),
            pltpu.VMEM((rows, cols), whole.dtype),
            pltpu.VMEM((n,) + extra.shape, extra.dtype),
        ]
        + [pltpu.SemaphoreType.DMA((n,))] * 6,
        compiler_params=pltpu.CompilerParams(
            collective_id=collective_id, has_side_effects=True, vmem_limit_bytes=VMEM_LIMIT
        ),
    )(whole, extra)


EPS = 1e-05
THETA = 1000000.0
NEGATIVE = -1e30


def rms_forward(values, norm_gain):
    inverse = lax.rsqrt(jnp.mean(values * values, axis=-1, keepdims=True) + EPS)
    return (values * inverse * norm_gain, inverse)


def rms_backward(values, inverse, norm_gain, upstream):
    scaled = upstream * norm_gain
    inner_mean = jnp.mean(scaled * values, axis=-1, keepdims=True)
    through = inverse * (scaled - values * inverse * inverse * inner_mean)
    return (through, upstream * values * inverse)


def rope_tables(positions, head_dim):
    halfway = head_dim // 2
    frequency = THETA ** (-(jnp.arange(halfway, dtype=jnp.float32) * 2.0 / head_dim))
    angles = positions.astype(jnp.float32)[:, None] * frequency[None, :]
    return (jnp.cos(angles)[:, None, :], jnp.sin(angles)[:, None, :])


def rope_apply(values, cosine, sine_table):
    halfway = values.shape[-1] // 2
    first_half = values[..., :halfway]
    second_half = values[..., halfway:]
    return jnp.concatenate(
        [
            first_half * cosine - second_half * sine_table,
            second_half * cosine + first_half * sine_table,
        ],
        axis=-1,
    )


def rope_back(upstream, cosine, sine_table):
    halfway = upstream.shape[-1] // 2
    first_half = upstream[..., :halfway]
    second_half = upstream[..., halfway:]
    return jnp.concatenate(
        [
            first_half * cosine + second_half * sine_table,
            second_half * cosine - first_half * sine_table,
        ],
        axis=-1,
    )


def row_places(block_map, holder, rows_total, place_count):
    piece_len = rows_total // 4
    within = jnp.arange(rows_total, dtype=jnp.int32)
    picked = jnp.sum(jnp.where(jnp.arange(place_count, dtype=jnp.int32) == holder, block_map, 0))
    later = within // piece_len % 2
    piece_index = jnp.where(later == 1, 2 * place_count - 1 - picked, picked)
    return piece_index * piece_len + within % piece_len


def span_places(block_map, first_anchor, shard_span, seq_rows, place_count):
    piece_len = seq_rows // 2
    anchors = first_anchor + jnp.arange(shard_span, dtype=jnp.int32)
    picked = jnp.sum(
        jnp.where(
            jnp.arange(place_count, dtype=jnp.int32)[None, :] == anchors[:, None],
            block_map[None, :],
            0,
        ),
        axis=1,
    )
    within = jnp.arange(seq_rows, dtype=jnp.int32)
    later = within // piece_len % 2
    piece_index = jnp.where(
        later[None, :] == 1, 2 * place_count - 1 - picked[:, None], picked[:, None]
    )
    return (piece_index * piece_len + (within % piece_len)[None, :]).reshape(shard_span * seq_rows)


def gather_rows(rows_low):
    return lax.all_gather(rows_low, "tp", axis=0, tiled=True)


def reduce_rows(partial_rows):
    return lax.psum_scatter(
        partial_rows.astype(jnp.bfloat16), "tp", scatter_dimension=0, tiled=True
    ).astype(jnp.float32)


def per_device(
    block_input,
    block_map,
    attn_gain,
    query_weight,
    key_weight,
    value_weight,
    query_gain,
    key_gain,
    output_weight,
    ffn_gain,
    gate_weight,
    up_weight,
    down_weight,
    cotangent,
):
    place_count = lax.axis_size("ctx")
    place_index = lax.axis_index("ctx")
    head_dim = query_gain.shape[0]
    query_heads = query_weight.shape[1] // head_dim
    kv_heads = key_weight.shape[1] // head_dim
    group_size = query_heads // kv_heads
    score_scale = 1.0 / math.sqrt(head_dim)
    shard_span = 4
    residual_in = block_input.astype(jnp.float32)
    normed_one, inverse_one = rms_forward(residual_in, attn_gain)
    rows_one = gather_rows(normed_one.astype(jnp.bfloat16))
    rows_total = rows_one.shape[0]
    seq_rows = rows_total // 2
    kv_width = kv_heads * head_dim
    own_places = row_places(block_map, place_index, rows_total, place_count)
    query_raw = jnp.dot(rows_one, query_weight, preferred_element_type=jnp.float32).reshape(
        rows_total, query_heads, head_dim
    )
    key_raw = jnp.dot(rows_one, key_weight, preferred_element_type=jnp.float32).reshape(
        rows_total, kv_heads, head_dim
    )
    values_own = jnp.dot(rows_one, value_weight, preferred_element_type=jnp.float32).astype(
        jnp.bfloat16
    )
    query_normed, query_inverse = rms_forward(query_raw, query_gain)
    key_normed, key_inverse = rms_forward(key_raw, key_gain)
    cosine, sine_table = rope_tables(own_places, head_dim)
    query_rot = rope_apply(query_normed, cosine, sine_table).astype(jnp.bfloat16)
    keys_own = (
        rope_apply(key_normed, cosine, sine_table)
        .astype(jnp.bfloat16)
        .reshape(rows_total, kv_width)
    )
    query_blocks = query_rot.reshape(2, seq_rows, kv_heads, group_size, head_dim)
    query_places = own_places[:seq_rows]

    whole_kv = ctx_gather(jnp.concatenate([keys_own, values_own], axis=1), place_count, 0)
    seq_kv = jnp.transpose(
        whole_kv.reshape(place_count, 2, seq_rows, 2 * kv_width), (1, 0, 2, 3)
    ).reshape(2, place_count * seq_rows, 2 * kv_width)
    key_heads = seq_kv[..., :kv_width].reshape(2, place_count * seq_rows, kv_heads, head_dim)
    value_heads = seq_kv[..., kv_width:].reshape(2, place_count * seq_rows, kv_heads, head_dim)
    key_places = span_places(block_map, 0, place_count, seq_rows, place_count)
    allowed = key_places[None, :] <= query_places[:, None]
    scores = (
        jnp.einsum(
            "sqhgd,skhd->shgqk", query_blocks, key_heads, preferred_element_type=jnp.float32
        )
        * score_scale
    )
    top = jnp.max(jnp.where(allowed, scores, NEGATIVE), axis=-1)
    weights = jnp.where(allowed, jnp.exp(scores - top[..., None]), 0.0)
    weight_total = jnp.sum(weights, axis=-1)
    weighted = jnp.einsum(
        "shgqk,skhd->shgqd",
        weights.astype(jnp.bfloat16),
        value_heads,
        preferred_element_type=jnp.float32,
    )
    log_total = top + jnp.log(weight_total)
    attn_rows = jnp.transpose(weighted / weight_total[..., None], (0, 3, 1, 2, 4))
    attn_low = attn_rows.reshape(rows_total, query_heads * head_dim).astype(jnp.bfloat16)
    residual_mid = residual_in + reduce_rows(
        jnp.dot(attn_low, output_weight, preferred_element_type=jnp.float32)
    )
    normed_two, inverse_two = rms_forward(residual_mid, ffn_gain)
    rows_two = gather_rows(normed_two.astype(jnp.bfloat16))
    gate_pre = jnp.dot(rows_two, gate_weight, preferred_element_type=jnp.float32)
    up_pre = jnp.dot(rows_two, up_weight, preferred_element_type=jnp.float32)
    gate_sig = jax.nn.sigmoid(gate_pre)
    activated = (gate_pre * gate_sig * up_pre).astype(jnp.bfloat16)
    block_output = residual_mid + reduce_rows(
        jnp.dot(activated, down_weight, preferred_element_type=jnp.float32)
    )
    grad_rows = gather_rows(cotangent)
    grad_down_t = jnp.dot(grad_rows.T, activated, preferred_element_type=jnp.float32)
    grad_act = jnp.dot(grad_rows, down_weight.T, preferred_element_type=jnp.float32)
    grad_gate_pre = (grad_act * up_pre * gate_sig * (1.0 + gate_pre * (1.0 - gate_sig))).astype(
        jnp.bfloat16
    )
    grad_up_pre = (grad_act * gate_pre * gate_sig).astype(jnp.bfloat16)
    grad_gate = jnp.dot(rows_two.T, grad_gate_pre, preferred_element_type=jnp.float32)
    grad_up = jnp.dot(rows_two.T, grad_up_pre, preferred_element_type=jnp.float32)
    grad_normed_two = reduce_rows(
        jnp.dot(grad_gate_pre, gate_weight.T, preferred_element_type=jnp.float32)
        + jnp.dot(grad_up_pre, up_weight.T, preferred_element_type=jnp.float32)
    )
    through_two, ffn_terms = rms_backward(residual_mid, inverse_two, ffn_gain, grad_normed_two)
    grad_mid = cotangent.astype(jnp.float32) + through_two
    grad_mid_rows = gather_rows(grad_mid.astype(jnp.bfloat16))
    grad_output_t = jnp.dot(grad_mid_rows.T, attn_low, preferred_element_type=jnp.float32)
    grad_attn = jnp.dot(grad_mid_rows, output_weight.T, preferred_element_type=jnp.float32).astype(
        jnp.bfloat16
    )
    grad_attn_blocks = grad_attn.reshape(2, seq_rows, kv_heads, group_size, head_dim)
    delta_rows = jnp.sum(grad_attn_blocks.astype(jnp.float32) * attn_rows, axis=-1)
    delta_rows = jnp.transpose(delta_rows, (0, 2, 3, 1))

    probs = jnp.where(allowed, jnp.exp(scores - log_total[..., None]), 0.0)
    grad_value_seq = jnp.einsum(
        "shgqk,sqhgd->skhd",
        probs.astype(jnp.bfloat16),
        grad_attn_blocks,
        preferred_element_type=jnp.float32,
    )
    grad_probs = jnp.einsum(
        "sqhgd,skhd->shgqk", grad_attn_blocks, value_heads, preferred_element_type=jnp.float32
    )
    grad_scores = (score_scale * probs * (grad_probs - delta_rows[..., None])).astype(jnp.bfloat16)
    query_acc = jnp.einsum(
        "shgqk,skhd->sqhgd", grad_scores, key_heads, preferred_element_type=jnp.float32
    )
    grad_key_seq = jnp.einsum(
        "shgqk,sqhgd->skhd", grad_scores, query_blocks, preferred_element_type=jnp.float32
    )
    grad_kv_seq = jnp.concatenate(
        [
            grad_key_seq.reshape(2, place_count, seq_rows, kv_width),
            grad_value_seq.reshape(2, place_count, seq_rows, kv_width),
        ],
        axis=-1,
    )
    grad_kv_all = jnp.transpose(grad_kv_seq, (1, 0, 2, 3)).reshape(
        place_count * rows_total, 2 * kv_width
    )
    grad_kv_flat = ctx_scatter(
        grad_kv_all.astype(jnp.bfloat16),
        place_count,
        1,
    )
    grad_keys_flat, grad_values_flat = grad_kv_flat[:, :kv_width], grad_kv_flat[:, kv_width:]
    grad_query_rot = query_acc.reshape(rows_total, query_heads, head_dim)
    grad_key_rot = grad_keys_flat.reshape(rows_total, kv_heads, head_dim)
    grad_query_raw, query_terms = rms_backward(
        query_raw, query_inverse, query_gain, rope_back(grad_query_rot, cosine, sine_table)
    )
    grad_key_raw, key_terms = rms_backward(
        key_raw, key_inverse, key_gain, rope_back(grad_key_rot, cosine, sine_table)
    )
    grad_query_low = grad_query_raw.reshape(rows_total, query_heads * head_dim).astype(jnp.bfloat16)
    grad_key_low = grad_key_raw.reshape(rows_total, kv_width).astype(jnp.bfloat16)
    grad_value_low = grad_values_flat.astype(jnp.bfloat16)
    grad_query = jnp.dot(rows_one.T, grad_query_low, preferred_element_type=jnp.float32)
    grad_key = jnp.dot(rows_one.T, grad_key_low, preferred_element_type=jnp.float32)
    grad_value = jnp.dot(rows_one.T, grad_value_low, preferred_element_type=jnp.float32)
    grad_normed_one = reduce_rows(
        jnp.dot(grad_query_low, query_weight.T, preferred_element_type=jnp.float32)
        + jnp.dot(grad_key_low, key_weight.T, preferred_element_type=jnp.float32)
        + jnp.dot(grad_value_low, value_weight.T, preferred_element_type=jnp.float32)
    )
    through_one, attn_terms = rms_backward(residual_in, inverse_one, attn_gain, grad_normed_one)
    input_grad = grad_mid + through_one
    weight_parts = (grad_query, grad_key, grad_value, grad_output_t, grad_gate, grad_up, grad_down_t)
    widths = [part.shape[1] for part in weight_parts]
    gain_parts = (
        jnp.sum(attn_terms, axis=0),
        jnp.sum(query_terms, axis=(0, 1)),
        jnp.sum(key_terms, axis=(0, 1)),
        jnp.sum(ffn_terms, axis=0),
    )
    gain_sizes = [part.shape[0] for part in gain_parts]
    gain_flat = lax.psum(jnp.concatenate(gain_parts), "tp")
    gain_pad = -gain_flat.shape[0] % 1024
    summed, gains = ctx_sum(
        jnp.concatenate([part.astype(jnp.bfloat16) for part in weight_parts], axis=1),
        jnp.pad(gain_flat, (0, gain_pad)).reshape(8, -1),
        place_count,
        2,
    )
    summed = summed.astype(jnp.float32)
    gains = gains.reshape(-1)
    offsets = [sum(widths[:k]) for k in range(len(widths) + 1)]
    shared_query, shared_key, shared_value, output_t, shared_gate, shared_up, down_t = (
        summed[:, offsets[k] : offsets[k + 1]] for k in range(len(widths))
    )
    shared_output = output_t.T
    shared_down = down_t.T
    gain_attn = gains[: gain_sizes[0]]
    gain_query = gains[gain_sizes[0] : gain_sizes[0] + gain_sizes[1]]
    gain_key = gains[gain_sizes[0] + gain_sizes[1] : gain_sizes[0] + gain_sizes[1] + gain_sizes[2]]
    gain_ffn = gains[gain_sizes[0] + gain_sizes[1] + gain_sizes[2] : sum(gain_sizes)]
    return (
        block_output,
        input_grad,
        gain_attn,
        shared_query,
        shared_key,
        shared_value,
        gain_query,
        gain_key,
        shared_output,
        gain_ffn,
        shared_gate,
        shared_up,
        shared_down,
    )


def solution(mesh):
    return jax.shard_map(
        per_device,
        mesh=mesh,
        in_specs=(
            P(("ctx", "tp"), None),
            P(),
            P(),
            P(None, "tp"),
            P(None, "tp"),
            P(None, "tp"),
            P(),
            P(),
            P("tp", None),
            P(),
            P(None, "tp"),
            P(None, "tp"),
            P("tp", None),
            P(("ctx", "tp"), None),
        ),
        out_specs=(
            P(("ctx", "tp"), None),
            P(("ctx", "tp"), None),
            P(),
            P(None, "tp"),
            P(None, "tp"),
            P(None, "tp"),
            P(),
            P(),
            P("tp", None),
            P(),
            P(None, "tp"),
            P(None, "tp"),
            P("tp", None),
        ),
        check_vma=False,
    )
```

```python
import functools
import math

import jax
import jax.numpy as jnp
from jax import lax
from jax.experimental import pallas as pl
from jax.experimental.pallas import tpu as pltpu
from jax.sharding import PartitionSpec as P

MESH = pl.DeviceIdType.MESH
VMEM_LIMIT = 60 * 1024 * 1024


def _shifts(n):
    order = []
    for k in range(1, n // 2 + 1):
        order.append(k)
        if n - k != k:
            order.append(n - k)
    return order


def _enter(n, me, peer_axis):
    barrier = pltpu.get_barrier_semaphore()
    for k in _shifts(n):
        pl.semaphore_signal(
            barrier, 1, device_id=(lax.rem(me + k, n), peer_axis), device_id_type=MESH
        )
    pl.semaphore_wait(barrier, n - 1)


def _gather_kernel(n, part_ref, out_ref, send_sem, recv_sem):
    me = lax.axis_index("ctx")
    other = lax.axis_index("tp")
    rows = part_ref.shape[0]
    _enter(n, me, other)
    copies = []
    for k in _shifts(n):
        copy = pltpu.make_async_remote_copy(
            src_ref=part_ref,
            dst_ref=out_ref.at[pl.ds(pl.multiple_of(me * rows, rows), rows)],
            send_sem=send_sem.at[k],
            recv_sem=recv_sem.at[k],
            device_id=(lax.rem(me + k, n), other),
            device_id_type=MESH,
        )
        copy.start()
        copies.append(copy)
    out_ref[pl.ds(pl.multiple_of(me * rows, rows), rows), :] = part_ref[...]
    for k in _shifts(n):
        source = lax.rem(me + n - k, n)
        pltpu.make_async_remote_copy(
            src_ref=part_ref,
            dst_ref=out_ref.at[pl.ds(pl.multiple_of(source * rows, rows), rows)],
            send_sem=send_sem.at[k],
            recv_sem=recv_sem.at[k],
            device_id=(source, other),
            device_id_type=MESH,
        ).wait_recv()
    for copy in copies:
        copy.wait_send()


def ctx_gather(part, n, collective_id):
    rows, cols = part.shape
    return pl.pallas_call(
        functools.partial(_gather_kernel, n),
        out_shape=jax.ShapeDtypeStruct((n * rows, cols), part.dtype),
        in_specs=[pl.BlockSpec(memory_space=pltpu.VMEM)],
        out_specs=pl.BlockSpec(memory_space=pltpu.VMEM),
        scratch_shapes=[pltpu.SemaphoreType.DMA((n,)), pltpu.SemaphoreType.DMA((n,))],
        compiler_params=pltpu.CompilerParams(
            collective_id=collective_id, has_side_effects=True, vmem_limit_bytes=VMEM_LIMIT
        ),
    )(part)


def _scatter_sum(n, me, other, whole_ref, held, send_sem, recv_sem, rows):
    copies = []
    for k in _shifts(n):
        target = lax.rem(me + k, n)
        copy = pltpu.make_async_remote_copy(
            src_ref=whole_ref.at[pl.ds(pl.multiple_of(target * rows, rows), rows)],
            dst_ref=held.at[k],
            send_sem=send_sem.at[k],
            recv_sem=recv_sem.at[k],
            device_id=(target, other),
            device_id_type=MESH,
        )
        copy.start()
        copies.append(copy)
    total = whole_ref[pl.ds(pl.multiple_of(me * rows, rows), rows), :].astype(jnp.float32)
    for k in _shifts(n):
        source = lax.rem(me + n - k, n)
        pltpu.make_async_remote_copy(
            src_ref=whole_ref.at[pl.ds(0, rows)],
            dst_ref=held.at[k],
            send_sem=send_sem.at[k],
            recv_sem=recv_sem.at[k],
            device_id=(source, other),
            device_id_type=MESH,
        ).wait_recv()
        total = total + held[k].astype(jnp.float32)
    for copy in copies:
        copy.wait_send()
    return total


def _scatter_kernel(n, whole_ref, out_ref, held, send_sem, recv_sem):
    me = lax.axis_index("ctx")
    other = lax.axis_index("tp")
    rows = out_ref.shape[0]
    _enter(n, me, other)
    out_ref[...] = _scatter_sum(n, me, other, whole_ref, held, send_sem, recv_sem, rows)


def ctx_scatter(whole, n, collective_id):
    rows, cols = whole.shape[0] // n, whole.shape[1]
    return pl.pallas_call(
        functools.partial(_scatter_kernel, n),
        out_shape=jax.ShapeDtypeStruct((rows, cols), jnp.float32),
        in_specs=[pl.BlockSpec(memory_space=pltpu.VMEM)],
        out_specs=pl.BlockSpec(memory_space=pltpu.VMEM),
        scratch_shapes=[
            pltpu.VMEM((n, rows, cols), whole.dtype),
            pltpu.SemaphoreType.DMA((n,)),
            pltpu.SemaphoreType.DMA((n,)),
        ],
        compiler_params=pltpu.CompilerParams(
            collective_id=collective_id, has_side_effects=True, vmem_limit_bytes=VMEM_LIMIT
        ),
    )(whole)


def _sum_kernel(
    n,
    whole_ref,
    extra_ref,
    out_ref,
    extra_out,
    held,
    mine,
    extra_held,
    send_sem,
    recv_sem,
    send_back,
    recv_back,
    send_extra,
    recv_extra,
):
    me = lax.axis_index("ctx")
    other = lax.axis_index("tp")
    rows = whole_ref.shape[0] // n
    _enter(n, me, other)
    extra_copies = []
    for k in _shifts(n):
        copy = pltpu.make_async_remote_copy(
            src_ref=extra_ref,
            dst_ref=extra_held.at[k],
            send_sem=send_extra.at[k],
            recv_sem=recv_extra.at[k],
            device_id=(lax.rem(me + k, n), other),
            device_id_type=MESH,
        )
        copy.start()
        extra_copies.append(copy)
    mine[...] = _scatter_sum(n, me, other, whole_ref, held, send_sem, recv_sem, rows).astype(
        mine.dtype
    )
    copies = []
    for k in _shifts(n):
        copy = pltpu.make_async_remote_copy(
            src_ref=mine,
            dst_ref=out_ref.at[pl.ds(pl.multiple_of(me * rows, rows), rows)],
            send_sem=send_back.at[k],
            recv_sem=recv_back.at[k],
            device_id=(lax.rem(me + k, n), other),
            device_id_type=MESH,
        )
        copy.start()
        copies.append(copy)
    out_ref[pl.ds(pl.multiple_of(me * rows, rows), rows), :] = mine[...]
    extra_total = extra_ref[...]
    for k in _shifts(n):
        source = lax.rem(me + n - k, n)
        pltpu.make_async_remote_copy(
            src_ref=extra_ref,
            dst_ref=extra_held.at[k],
            send_sem=send_extra.at[k],
            recv_sem=recv_extra.at[k],
            device_id=(source, other),
            device_id_type=MESH,
        ).wait_recv()
        extra_total = extra_total + extra_held[k]
    extra_out[...] = extra_total
    for k in _shifts(n):
        source = lax.rem(me + n - k, n)
        pltpu.make_async_remote_copy(
            src_ref=mine,
            dst_ref=out_ref.at[pl.ds(pl.multiple_of(source * rows, rows), rows)],
            send_sem=send_back.at[k],
            recv_sem=recv_back.at[k],
            device_id=(source, other),
            device_id_type=MESH,
        ).wait_recv()
    for copy in copies + extra_copies:
        copy.wait_send()


def ctx_sum(whole, extra, n, collective_id):
    rows, cols = whole.shape[0] // n, whole.shape[1]
    return pl.pallas_call(
        functools.partial(_sum_kernel, n),
        out_shape=(
            jax.ShapeDtypeStruct(whole.shape, whole.dtype),
            jax.ShapeDtypeStruct(extra.shape, extra.dtype),
        ),
        in_specs=[pl.BlockSpec(memory_space=pltpu.VMEM)] * 2,
        out_specs=(pl.BlockSpec(memory_space=pltpu.VMEM),) * 2,
        scratch_shapes=[
            pltpu.VMEM((n, rows, cols), whole.dtype),
            pltpu.VMEM((rows, cols), whole.dtype),
            pltpu.VMEM((n,) + extra.shape, extra.dtype),
        ]
        + [pltpu.SemaphoreType.DMA((n,))] * 6,
        compiler_params=pltpu.CompilerParams(
            collective_id=collective_id, has_side_effects=True, vmem_limit_bytes=VMEM_LIMIT
        ),
    )(whole, extra)


EPS = 1e-05
THETA = 1000000.0
NEGATIVE = -1e30


def rms_forward(values, norm_gain):
    inverse = lax.rsqrt(jnp.mean(values * values, axis=-1, keepdims=True) + EPS)
    return (values * inverse * norm_gain, inverse)


def rms_backward(values, inverse, norm_gain, upstream):
    scaled = upstream * norm_gain
    inner_mean = jnp.mean(scaled * values, axis=-1, keepdims=True)
    through = inverse * (scaled - values * inverse * inverse * inner_mean)
    return (through, upstream * values * inverse)


def rope_tables(positions, head_dim):
    halfway = head_dim // 2
    frequency = THETA ** (-(jnp.arange(halfway, dtype=jnp.float32) * 2.0 / head_dim))
    angles = positions.astype(jnp.float32)[:, None] * frequency[None, :]
    return (jnp.cos(angles)[:, None, :], jnp.sin(angles)[:, None, :])


def rope_apply(values, cosine, sine_table):
    halfway = values.shape[-1] // 2
    first_half = values[..., :halfway]
    second_half = values[..., halfway:]
    return jnp.concatenate(
        [
            first_half * cosine - second_half * sine_table,
            second_half * cosine + first_half * sine_table,
        ],
        axis=-1,
    )


def rope_back(upstream, cosine, sine_table):
    halfway = upstream.shape[-1] // 2
    first_half = upstream[..., :halfway]
    second_half = upstream[..., halfway:]
    return jnp.concatenate(
        [
            first_half * cosine + second_half * sine_table,
            second_half * cosine - first_half * sine_table,
        ],
        axis=-1,
    )


def row_places(block_map, holder, rows_total, place_count):
    piece_len = rows_total // 4
    within = jnp.arange(rows_total, dtype=jnp.int32)
    picked = jnp.sum(jnp.where(jnp.arange(place_count, dtype=jnp.int32) == holder, block_map, 0))
    later = within // piece_len % 2
    piece_index = jnp.where(later == 1, 2 * place_count - 1 - picked, picked)
    return piece_index * piece_len + within % piece_len


def span_places(block_map, first_anchor, shard_span, seq_rows, place_count):
    piece_len = seq_rows // 2
    anchors = first_anchor + jnp.arange(shard_span, dtype=jnp.int32)
    picked = jnp.sum(
        jnp.where(
            jnp.arange(place_count, dtype=jnp.int32)[None, :] == anchors[:, None],
            block_map[None, :],
            0,
        ),
        axis=1,
    )
    within = jnp.arange(seq_rows, dtype=jnp.int32)
    later = within // piece_len % 2
    piece_index = jnp.where(
        later[None, :] == 1, 2 * place_count - 1 - picked[:, None], picked[:, None]
    )
    return (piece_index * piece_len + (within % piece_len)[None, :]).reshape(shard_span * seq_rows)


def gather_rows(rows_low):
    return lax.all_gather(rows_low, "tp", axis=0, tiled=True)


def reduce_rows(partial_rows):
    return lax.psum_scatter(
        partial_rows.astype(jnp.bfloat16), "tp", scatter_dimension=0, tiled=True
    ).astype(jnp.float32)


def per_device(
    block_input,
    block_map,
    attn_gain,
    query_weight,
    key_weight,
    value_weight,
    query_gain,
    key_gain,
    output_weight,
    ffn_gain,
    gate_weight,
    up_weight,
    down_weight,
    cotangent,
):
    place_count = lax.axis_size("ctx")
    place_index = lax.axis_index("ctx")
    head_dim = query_gain.shape[0]
    query_heads = query_weight.shape[1] // head_dim
    kv_heads = key_weight.shape[1] // head_dim
    group_size = query_heads // kv_heads
    score_scale = 1.0 / math.sqrt(head_dim)
    shard_span = 4
    residual_in = block_input.astype(jnp.float32)
    normed_one, inverse_one = rms_forward(residual_in, attn_gain)
    rows_one = gather_rows(normed_one.astype(jnp.bfloat16))
    rows_total = rows_one.shape[0]
    seq_rows = rows_total // 2
    kv_width = kv_heads * head_dim
    own_places = row_places(block_map, place_index, rows_total, place_count)
    query_raw = jnp.dot(rows_one, query_weight, preferred_element_type=jnp.float32).reshape(
        rows_total, query_heads, head_dim
    )
    key_raw = jnp.dot(rows_one, key_weight, preferred_element_type=jnp.float32).reshape(
        rows_total, kv_heads, head_dim
    )
    values_own = jnp.dot(rows_one, value_weight, preferred_element_type=jnp.float32).astype(
        jnp.bfloat16
    )
    query_normed, query_inverse = rms_forward(query_raw, query_gain)
    key_normed, key_inverse = rms_forward(key_raw, key_gain)
    cosine, sine_table = rope_tables(own_places, head_dim)
    query_rot = rope_apply(query_normed, cosine, sine_table).astype(jnp.bfloat16)
    keys_own = (
        rope_apply(key_normed, cosine, sine_table)
        .astype(jnp.bfloat16)
        .reshape(rows_total, kv_width)
    )
    query_blocks = query_rot.reshape(2, seq_rows, kv_heads, group_size, head_dim)
    query_places = own_places[:seq_rows]

    whole_kv = ctx_gather(jnp.concatenate([keys_own, values_own], axis=1), place_count, 0)
    seq_kv = jnp.transpose(
        whole_kv.reshape(place_count, 2, seq_rows, 2 * kv_width), (1, 0, 2, 3)
    ).reshape(2, place_count * seq_rows, 2 * kv_width)
    key_heads = seq_kv[..., :kv_width].reshape(2, place_count * seq_rows, kv_heads, head_dim)
    value_heads = seq_kv[..., kv_width:].reshape(2, place_count * seq_rows, kv_heads, head_dim)
    key_places = span_places(block_map, 0, place_count, seq_rows, place_count)
    allowed = key_places[None, :] <= query_places[:, None]
    scores = (
        jnp.einsum(
            "sqhgd,skhd->shgqk", query_blocks, key_heads, preferred_element_type=jnp.float32
        )
        * score_scale
    )
    top = jnp.max(jnp.where(allowed, scores, NEGATIVE), axis=-1)
    weights = jnp.where(allowed, jnp.exp(scores - top[..., None]), 0.0)
    weight_total = jnp.sum(weights, axis=-1)
    weighted = jnp.einsum(
        "shgqk,skhd->shgqd",
        weights.astype(jnp.bfloat16),
        value_heads,
        preferred_element_type=jnp.float32,
    )
    log_total = top + jnp.log(weight_total)
    attn_rows = jnp.transpose(weighted / weight_total[..., None], (0, 3, 1, 2, 4))
    attn_low = attn_rows.reshape(rows_total, query_heads * head_dim).astype(jnp.bfloat16)
    residual_mid = residual_in + reduce_rows(
        jnp.dot(attn_low, output_weight, preferred_element_type=jnp.float32)
    )
    normed_two, inverse_two = rms_forward(residual_mid, ffn_gain)
    rows_two = gather_rows(normed_two.astype(jnp.bfloat16))
    gate_pre = jnp.dot(rows_two, gate_weight, preferred_element_type=jnp.float32)
    up_pre = jnp.dot(rows_two, up_weight, preferred_element_type=jnp.float32)
    gate_sig = jax.nn.sigmoid(gate_pre)
    activated = (gate_pre * gate_sig * up_pre).astype(jnp.bfloat16)
    block_output = residual_mid + reduce_rows(
        jnp.dot(activated, down_weight, preferred_element_type=jnp.float32)
    )
    grad_rows = gather_rows(cotangent)
    grad_down_t = jnp.dot(grad_rows.T, activated, preferred_element_type=jnp.float32)
    grad_act = jnp.dot(grad_rows, down_weight.T, preferred_element_type=jnp.float32)
    grad_gate_pre = (grad_act * up_pre * gate_sig * (1.0 + gate_pre * (1.0 - gate_sig))).astype(
        jnp.bfloat16
    )
    grad_up_pre = (grad_act * gate_pre * gate_sig).astype(jnp.bfloat16)
    grad_gate = jnp.dot(rows_two.T, grad_gate_pre, preferred_element_type=jnp.float32)
    grad_up = jnp.dot(rows_two.T, grad_up_pre, preferred_element_type=jnp.float32)
    grad_normed_two = reduce_rows(
        jnp.dot(grad_gate_pre, gate_weight.T, preferred_element_type=jnp.float32)
        + jnp.dot(grad_up_pre, up_weight.T, preferred_element_type=jnp.float32)
    )
    through_two, ffn_terms = rms_backward(residual_mid, inverse_two, ffn_gain, grad_normed_two)
    grad_mid = cotangent.astype(jnp.float32) + through_two
    grad_mid_rows = gather_rows(grad_mid.astype(jnp.bfloat16))
    grad_output_t = jnp.dot(grad_mid_rows.T, attn_low, preferred_element_type=jnp.float32)
    grad_attn = jnp.dot(grad_mid_rows, output_weight.T, preferred_element_type=jnp.float32).astype(
        jnp.bfloat16
    )
    grad_attn_blocks = grad_attn.reshape(2, seq_rows, kv_heads, group_size, head_dim)
    delta_rows = jnp.sum(grad_attn_blocks.astype(jnp.float32) * attn_rows, axis=-1)
    delta_rows = jnp.transpose(delta_rows, (0, 2, 3, 1))

    probs = jnp.where(allowed, jnp.exp(scores - log_total[..., None]), 0.0)
    grad_value_seq = jnp.einsum(
        "shgqk,sqhgd->skhd",
        probs.astype(jnp.bfloat16),
        grad_attn_blocks,
        preferred_element_type=jnp.float32,
    )
    grad_probs = jnp.einsum(
        "sqhgd,skhd->shgqk", grad_attn_blocks, value_heads, preferred_element_type=jnp.float32
    )
    grad_scores = (score_scale * probs * (grad_probs - delta_rows[..., None])).astype(jnp.bfloat16)
    query_acc = jnp.einsum(
        "shgqk,skhd->sqhgd", grad_scores, key_heads, preferred_element_type=jnp.float32
    )
    grad_key_seq = jnp.einsum(
        "shgqk,sqhgd->skhd", grad_scores, query_blocks, preferred_element_type=jnp.float32
    )
    grad_kv_seq = jnp.concatenate(
        [
            grad_key_seq.reshape(2, place_count, seq_rows, kv_width),
            grad_value_seq.reshape(2, place_count, seq_rows, kv_width),
        ],
        axis=-1,
    )
    grad_kv_all = jnp.transpose(grad_kv_seq, (1, 0, 2, 3)).reshape(
        place_count * rows_total, 2 * kv_width
    )
    grad_kv_flat = ctx_scatter(
        grad_kv_all.astype(jnp.bfloat16),
        place_count,
        1,
    )
    grad_keys_flat, grad_values_flat = grad_kv_flat[:, :kv_width], grad_kv_flat[:, kv_width:]
    grad_query_rot = query_acc.reshape(rows_total, query_heads, head_dim)
    grad_key_rot = grad_keys_flat.reshape(rows_total, kv_heads, head_dim)
    grad_query_raw, query_terms = rms_backward(
        query_raw, query_inverse, query_gain, rope_back(grad_query_rot, cosine, sine_table)
    )
    grad_key_raw, key_terms = rms_backward(
        key_raw, key_inverse, key_gain, rope_back(grad_key_rot, cosine, sine_table)
    )
    grad_query_low = grad_query_raw.reshape(rows_total, query_heads * head_dim).astype(jnp.bfloat16)
    grad_key_low = grad_key_raw.reshape(rows_total, kv_width).astype(jnp.bfloat16)
    grad_value_low = grad_values_flat.astype(jnp.bfloat16)
    grad_query = jnp.dot(rows_one.T, grad_query_low, preferred_element_type=jnp.float32)
    grad_key = jnp.dot(rows_one.T, grad_key_low, preferred_element_type=jnp.float32)
    grad_value = jnp.dot(rows_one.T, grad_value_low, preferred_element_type=jnp.float32)
    grad_normed_one = reduce_rows(
        jnp.dot(grad_query_low, query_weight.T, preferred_element_type=jnp.float32)
        + jnp.dot(grad_key_low, key_weight.T, preferred_element_type=jnp.float32)
        + jnp.dot(grad_value_low, value_weight.T, preferred_element_type=jnp.float32)
    )
    through_one, attn_terms = rms_backward(residual_in, inverse_one, attn_gain, grad_normed_one)
    input_grad = grad_mid + through_one
    weight_parts = (grad_query, grad_key, grad_value, grad_output_t, grad_gate, grad_up, grad_down_t)
    widths = [part.shape[1] for part in weight_parts]
    gain_parts = (
        jnp.sum(attn_terms, axis=0),
        jnp.sum(query_terms, axis=(0, 1)),
        jnp.sum(key_terms, axis=(0, 1)),
        jnp.sum(ffn_terms, axis=0),
    )
    gain_sizes = [part.shape[0] for part in gain_parts]
    gain_flat = lax.psum(jnp.concatenate(gain_parts), "tp")
    gain_pad = -gain_flat.shape[0] % 1024
    summed, gains = ctx_sum(
        jnp.concatenate([part.astype(jnp.bfloat16) for part in weight_parts], axis=1),
        jnp.pad(gain_flat, (0, gain_pad)).reshape(8, -1),
        place_count,
        2,
    )
    summed = summed.astype(jnp.float32)
    gains = gains.reshape(-1)
    offsets = [sum(widths[:k]) for k in range(len(widths) + 1)]
    shared_query, shared_key, shared_value, output_t, shared_gate, shared_up, down_t = (
        summed[:, offsets[k] : offsets[k + 1]] for k in range(len(widths))
    )
    shared_output = output_t.T
    shared_down = down_t.T
    gain_attn = gains[: gain_sizes[0]]
    gain_query = gains[gain_sizes[0] : gain_sizes[0] + gain_sizes[1]]
    gain_key = gains[gain_sizes[0] + gain_sizes[1] : gain_sizes[0] + gain_sizes[1] + gain_sizes[2]]
    gain_ffn = gains[gain_sizes[0] + gain_sizes[1] + gain_sizes[2] : sum(gain_sizes)]
    return (
        block_output,
        input_grad,
        gain_attn,
        shared_query,
        shared_key,
        shared_value,
        gain_query,
        gain_key,
        shared_output,
        gain_ffn,
        shared_gate,
        shared_up,
        shared_down,
    )


def solution(mesh):
    return jax.shard_map(
        per_device,
        mesh=mesh,
        in_specs=(
            P(("ctx", "tp"), None),
            P(),
            P(),
            P(None, "tp"),
            P(None, "tp"),
            P(None, "tp"),
            P(),
            P(),
            P("tp", None),
            P(),
            P(None, "tp"),
            P(None, "tp"),
            P("tp", None),
            P(("ctx", "tp"), None),
        ),
        out_specs=(
            P(("ctx", "tp"), None),
            P(("ctx", "tp"), None),
            P(),
            P(None, "tp"),
            P(None, "tp"),
            P(None, "tp"),
            P(),
            P(),
            P("tp", None),
            P(),
            P(None, "tp"),
            P(None, "tp"),
            P("tp", None),
        ),
        check_vma=False,
    )
```

```python
import functools
import math

import jax
import jax.numpy as jnp
from jax import lax
from jax.experimental import pallas as pl
from jax.experimental.pallas import tpu as pltpu
from jax.sharding import PartitionSpec as P

MESH = pl.DeviceIdType.MESH
VMEM_LIMIT = 60 * 1024 * 1024


def _shifts(n):
    order = []
    for k in range(1, n // 2 + 1):
        order.append(k)
        if n - k != k:
            order.append(n - k)
    return order


def _enter(n, me, peer_axis):
    barrier = pltpu.get_barrier_semaphore()
    for k in _shifts(n):
        pl.semaphore_signal(
            barrier, 1, device_id=(lax.rem(me + k, n), peer_axis), device_id_type=MESH
        )
    pl.semaphore_wait(barrier, n - 1)


def _gather_kernel(n, part_ref, out_ref, send_sem, recv_sem):
    me = lax.axis_index("ctx")
    other = lax.axis_index("tp")
    rows = part_ref.shape[0]
    _enter(n, me, other)
    copies = []
    for k in _shifts(n):
        copy = pltpu.make_async_remote_copy(
            src_ref=part_ref,
            dst_ref=out_ref.at[pl.ds(pl.multiple_of(me * rows, rows), rows)],
            send_sem=send_sem.at[k],
            recv_sem=recv_sem.at[k],
            device_id=(lax.rem(me + k, n), other),
            device_id_type=MESH,
        )
        copy.start()
        copies.append(copy)
    out_ref[pl.ds(pl.multiple_of(me * rows, rows), rows), :] = part_ref[...]
    for k in _shifts(n):
        source = lax.rem(me + n - k, n)
        pltpu.make_async_remote_copy(
            src_ref=part_ref,
            dst_ref=out_ref.at[pl.ds(pl.multiple_of(source * rows, rows), rows)],
            send_sem=send_sem.at[k],
            recv_sem=recv_sem.at[k],
            device_id=(source, other),
            device_id_type=MESH,
        ).wait_recv()
    for copy in copies:
        copy.wait_send()


def ctx_gather(part, n, collective_id):
    rows, cols = part.shape
    return pl.pallas_call(
        functools.partial(_gather_kernel, n),
        out_shape=jax.ShapeDtypeStruct((n * rows, cols), part.dtype),
        in_specs=[pl.BlockSpec(memory_space=pltpu.VMEM)],
        out_specs=pl.BlockSpec(memory_space=pltpu.VMEM),
        scratch_shapes=[pltpu.SemaphoreType.DMA((n,)), pltpu.SemaphoreType.DMA((n,))],
        compiler_params=pltpu.CompilerParams(
            collective_id=collective_id, has_side_effects=True, vmem_limit_bytes=VMEM_LIMIT
        ),
    )(part)


def _scatter_sum(n, me, other, whole_ref, held, send_sem, recv_sem, rows):
    copies = []
    for k in _shifts(n):
        target = lax.rem(me + k, n)
        copy = pltpu.make_async_remote_copy(
            src_ref=whole_ref.at[pl.ds(pl.multiple_of(target * rows, rows), rows)],
            dst_ref=held.at[k],
            send_sem=send_sem.at[k],
            recv_sem=recv_sem.at[k],
            device_id=(target, other),
            device_id_type=MESH,
        )
        copy.start()
        copies.append(copy)
    total = whole_ref[pl.ds(pl.multiple_of(me * rows, rows), rows), :].astype(jnp.float32)
    for k in _shifts(n):
        source = lax.rem(me + n - k, n)
        pltpu.make_async_remote_copy(
            src_ref=whole_ref.at[pl.ds(0, rows)],
            dst_ref=held.at[k],
            send_sem=send_sem.at[k],
            recv_sem=recv_sem.at[k],
            device_id=(source, other),
            device_id_type=MESH,
        ).wait_recv()
        total = total + held[k].astype(jnp.float32)
    for copy in copies:
        copy.wait_send()
    return total


def _scatter_kernel(n, whole_ref, out_ref, held, send_sem, recv_sem):
    me = lax.axis_index("ctx")
    other = lax.axis_index("tp")
    rows = out_ref.shape[0]
    _enter(n, me, other)
    out_ref[...] = _scatter_sum(n, me, other, whole_ref, held, send_sem, recv_sem, rows)


def ctx_scatter(whole, n, collective_id):
    rows, cols = whole.shape[0] // n, whole.shape[1]
    return pl.pallas_call(
        functools.partial(_scatter_kernel, n),
        out_shape=jax.ShapeDtypeStruct((rows, cols), jnp.float32),
        in_specs=[pl.BlockSpec(memory_space=pltpu.VMEM)],
        out_specs=pl.BlockSpec(memory_space=pltpu.VMEM),
        scratch_shapes=[
            pltpu.VMEM((n, rows, cols), whole.dtype),
            pltpu.SemaphoreType.DMA((n,)),
            pltpu.SemaphoreType.DMA((n,)),
        ],
        compiler_params=pltpu.CompilerParams(
            collective_id=collective_id, has_side_effects=True, vmem_limit_bytes=VMEM_LIMIT
        ),
    )(whole)


def _sum_kernel(n, spans, whole_ref, extra_ref, out_ref, extra_out, *scratch):
    pieces = len(spans)
    helds, mines, extra_held = scratch[:pieces], scratch[pieces : 2 * pieces], scratch[2 * pieces]
    sems = scratch[2 * pieces + 1 :]
    send_extra, recv_extra = sems[4 * pieces], sems[4 * pieces + 1]
    me = lax.axis_index("ctx")
    other = lax.axis_index("tp")
    rows = whole_ref.shape[0] // n
    own_rows = pl.ds(pl.multiple_of(me * rows, rows), rows)
    _enter(n, me, other)
    sent = []
    for k in _shifts(n):
        copy = pltpu.make_async_remote_copy(
            src_ref=extra_ref,
            dst_ref=extra_held.at[k],
            send_sem=send_extra.at[k],
            recv_sem=recv_extra.at[k],
            device_id=(lax.rem(me + k, n), other),
            device_id_type=MESH,
        )
        copy.start()
        sent.append(copy)
    for piece, (first, width) in enumerate(spans):
        for k in _shifts(n):
            target = lax.rem(me + k, n)
            copy = pltpu.make_async_remote_copy(
                src_ref=whole_ref.at[
                    pl.ds(pl.multiple_of(target * rows, rows), rows), pl.ds(first, width)
                ],
                dst_ref=helds[piece].at[k],
                send_sem=sems[4 * piece].at[k],
                recv_sem=sems[4 * piece + 1].at[k],
                device_id=(target, other),
                device_id_type=MESH,
            )
            copy.start()
            sent.append(copy)
    for piece, (first, width) in enumerate(spans):
        total = whole_ref[own_rows, pl.ds(first, width)].astype(jnp.float32)
        for k in _shifts(n):
            pltpu.make_async_remote_copy(
                src_ref=whole_ref.at[pl.ds(0, rows), pl.ds(first, width)],
                dst_ref=helds[piece].at[k],
                send_sem=sems[4 * piece].at[k],
                recv_sem=sems[4 * piece + 1].at[k],
                device_id=(lax.rem(me + n - k, n), other),
                device_id_type=MESH,
            ).wait_recv()
            total = total + helds[piece][k].astype(jnp.float32)
        mines[piece][...] = total.astype(mines[piece].dtype)
        for k in _shifts(n):
            copy = pltpu.make_async_remote_copy(
                src_ref=mines[piece],
                dst_ref=out_ref.at[own_rows, pl.ds(first, width)],
                send_sem=sems[4 * piece + 2].at[k],
                recv_sem=sems[4 * piece + 3].at[k],
                device_id=(lax.rem(me + k, n), other),
                device_id_type=MESH,
            )
            copy.start()
            sent.append(copy)
        out_ref[own_rows, pl.ds(first, width)] = mines[piece][...]
    extra_total = extra_ref[...]
    for k in _shifts(n):
        pltpu.make_async_remote_copy(
            src_ref=extra_ref,
            dst_ref=extra_held.at[k],
            send_sem=send_extra.at[k],
            recv_sem=recv_extra.at[k],
            device_id=(lax.rem(me + n - k, n), other),
            device_id_type=MESH,
        ).wait_recv()
        extra_total = extra_total + extra_held[k]
    extra_out[...] = extra_total
    for piece, (first, width) in enumerate(spans):
        for k in _shifts(n):
            source = lax.rem(me + n - k, n)
            pltpu.make_async_remote_copy(
                src_ref=mines[piece],
                dst_ref=out_ref.at[
                    pl.ds(pl.multiple_of(source * rows, rows), rows), pl.ds(first, width)
                ],
                send_sem=sems[4 * piece + 2].at[k],
                recv_sem=sems[4 * piece + 3].at[k],
                device_id=(source, other),
                device_id_type=MESH,
            ).wait_recv()
    for copy in sent:
        copy.wait_send()


def ctx_sum(whole, extra, n, collective_id, pieces=2):
    rows, cols = whole.shape[0] // n, whole.shape[1]
    lanes = cols // 128
    edges = [128 * (lanes * p // pieces) for p in range(pieces + 1)]
    spans = tuple((edges[p], edges[p + 1] - edges[p]) for p in range(pieces))
    return pl.pallas_call(
        functools.partial(_sum_kernel, n, spans),
        out_shape=(
            jax.ShapeDtypeStruct(whole.shape, whole.dtype),
            jax.ShapeDtypeStruct(extra.shape, extra.dtype),
        ),
        in_specs=[pl.BlockSpec(memory_space=pltpu.VMEM)] * 2,
        out_specs=(pl.BlockSpec(memory_space=pltpu.VMEM),) * 2,
        scratch_shapes=[pltpu.VMEM((n, rows, width), whole.dtype) for _, width in spans]
        + [pltpu.VMEM((rows, width), whole.dtype) for _, width in spans]
        + [pltpu.VMEM((n,) + extra.shape, extra.dtype)]
        + [pltpu.SemaphoreType.DMA((n,))] * (4 * pieces + 2),
        compiler_params=pltpu.CompilerParams(
            collective_id=collective_id, has_side_effects=True, vmem_limit_bytes=VMEM_LIMIT
        ),
    )(whole, extra)


EPS = 1e-05
THETA = 1000000.0
NEGATIVE = -1e30


def rms_forward(values, norm_gain):
    inverse = lax.rsqrt(jnp.mean(values * values, axis=-1, keepdims=True) + EPS)
    return (values * inverse * norm_gain, inverse)


def rms_backward(values, inverse, norm_gain, upstream):
    scaled = upstream * norm_gain
    inner_mean = jnp.mean(scaled * values, axis=-1, keepdims=True)
    through = inverse * (scaled - values * inverse * inverse * inner_mean)
    return (through, upstream * values * inverse)


def rope_tables(positions, head_dim):
    halfway = head_dim // 2
    frequency = THETA ** (-(jnp.arange(halfway, dtype=jnp.float32) * 2.0 / head_dim))
    angles = positions.astype(jnp.float32)[:, None] * frequency[None, :]
    return (jnp.cos(angles)[:, None, :], jnp.sin(angles)[:, None, :])


def rope_apply(values, cosine, sine_table):
    halfway = values.shape[-1] // 2
    first_half = values[..., :halfway]
    second_half = values[..., halfway:]
    return jnp.concatenate(
        [
            first_half * cosine - second_half * sine_table,
            second_half * cosine + first_half * sine_table,
        ],
        axis=-1,
    )


def rope_back(upstream, cosine, sine_table):
    halfway = upstream.shape[-1] // 2
    first_half = upstream[..., :halfway]
    second_half = upstream[..., halfway:]
    return jnp.concatenate(
        [
            first_half * cosine + second_half * sine_table,
            second_half * cosine - first_half * sine_table,
        ],
        axis=-1,
    )


def row_places(block_map, holder, rows_total, place_count):
    piece_len = rows_total // 4
    within = jnp.arange(rows_total, dtype=jnp.int32)
    picked = jnp.sum(jnp.where(jnp.arange(place_count, dtype=jnp.int32) == holder, block_map, 0))
    later = within // piece_len % 2
    piece_index = jnp.where(later == 1, 2 * place_count - 1 - picked, picked)
    return piece_index * piece_len + within % piece_len


def span_places(block_map, first_anchor, shard_span, seq_rows, place_count):
    piece_len = seq_rows // 2
    anchors = first_anchor + jnp.arange(shard_span, dtype=jnp.int32)
    picked = jnp.sum(
        jnp.where(
            jnp.arange(place_count, dtype=jnp.int32)[None, :] == anchors[:, None],
            block_map[None, :],
            0,
        ),
        axis=1,
    )
    within = jnp.arange(seq_rows, dtype=jnp.int32)
    later = within // piece_len % 2
    piece_index = jnp.where(
        later[None, :] == 1, 2 * place_count - 1 - picked[:, None], picked[:, None]
    )
    return (piece_index * piece_len + (within % piece_len)[None, :]).reshape(shard_span * seq_rows)


def gather_rows(rows_low):
    return lax.all_gather(rows_low, "tp", axis=0, tiled=True)


def reduce_rows(partial_rows):
    return lax.psum_scatter(
        partial_rows.astype(jnp.bfloat16), "tp", scatter_dimension=0, tiled=True
    ).astype(jnp.float32)


def per_device(
    block_input,
    block_map,
    attn_gain,
    query_weight,
    key_weight,
    value_weight,
    query_gain,
    key_gain,
    output_weight,
    ffn_gain,
    gate_weight,
    up_weight,
    down_weight,
    cotangent,
):
    place_count = lax.axis_size("ctx")
    place_index = lax.axis_index("ctx")
    head_dim = query_gain.shape[0]
    query_heads = query_weight.shape[1] // head_dim
    kv_heads = key_weight.shape[1] // head_dim
    group_size = query_heads // kv_heads
    score_scale = 1.0 / math.sqrt(head_dim)
    shard_span = 4
    residual_in = block_input.astype(jnp.float32)
    normed_one, inverse_one = rms_forward(residual_in, attn_gain)
    rows_one = gather_rows(normed_one.astype(jnp.bfloat16))
    rows_total = rows_one.shape[0]
    seq_rows = rows_total // 2
    kv_width = kv_heads * head_dim
    own_places = row_places(block_map, place_index, rows_total, place_count)
    query_raw = jnp.dot(rows_one, query_weight, preferred_element_type=jnp.float32).reshape(
        rows_total, query_heads, head_dim
    )
    key_raw = jnp.dot(rows_one, key_weight, preferred_element_type=jnp.float32).reshape(
        rows_total, kv_heads, head_dim
    )
    values_own = jnp.dot(rows_one, value_weight, preferred_element_type=jnp.float32).astype(
        jnp.bfloat16
    )
    query_normed, query_inverse = rms_forward(query_raw, query_gain)
    key_normed, key_inverse = rms_forward(key_raw, key_gain)
    cosine, sine_table = rope_tables(own_places, head_dim)
    query_rot = rope_apply(query_normed, cosine, sine_table).astype(jnp.bfloat16)
    keys_own = (
        rope_apply(key_normed, cosine, sine_table)
        .astype(jnp.bfloat16)
        .reshape(rows_total, kv_width)
    )
    query_blocks = query_rot.reshape(2, seq_rows, kv_heads, group_size, head_dim)
    query_places = own_places[:seq_rows]

    whole_kv = ctx_gather(jnp.concatenate([keys_own, values_own], axis=1), place_count, 0)
    seq_kv = jnp.transpose(
        whole_kv.reshape(place_count, 2, seq_rows, 2 * kv_width), (1, 0, 2, 3)
    ).reshape(2, place_count * seq_rows, 2 * kv_width)
    key_heads = seq_kv[..., :kv_width].reshape(2, place_count * seq_rows, kv_heads, head_dim)
    value_heads = seq_kv[..., kv_width:].reshape(2, place_count * seq_rows, kv_heads, head_dim)
    key_places = span_places(block_map, 0, place_count, seq_rows, place_count)
    allowed = key_places[None, :] <= query_places[:, None]
    scores = (
        jnp.einsum(
            "sqhgd,skhd->shgqk", query_blocks, key_heads, preferred_element_type=jnp.float32
        )
        * score_scale
    )
    top = jnp.max(jnp.where(allowed, scores, NEGATIVE), axis=-1)
    weights = jnp.where(allowed, jnp.exp(scores - top[..., None]), 0.0)
    weight_total = jnp.sum(weights, axis=-1)
    weighted = jnp.einsum(
        "shgqk,skhd->shgqd",
        weights.astype(jnp.bfloat16),
        value_heads,
        preferred_element_type=jnp.float32,
    )
    log_total = top + jnp.log(weight_total)
    attn_rows = jnp.transpose(weighted / weight_total[..., None], (0, 3, 1, 2, 4))
    attn_low = attn_rows.reshape(rows_total, query_heads * head_dim).astype(jnp.bfloat16)
    residual_mid = residual_in + reduce_rows(
        jnp.dot(attn_low, output_weight, preferred_element_type=jnp.float32)
    )
    normed_two, inverse_two = rms_forward(residual_mid, ffn_gain)
    rows_two = gather_rows(normed_two.astype(jnp.bfloat16))
    gate_pre = jnp.dot(rows_two, gate_weight, preferred_element_type=jnp.float32)
    up_pre = jnp.dot(rows_two, up_weight, preferred_element_type=jnp.float32)
    gate_sig = jax.nn.sigmoid(gate_pre)
    activated = (gate_pre * gate_sig * up_pre).astype(jnp.bfloat16)
    block_output = residual_mid + reduce_rows(
        jnp.dot(activated, down_weight, preferred_element_type=jnp.float32)
    )
    grad_rows = gather_rows(cotangent)
    grad_down_t = jnp.dot(grad_rows.T, activated, preferred_element_type=jnp.float32)
    grad_act = jnp.dot(grad_rows, down_weight.T, preferred_element_type=jnp.float32)
    grad_gate_pre = (grad_act * up_pre * gate_sig * (1.0 + gate_pre * (1.0 - gate_sig))).astype(
        jnp.bfloat16
    )
    grad_up_pre = (grad_act * gate_pre * gate_sig).astype(jnp.bfloat16)
    grad_gate = jnp.dot(rows_two.T, grad_gate_pre, preferred_element_type=jnp.float32)
    grad_up = jnp.dot(rows_two.T, grad_up_pre, preferred_element_type=jnp.float32)
    grad_normed_two = reduce_rows(
        jnp.dot(grad_gate_pre, gate_weight.T, preferred_element_type=jnp.float32)
        + jnp.dot(grad_up_pre, up_weight.T, preferred_element_type=jnp.float32)
    )
    through_two, ffn_terms = rms_backward(residual_mid, inverse_two, ffn_gain, grad_normed_two)
    grad_mid = cotangent.astype(jnp.float32) + through_two
    grad_mid_rows = gather_rows(grad_mid.astype(jnp.bfloat16))
    grad_output_t = jnp.dot(grad_mid_rows.T, attn_low, preferred_element_type=jnp.float32)
    grad_attn = jnp.dot(grad_mid_rows, output_weight.T, preferred_element_type=jnp.float32).astype(
        jnp.bfloat16
    )
    grad_attn_blocks = grad_attn.reshape(2, seq_rows, kv_heads, group_size, head_dim)
    delta_rows = jnp.sum(grad_attn_blocks.astype(jnp.float32) * attn_rows, axis=-1)
    delta_rows = jnp.transpose(delta_rows, (0, 2, 3, 1))

    probs = jnp.where(allowed, jnp.exp(scores - log_total[..., None]), 0.0)
    grad_value_seq = jnp.einsum(
        "shgqk,sqhgd->skhd",
        probs.astype(jnp.bfloat16),
        grad_attn_blocks,
        preferred_element_type=jnp.float32,
    )
    grad_probs = jnp.einsum(
        "sqhgd,skhd->shgqk", grad_attn_blocks, value_heads, preferred_element_type=jnp.float32
    )
    grad_scores = (score_scale * probs * (grad_probs - delta_rows[..., None])).astype(jnp.bfloat16)
    query_acc = jnp.einsum(
        "shgqk,skhd->sqhgd", grad_scores, key_heads, preferred_element_type=jnp.float32
    )
    grad_key_seq = jnp.einsum(
        "shgqk,sqhgd->skhd", grad_scores, query_blocks, preferred_element_type=jnp.float32
    )
    grad_kv_seq = jnp.concatenate(
        [
            grad_key_seq.reshape(2, place_count, seq_rows, kv_width),
            grad_value_seq.reshape(2, place_count, seq_rows, kv_width),
        ],
        axis=-1,
    )
    grad_kv_all = jnp.transpose(grad_kv_seq, (1, 0, 2, 3)).reshape(
        place_count * rows_total, 2 * kv_width
    )
    grad_kv_flat = ctx_scatter(
        grad_kv_all.astype(jnp.bfloat16),
        place_count,
        1,
    )
    grad_keys_flat, grad_values_flat = grad_kv_flat[:, :kv_width], grad_kv_flat[:, kv_width:]
    grad_query_rot = query_acc.reshape(rows_total, query_heads, head_dim)
    grad_key_rot = grad_keys_flat.reshape(rows_total, kv_heads, head_dim)
    grad_query_raw, query_terms = rms_backward(
        query_raw, query_inverse, query_gain, rope_back(grad_query_rot, cosine, sine_table)
    )
    grad_key_raw, key_terms = rms_backward(
        key_raw, key_inverse, key_gain, rope_back(grad_key_rot, cosine, sine_table)
    )
    grad_query_low = grad_query_raw.reshape(rows_total, query_heads * head_dim).astype(jnp.bfloat16)
    grad_key_low = grad_key_raw.reshape(rows_total, kv_width).astype(jnp.bfloat16)
    grad_value_low = grad_values_flat.astype(jnp.bfloat16)
    grad_query = jnp.dot(rows_one.T, grad_query_low, preferred_element_type=jnp.float32)
    grad_key = jnp.dot(rows_one.T, grad_key_low, preferred_element_type=jnp.float32)
    grad_value = jnp.dot(rows_one.T, grad_value_low, preferred_element_type=jnp.float32)
    grad_normed_one = reduce_rows(
        jnp.dot(grad_query_low, query_weight.T, preferred_element_type=jnp.float32)
        + jnp.dot(grad_key_low, key_weight.T, preferred_element_type=jnp.float32)
        + jnp.dot(grad_value_low, value_weight.T, preferred_element_type=jnp.float32)
    )
    through_one, attn_terms = rms_backward(residual_in, inverse_one, attn_gain, grad_normed_one)
    input_grad = grad_mid + through_one
    weight_parts = (grad_query, grad_key, grad_value, grad_output_t, grad_gate, grad_up, grad_down_t)
    widths = [part.shape[1] for part in weight_parts]
    gain_parts = (
        jnp.sum(attn_terms, axis=0),
        jnp.sum(query_terms, axis=(0, 1)),
        jnp.sum(key_terms, axis=(0, 1)),
        jnp.sum(ffn_terms, axis=0),
    )
    gain_sizes = [part.shape[0] for part in gain_parts]
    gain_flat = lax.psum(jnp.concatenate(gain_parts), "tp")
    gain_pad = -gain_flat.shape[0] % 1024
    summed, gains = ctx_sum(
        jnp.concatenate([part.astype(jnp.bfloat16) for part in weight_parts], axis=1),
        jnp.pad(gain_flat, (0, gain_pad)).reshape(8, -1),
        place_count,
        2,
    )
    summed = summed.astype(jnp.float32)
    gains = gains.reshape(-1)
    offsets = [sum(widths[:k]) for k in range(len(widths) + 1)]
    shared_query, shared_key, shared_value, output_t, shared_gate, shared_up, down_t = (
        summed[:, offsets[k] : offsets[k + 1]] for k in range(len(widths))
    )
    shared_output = output_t.T
    shared_down = down_t.T
    gain_attn = gains[: gain_sizes[0]]
    gain_query = gains[gain_sizes[0] : gain_sizes[0] + gain_sizes[1]]
    gain_key = gains[gain_sizes[0] + gain_sizes[1] : gain_sizes[0] + gain_sizes[1] + gain_sizes[2]]
    gain_ffn = gains[gain_sizes[0] + gain_sizes[1] + gain_sizes[2] : sum(gain_sizes)]
    return (
        block_output,
        input_grad,
        gain_attn,
        shared_query,
        shared_key,
        shared_value,
        gain_query,
        gain_key,
        shared_output,
        gain_ffn,
        shared_gate,
        shared_up,
        shared_down,
    )


def solution(mesh):
    return jax.shard_map(
        per_device,
        mesh=mesh,
        in_specs=(
            P(("ctx", "tp"), None),
            P(),
            P(),
            P(None, "tp"),
            P(None, "tp"),
            P(None, "tp"),
            P(),
            P(),
            P("tp", None),
            P(),
            P(None, "tp"),
            P(None, "tp"),
            P("tp", None),
            P(("ctx", "tp"), None),
        ),
        out_specs=(
            P(("ctx", "tp"), None),
            P(("ctx", "tp"), None),
            P(),
            P(None, "tp"),
            P(None, "tp"),
            P(None, "tp"),
            P(),
            P(),
            P("tp", None),
            P(),
            P(None, "tp"),
            P(None, "tp"),
            P("tp", None),
        ),
        check_vma=False,
    )
```

```python
import functools
import math

import jax
import jax.numpy as jnp
from jax import lax
from jax.experimental import pallas as pl
from jax.experimental.pallas import tpu as pltpu
from jax.sharding import PartitionSpec as P

MESH = pl.DeviceIdType.MESH
VMEM_LIMIT = 60 * 1024 * 1024


def _shifts(n):
    order = []
    for k in range(1, n // 2 + 1):
        order.append(k)
        if n - k != k:
            order.append(n - k)
    return order


def _enter(n, me, peer_axis):
    barrier = pltpu.get_barrier_semaphore()
    for k in _shifts(n):
        pl.semaphore_signal(
            barrier, 1, device_id=(lax.rem(me + k, n), peer_axis), device_id_type=MESH
        )
    pl.semaphore_wait(barrier, n - 1)


def _gather_kernel(n, part_ref, out_ref, send_sem, recv_sem):
    me = lax.axis_index("ctx")
    other = lax.axis_index("tp")
    rows = part_ref.shape[0]
    _enter(n, me, other)
    copies = []
    for k in _shifts(n):
        copy = pltpu.make_async_remote_copy(
            src_ref=part_ref,
            dst_ref=out_ref.at[pl.ds(pl.multiple_of(me * rows, rows), rows)],
            send_sem=send_sem.at[k],
            recv_sem=recv_sem.at[k],
            device_id=(lax.rem(me + k, n), other),
            device_id_type=MESH,
        )
        copy.start()
        copies.append(copy)
    out_ref[pl.ds(pl.multiple_of(me * rows, rows), rows), :] = part_ref[...]
    for k in _shifts(n):
        source = lax.rem(me + n - k, n)
        pltpu.make_async_remote_copy(
            src_ref=part_ref,
            dst_ref=out_ref.at[pl.ds(pl.multiple_of(source * rows, rows), rows)],
            send_sem=send_sem.at[k],
            recv_sem=recv_sem.at[k],
            device_id=(source, other),
            device_id_type=MESH,
        ).wait_recv()
    for copy in copies:
        copy.wait_send()


def ctx_gather(part, n, collective_id):
    rows, cols = part.shape
    return pl.pallas_call(
        functools.partial(_gather_kernel, n),
        out_shape=jax.ShapeDtypeStruct((n * rows, cols), part.dtype),
        in_specs=[pl.BlockSpec(memory_space=pltpu.VMEM)],
        out_specs=pl.BlockSpec(memory_space=pltpu.VMEM),
        scratch_shapes=[pltpu.SemaphoreType.DMA((n,)), pltpu.SemaphoreType.DMA((n,))],
        compiler_params=pltpu.CompilerParams(
            collective_id=collective_id, has_side_effects=True, vmem_limit_bytes=VMEM_LIMIT
        ),
    )(part)


def _scatter_sum(n, me, other, whole_ref, held, send_sem, recv_sem, rows):
    copies = []
    for k in _shifts(n):
        target = lax.rem(me + k, n)
        copy = pltpu.make_async_remote_copy(
            src_ref=whole_ref.at[pl.ds(pl.multiple_of(target * rows, rows), rows)],
            dst_ref=held.at[k],
            send_sem=send_sem.at[k],
            recv_sem=recv_sem.at[k],
            device_id=(target, other),
            device_id_type=MESH,
        )
        copy.start()
        copies.append(copy)
    total = whole_ref[pl.ds(pl.multiple_of(me * rows, rows), rows), :].astype(jnp.float32)
    for k in _shifts(n):
        source = lax.rem(me + n - k, n)
        pltpu.make_async_remote_copy(
            src_ref=whole_ref.at[pl.ds(0, rows)],
            dst_ref=held.at[k],
            send_sem=send_sem.at[k],
            recv_sem=recv_sem.at[k],
            device_id=(source, other),
            device_id_type=MESH,
        ).wait_recv()
        total = total + held[k].astype(jnp.float32)
    for copy in copies:
        copy.wait_send()
    return total


def _scatter_kernel(n, whole_ref, out_ref, held, send_sem, recv_sem):
    me = lax.axis_index("ctx")
    other = lax.axis_index("tp")
    rows = out_ref.shape[0]
    _enter(n, me, other)
    out_ref[...] = _scatter_sum(n, me, other, whole_ref, held, send_sem, recv_sem, rows)


def ctx_scatter(whole, n, collective_id):
    rows, cols = whole.shape[0] // n, whole.shape[1]
    return pl.pallas_call(
        functools.partial(_scatter_kernel, n),
        out_shape=jax.ShapeDtypeStruct((rows, cols), jnp.float32),
        in_specs=[pl.BlockSpec(memory_space=pltpu.VMEM)],
        out_specs=pl.BlockSpec(memory_space=pltpu.VMEM),
        scratch_shapes=[
            pltpu.VMEM((n, rows, cols), whole.dtype),
            pltpu.SemaphoreType.DMA((n,)),
            pltpu.SemaphoreType.DMA((n,)),
        ],
        compiler_params=pltpu.CompilerParams(
            collective_id=collective_id, has_side_effects=True, vmem_limit_bytes=VMEM_LIMIT
        ),
    )(whole)


def _sum_kernel(n, spans, whole_ref, extra_ref, out_ref, extra_out, *scratch):
    pieces = len(spans)
    helds, mines, extra_held = scratch[:pieces], scratch[pieces : 2 * pieces], scratch[2 * pieces]
    sems = scratch[2 * pieces + 1 :]
    send_extra, recv_extra = sems[4 * pieces], sems[4 * pieces + 1]
    me = lax.axis_index("ctx")
    other = lax.axis_index("tp")
    rows = whole_ref.shape[0] // n
    own_rows = pl.ds(pl.multiple_of(me * rows, rows), rows)
    _enter(n, me, other)
    sent = []
    for k in _shifts(n):
        copy = pltpu.make_async_remote_copy(
            src_ref=extra_ref,
            dst_ref=extra_held.at[k],
            send_sem=send_extra.at[k],
            recv_sem=recv_extra.at[k],
            device_id=(lax.rem(me + k, n), other),
            device_id_type=MESH,
        )
        copy.start()
        sent.append(copy)
    for piece, (first, width) in enumerate(spans):
        for k in _shifts(n):
            target = lax.rem(me + k, n)
            copy = pltpu.make_async_remote_copy(
                src_ref=whole_ref.at[
                    pl.ds(pl.multiple_of(target * rows, rows), rows), pl.ds(first, width)
                ],
                dst_ref=helds[piece].at[k],
                send_sem=sems[4 * piece].at[k],
                recv_sem=sems[4 * piece + 1].at[k],
                device_id=(target, other),
                device_id_type=MESH,
            )
            copy.start()
            sent.append(copy)
    for piece, (first, width) in enumerate(spans):
        total = whole_ref[own_rows, pl.ds(first, width)].astype(jnp.float32)
        for k in _shifts(n):
            pltpu.make_async_remote_copy(
                src_ref=whole_ref.at[pl.ds(0, rows), pl.ds(first, width)],
                dst_ref=helds[piece].at[k],
                send_sem=sems[4 * piece].at[k],
                recv_sem=sems[4 * piece + 1].at[k],
                device_id=(lax.rem(me + n - k, n), other),
                device_id_type=MESH,
            ).wait_recv()
            total = total + helds[piece][k].astype(jnp.float32)
        mines[piece][...] = total.astype(mines[piece].dtype)
        for k in _shifts(n):
            copy = pltpu.make_async_remote_copy(
                src_ref=mines[piece],
                dst_ref=out_ref.at[own_rows, pl.ds(first, width)],
                send_sem=sems[4 * piece + 2].at[k],
                recv_sem=sems[4 * piece + 3].at[k],
                device_id=(lax.rem(me + k, n), other),
                device_id_type=MESH,
            )
            copy.start()
            sent.append(copy)
        out_ref[own_rows, pl.ds(first, width)] = mines[piece][...]
    extra_total = extra_ref[...]
    for k in _shifts(n):
        pltpu.make_async_remote_copy(
            src_ref=extra_ref,
            dst_ref=extra_held.at[k],
            send_sem=send_extra.at[k],
            recv_sem=recv_extra.at[k],
            device_id=(lax.rem(me + n - k, n), other),
            device_id_type=MESH,
        ).wait_recv()
        extra_total = extra_total + extra_held[k]
    extra_out[...] = extra_total
    for piece, (first, width) in enumerate(spans):
        for k in _shifts(n):
            source = lax.rem(me + n - k, n)
            pltpu.make_async_remote_copy(
                src_ref=mines[piece],
                dst_ref=out_ref.at[
                    pl.ds(pl.multiple_of(source * rows, rows), rows), pl.ds(first, width)
                ],
                send_sem=sems[4 * piece + 2].at[k],
                recv_sem=sems[4 * piece + 3].at[k],
                device_id=(source, other),
                device_id_type=MESH,
            ).wait_recv()
    for copy in sent:
        copy.wait_send()


def ctx_sum(whole, extra, n, collective_id, pieces=4):
    rows, cols = whole.shape[0] // n, whole.shape[1]
    lanes = cols // 128
    edges = [128 * (lanes * p // pieces) for p in range(pieces + 1)]
    spans = tuple((edges[p], edges[p + 1] - edges[p]) for p in range(pieces))
    return pl.pallas_call(
        functools.partial(_sum_kernel, n, spans),
        out_shape=(
            jax.ShapeDtypeStruct(whole.shape, whole.dtype),
            jax.ShapeDtypeStruct(extra.shape, extra.dtype),
        ),
        in_specs=[pl.BlockSpec(memory_space=pltpu.VMEM)] * 2,
        out_specs=(pl.BlockSpec(memory_space=pltpu.VMEM),) * 2,
        scratch_shapes=[pltpu.VMEM((n, rows, width), whole.dtype) for _, width in spans]
        + [pltpu.VMEM((rows, width), whole.dtype) for _, width in spans]
        + [pltpu.VMEM((n,) + extra.shape, extra.dtype)]
        + [pltpu.SemaphoreType.DMA((n,))] * (4 * pieces + 2),
        compiler_params=pltpu.CompilerParams(
            collective_id=collective_id, has_side_effects=True, vmem_limit_bytes=VMEM_LIMIT
        ),
    )(whole, extra)


EPS = 1e-05
THETA = 1000000.0
NEGATIVE = -1e30


def rms_forward(values, norm_gain):
    inverse = lax.rsqrt(jnp.mean(values * values, axis=-1, keepdims=True) + EPS)
    return (values * inverse * norm_gain, inverse)


def rms_backward(values, inverse, norm_gain, upstream):
    scaled = upstream * norm_gain
    inner_mean = jnp.mean(scaled * values, axis=-1, keepdims=True)
    through = inverse * (scaled - values * inverse * inverse * inner_mean)
    return (through, upstream * values * inverse)


def rope_tables(positions, head_dim):
    halfway = head_dim // 2
    frequency = THETA ** (-(jnp.arange(halfway, dtype=jnp.float32) * 2.0 / head_dim))
    angles = positions.astype(jnp.float32)[:, None] * frequency[None, :]
    return (jnp.cos(angles)[:, None, :], jnp.sin(angles)[:, None, :])


def rope_apply(values, cosine, sine_table):
    halfway = values.shape[-1] // 2
    first_half = values[..., :halfway]
    second_half = values[..., halfway:]
    return jnp.concatenate(
        [
            first_half * cosine - second_half * sine_table,
            second_half * cosine + first_half * sine_table,
        ],
        axis=-1,
    )


def rope_back(upstream, cosine, sine_table):
    halfway = upstream.shape[-1] // 2
    first_half = upstream[..., :halfway]
    second_half = upstream[..., halfway:]
    return jnp.concatenate(
        [
            first_half * cosine + second_half * sine_table,
            second_half * cosine - first_half * sine_table,
        ],
        axis=-1,
    )


def row_places(block_map, holder, rows_total, place_count):
    piece_len = rows_total // 4
    within = jnp.arange(rows_total, dtype=jnp.int32)
    picked = jnp.sum(jnp.where(jnp.arange(place_count, dtype=jnp.int32) == holder, block_map, 0))
    later = within // piece_len % 2
    piece_index = jnp.where(later == 1, 2 * place_count - 1 - picked, picked)
    return piece_index * piece_len + within % piece_len


def span_places(block_map, first_anchor, shard_span, seq_rows, place_count):
    piece_len = seq_rows // 2
    anchors = first_anchor + jnp.arange(shard_span, dtype=jnp.int32)
    picked = jnp.sum(
        jnp.where(
            jnp.arange(place_count, dtype=jnp.int32)[None, :] == anchors[:, None],
            block_map[None, :],
            0,
        ),
        axis=1,
    )
    within = jnp.arange(seq_rows, dtype=jnp.int32)
    later = within // piece_len % 2
    piece_index = jnp.where(
        later[None, :] == 1, 2 * place_count - 1 - picked[:, None], picked[:, None]
    )
    return (piece_index * piece_len + (within % piece_len)[None, :]).reshape(shard_span * seq_rows)


def gather_rows(rows_low):
    return lax.all_gather(rows_low, "tp", axis=0, tiled=True)


def reduce_rows(partial_rows):
    return lax.psum_scatter(
        partial_rows.astype(jnp.bfloat16), "tp", scatter_dimension=0, tiled=True
    ).astype(jnp.float32)


def per_device(
    block_input,
    block_map,
    attn_gain,
    query_weight,
    key_weight,
    value_weight,
    query_gain,
    key_gain,
    output_weight,
    ffn_gain,
    gate_weight,
    up_weight,
    down_weight,
    cotangent,
):
    place_count = lax.axis_size("ctx")
    place_index = lax.axis_index("ctx")
    head_dim = query_gain.shape[0]
    query_heads = query_weight.shape[1] // head_dim
    kv_heads = key_weight.shape[1] // head_dim
    group_size = query_heads // kv_heads
    score_scale = 1.0 / math.sqrt(head_dim)
    shard_span = 4
    residual_in = block_input.astype(jnp.float32)
    normed_one, inverse_one = rms_forward(residual_in, attn_gain)
    rows_one = gather_rows(normed_one.astype(jnp.bfloat16))
    rows_total = rows_one.shape[0]
    seq_rows = rows_total // 2
    kv_width = kv_heads * head_dim
    own_places = row_places(block_map, place_index, rows_total, place_count)
    query_raw = jnp.dot(rows_one, query_weight, preferred_element_type=jnp.float32).reshape(
        rows_total, query_heads, head_dim
    )
    key_raw = jnp.dot(rows_one, key_weight, preferred_element_type=jnp.float32).reshape(
        rows_total, kv_heads, head_dim
    )
    values_own = jnp.dot(rows_one, value_weight, preferred_element_type=jnp.float32).astype(
        jnp.bfloat16
    )
    query_normed, query_inverse = rms_forward(query_raw, query_gain)
    key_normed, key_inverse = rms_forward(key_raw, key_gain)
    cosine, sine_table = rope_tables(own_places, head_dim)
    query_rot = rope_apply(query_normed, cosine, sine_table).astype(jnp.bfloat16)
    keys_own = (
        rope_apply(key_normed, cosine, sine_table)
        .astype(jnp.bfloat16)
        .reshape(rows_total, kv_width)
    )
    query_blocks = query_rot.reshape(2, seq_rows, kv_heads, group_size, head_dim)
    query_places = own_places[:seq_rows]

    whole_kv = ctx_gather(jnp.concatenate([keys_own, values_own], axis=1), place_count, 0)
    seq_kv = jnp.transpose(
        whole_kv.reshape(place_count, 2, seq_rows, 2 * kv_width), (1, 0, 2, 3)
    ).reshape(2, place_count * seq_rows, 2 * kv_width)
    key_heads = seq_kv[..., :kv_width].reshape(2, place_count * seq_rows, kv_heads, head_dim)
    value_heads = seq_kv[..., kv_width:].reshape(2, place_count * seq_rows, kv_heads, head_dim)
    key_places = span_places(block_map, 0, place_count, seq_rows, place_count)
    allowed = key_places[None, :] <= query_places[:, None]
    scores = (
        jnp.einsum(
            "sqhgd,skhd->shgqk", query_blocks, key_heads, preferred_element_type=jnp.float32
        )
        * score_scale
    )
    top = jnp.max(jnp.where(allowed, scores, NEGATIVE), axis=-1)
    weights = jnp.where(allowed, jnp.exp(scores - top[..., None]), 0.0)
    weight_total = jnp.sum(weights, axis=-1)
    weighted = jnp.einsum(
        "shgqk,skhd->shgqd",
        weights.astype(jnp.bfloat16),
        value_heads,
        preferred_element_type=jnp.float32,
    )
    log_total = top + jnp.log(weight_total)
    attn_rows = jnp.transpose(weighted / weight_total[..., None], (0, 3, 1, 2, 4))
    attn_low = attn_rows.reshape(rows_total, query_heads * head_dim).astype(jnp.bfloat16)
    residual_mid = residual_in + reduce_rows(
        jnp.dot(attn_low, output_weight, preferred_element_type=jnp.float32)
    )
    normed_two, inverse_two = rms_forward(residual_mid, ffn_gain)
    rows_two = gather_rows(normed_two.astype(jnp.bfloat16))
    gate_pre = jnp.dot(rows_two, gate_weight, preferred_element_type=jnp.float32)
    up_pre = jnp.dot(rows_two, up_weight, preferred_element_type=jnp.float32)
    gate_sig = jax.nn.sigmoid(gate_pre)
    activated = (gate_pre * gate_sig * up_pre).astype(jnp.bfloat16)
    block_output = residual_mid + reduce_rows(
        jnp.dot(activated, down_weight, preferred_element_type=jnp.float32)
    )
    grad_rows = gather_rows(cotangent)
    grad_down_t = jnp.dot(grad_rows.T, activated, preferred_element_type=jnp.float32)
    grad_act = jnp.dot(grad_rows, down_weight.T, preferred_element_type=jnp.float32)
    grad_gate_pre = (grad_act * up_pre * gate_sig * (1.0 + gate_pre * (1.0 - gate_sig))).astype(
        jnp.bfloat16
    )
    grad_up_pre = (grad_act * gate_pre * gate_sig).astype(jnp.bfloat16)
    grad_gate = jnp.dot(rows_two.T, grad_gate_pre, preferred_element_type=jnp.float32)
    grad_up = jnp.dot(rows_two.T, grad_up_pre, preferred_element_type=jnp.float32)
    grad_normed_two = reduce_rows(
        jnp.dot(grad_gate_pre, gate_weight.T, preferred_element_type=jnp.float32)
        + jnp.dot(grad_up_pre, up_weight.T, preferred_element_type=jnp.float32)
    )
    through_two, ffn_terms = rms_backward(residual_mid, inverse_two, ffn_gain, grad_normed_two)
    grad_mid = cotangent.astype(jnp.float32) + through_two
    grad_mid_rows = gather_rows(grad_mid.astype(jnp.bfloat16))
    grad_output_t = jnp.dot(grad_mid_rows.T, attn_low, preferred_element_type=jnp.float32)
    grad_attn = jnp.dot(grad_mid_rows, output_weight.T, preferred_element_type=jnp.float32).astype(
        jnp.bfloat16
    )
    grad_attn_blocks = grad_attn.reshape(2, seq_rows, kv_heads, group_size, head_dim)
    delta_rows = jnp.sum(grad_attn_blocks.astype(jnp.float32) * attn_rows, axis=-1)
    delta_rows = jnp.transpose(delta_rows, (0, 2, 3, 1))

    probs = jnp.where(allowed, jnp.exp(scores - log_total[..., None]), 0.0)
    grad_value_seq = jnp.einsum(
        "shgqk,sqhgd->skhd",
        probs.astype(jnp.bfloat16),
        grad_attn_blocks,
        preferred_element_type=jnp.float32,
    )
    grad_probs = jnp.einsum(
        "sqhgd,skhd->shgqk", grad_attn_blocks, value_heads, preferred_element_type=jnp.float32
    )
    grad_scores = (score_scale * probs * (grad_probs - delta_rows[..., None])).astype(jnp.bfloat16)
    query_acc = jnp.einsum(
        "shgqk,skhd->sqhgd", grad_scores, key_heads, preferred_element_type=jnp.float32
    )
    grad_key_seq = jnp.einsum(
        "shgqk,sqhgd->skhd", grad_scores, query_blocks, preferred_element_type=jnp.float32
    )
    grad_kv_seq = jnp.concatenate(
        [
            grad_key_seq.reshape(2, place_count, seq_rows, kv_width),
            grad_value_seq.reshape(2, place_count, seq_rows, kv_width),
        ],
        axis=-1,
    )
    grad_kv_all = jnp.transpose(grad_kv_seq, (1, 0, 2, 3)).reshape(
        place_count * rows_total, 2 * kv_width
    )
    grad_kv_flat = ctx_scatter(
        grad_kv_all.astype(jnp.bfloat16),
        place_count,
        1,
    )
    grad_keys_flat, grad_values_flat = grad_kv_flat[:, :kv_width], grad_kv_flat[:, kv_width:]
    grad_query_rot = query_acc.reshape(rows_total, query_heads, head_dim)
    grad_key_rot = grad_keys_flat.reshape(rows_total, kv_heads, head_dim)
    grad_query_raw, query_terms = rms_backward(
        query_raw, query_inverse, query_gain, rope_back(grad_query_rot, cosine, sine_table)
    )
    grad_key_raw, key_terms = rms_backward(
        key_raw, key_inverse, key_gain, rope_back(grad_key_rot, cosine, sine_table)
    )
    grad_query_low = grad_query_raw.reshape(rows_total, query_heads * head_dim).astype(jnp.bfloat16)
    grad_key_low = grad_key_raw.reshape(rows_total, kv_width).astype(jnp.bfloat16)
    grad_value_low = grad_values_flat.astype(jnp.bfloat16)
    grad_query = jnp.dot(rows_one.T, grad_query_low, preferred_element_type=jnp.float32)
    grad_key = jnp.dot(rows_one.T, grad_key_low, preferred_element_type=jnp.float32)
    grad_value = jnp.dot(rows_one.T, grad_value_low, preferred_element_type=jnp.float32)
    grad_normed_one = reduce_rows(
        jnp.dot(grad_query_low, query_weight.T, preferred_element_type=jnp.float32)
        + jnp.dot(grad_key_low, key_weight.T, preferred_element_type=jnp.float32)
        + jnp.dot(grad_value_low, value_weight.T, preferred_element_type=jnp.float32)
    )
    through_one, attn_terms = rms_backward(residual_in, inverse_one, attn_gain, grad_normed_one)
    input_grad = grad_mid + through_one
    weight_parts = (grad_query, grad_key, grad_value, grad_output_t, grad_gate, grad_up, grad_down_t)
    widths = [part.shape[1] for part in weight_parts]
    gain_parts = (
        jnp.sum(attn_terms, axis=0),
        jnp.sum(query_terms, axis=(0, 1)),
        jnp.sum(key_terms, axis=(0, 1)),
        jnp.sum(ffn_terms, axis=0),
    )
    gain_sizes = [part.shape[0] for part in gain_parts]
    gain_flat = lax.psum(jnp.concatenate(gain_parts), "tp")
    gain_pad = -gain_flat.shape[0] % 1024
    summed, gains = ctx_sum(
        jnp.concatenate([part.astype(jnp.bfloat16) for part in weight_parts], axis=1),
        jnp.pad(gain_flat, (0, gain_pad)).reshape(8, -1),
        place_count,
        2,
    )
    summed = summed.astype(jnp.float32)
    gains = gains.reshape(-1)
    offsets = [sum(widths[:k]) for k in range(len(widths) + 1)]
    shared_query, shared_key, shared_value, output_t, shared_gate, shared_up, down_t = (
        summed[:, offsets[k] : offsets[k + 1]] for k in range(len(widths))
    )
    shared_output = output_t.T
    shared_down = down_t.T
    gain_attn = gains[: gain_sizes[0]]
    gain_query = gains[gain_sizes[0] : gain_sizes[0] + gain_sizes[1]]
    gain_key = gains[gain_sizes[0] + gain_sizes[1] : gain_sizes[0] + gain_sizes[1] + gain_sizes[2]]
    gain_ffn = gains[gain_sizes[0] + gain_sizes[1] + gain_sizes[2] : sum(gain_sizes)]
    return (
        block_output,
        input_grad,
        gain_attn,
        shared_query,
        shared_key,
        shared_value,
        gain_query,
        gain_key,
        shared_output,
        gain_ffn,
        shared_gate,
        shared_up,
        shared_down,
    )


def solution(mesh):
    return jax.shard_map(
        per_device,
        mesh=mesh,
        in_specs=(
            P(("ctx", "tp"), None),
            P(),
            P(),
            P(None, "tp"),
            P(None, "tp"),
            P(None, "tp"),
            P(),
            P(),
            P("tp", None),
            P(),
            P(None, "tp"),
            P(None, "tp"),
            P("tp", None),
            P(("ctx", "tp"), None),
        ),
        out_specs=(
            P(("ctx", "tp"), None),
            P(("ctx", "tp"), None),
            P(),
            P(None, "tp"),
            P(None, "tp"),
            P(None, "tp"),
            P(),
            P(),
            P("tp", None),
            P(),
            P(None, "tp"),
            P(None, "tp"),
            P("tp", None),
        ),
        check_vma=False,
    )
```

```python
import functools
import math

import jax
import jax.numpy as jnp
from jax import lax
from jax.experimental import pallas as pl
from jax.experimental.pallas import tpu as pltpu
from jax.sharding import PartitionSpec as P

MESH = pl.DeviceIdType.MESH
VMEM_LIMIT = 60 * 1024 * 1024


def _shifts(n):
    order = []
    for k in range(1, n // 2 + 1):
        order.append(k)
        if n - k != k:
            order.append(n - k)
    return order


def _enter(n, me, peer_axis):
    barrier = pltpu.get_barrier_semaphore()
    for k in _shifts(n):
        pl.semaphore_signal(
            barrier, 1, device_id=(lax.rem(me + k, n), peer_axis), device_id_type=MESH
        )
    pl.semaphore_wait(barrier, n - 1)


def _gather_kernel(n, part_ref, out_ref, send_sem, recv_sem):
    me = lax.axis_index("ctx")
    other = lax.axis_index("tp")
    rows = part_ref.shape[0]
    _enter(n, me, other)
    copies = []
    for k in _shifts(n):
        copy = pltpu.make_async_remote_copy(
            src_ref=part_ref,
            dst_ref=out_ref.at[pl.ds(pl.multiple_of(me * rows, rows), rows)],
            send_sem=send_sem.at[k],
            recv_sem=recv_sem.at[k],
            device_id=(lax.rem(me + k, n), other),
            device_id_type=MESH,
        )
        copy.start()
        copies.append(copy)
    out_ref[pl.ds(pl.multiple_of(me * rows, rows), rows), :] = part_ref[...]
    for k in _shifts(n):
        source = lax.rem(me + n - k, n)
        pltpu.make_async_remote_copy(
            src_ref=part_ref,
            dst_ref=out_ref.at[pl.ds(pl.multiple_of(source * rows, rows), rows)],
            send_sem=send_sem.at[k],
            recv_sem=recv_sem.at[k],
            device_id=(source, other),
            device_id_type=MESH,
        ).wait_recv()
    for copy in copies:
        copy.wait_send()


def ctx_gather(part, n, collective_id):
    rows, cols = part.shape
    return pl.pallas_call(
        functools.partial(_gather_kernel, n),
        out_shape=jax.ShapeDtypeStruct((n * rows, cols), part.dtype),
        in_specs=[pl.BlockSpec(memory_space=pltpu.VMEM)],
        out_specs=pl.BlockSpec(memory_space=pltpu.VMEM),
        scratch_shapes=[pltpu.SemaphoreType.DMA((n,)), pltpu.SemaphoreType.DMA((n,))],
        compiler_params=pltpu.CompilerParams(
            collective_id=collective_id, has_side_effects=True, vmem_limit_bytes=VMEM_LIMIT
        ),
    )(part)


def _scatter_sum(n, me, other, whole_ref, held, send_sem, recv_sem, rows):
    copies = []
    for k in _shifts(n):
        target = lax.rem(me + k, n)
        copy = pltpu.make_async_remote_copy(
            src_ref=whole_ref.at[pl.ds(pl.multiple_of(target * rows, rows), rows)],
            dst_ref=held.at[k],
            send_sem=send_sem.at[k],
            recv_sem=recv_sem.at[k],
            device_id=(target, other),
            device_id_type=MESH,
        )
        copy.start()
        copies.append(copy)
    total = whole_ref[pl.ds(pl.multiple_of(me * rows, rows), rows), :].astype(jnp.float32)
    for k in _shifts(n):
        source = lax.rem(me + n - k, n)
        pltpu.make_async_remote_copy(
            src_ref=whole_ref.at[pl.ds(0, rows)],
            dst_ref=held.at[k],
            send_sem=send_sem.at[k],
            recv_sem=recv_sem.at[k],
            device_id=(source, other),
            device_id_type=MESH,
        ).wait_recv()
        total = total + held[k].astype(jnp.float32)
    for copy in copies:
        copy.wait_send()
    return total


def _scatter_kernel(n, whole_ref, out_ref, held, send_sem, recv_sem):
    me = lax.axis_index("ctx")
    other = lax.axis_index("tp")
    rows = out_ref.shape[0]
    _enter(n, me, other)
    out_ref[...] = _scatter_sum(n, me, other, whole_ref, held, send_sem, recv_sem, rows)


def ctx_scatter(whole, n, collective_id):
    rows, cols = whole.shape[0] // n, whole.shape[1]
    return pl.pallas_call(
        functools.partial(_scatter_kernel, n),
        out_shape=jax.ShapeDtypeStruct((rows, cols), jnp.float32),
        in_specs=[pl.BlockSpec(memory_space=pltpu.VMEM)],
        out_specs=pl.BlockSpec(memory_space=pltpu.VMEM),
        scratch_shapes=[
            pltpu.VMEM((n, rows, cols), whole.dtype),
            pltpu.SemaphoreType.DMA((n,)),
            pltpu.SemaphoreType.DMA((n,)),
        ],
        compiler_params=pltpu.CompilerParams(
            collective_id=collective_id, has_side_effects=True, vmem_limit_bytes=VMEM_LIMIT
        ),
    )(whole)


def _sum_kernel(n, spans, whole_ref, extra_ref, out_ref, extra_out, *scratch):
    pieces = len(spans)
    helds, mines, extra_held = scratch[:pieces], scratch[pieces : 2 * pieces], scratch[2 * pieces]
    sems = scratch[2 * pieces + 1 :]
    send_extra, recv_extra = sems[4 * pieces], sems[4 * pieces + 1]
    me = lax.axis_index("ctx")
    other = lax.axis_index("tp")
    rows = whole_ref.shape[0] // n
    own_rows = pl.ds(pl.multiple_of(me * rows, rows), rows)
    _enter(n, me, other)
    sent = []
    for k in _shifts(n):
        copy = pltpu.make_async_remote_copy(
            src_ref=extra_ref,
            dst_ref=extra_held.at[k],
            send_sem=send_extra.at[k],
            recv_sem=recv_extra.at[k],
            device_id=(lax.rem(me + k, n), other),
            device_id_type=MESH,
        )
        copy.start()
        sent.append(copy)
    for piece, (first, width) in enumerate(spans):
        for k in _shifts(n):
            target = lax.rem(me + k, n)
            copy = pltpu.make_async_remote_copy(
                src_ref=whole_ref.at[
                    pl.ds(pl.multiple_of(target * rows, rows), rows), pl.ds(first, width)
                ],
                dst_ref=helds[piece].at[k],
                send_sem=sems[4 * piece].at[k],
                recv_sem=sems[4 * piece + 1].at[k],
                device_id=(target, other),
                device_id_type=MESH,
            )
            copy.start()
            sent.append(copy)
    for piece, (first, width) in enumerate(spans):
        total = whole_ref[own_rows, pl.ds(first, width)].astype(jnp.float32)
        for k in _shifts(n):
            pltpu.make_async_remote_copy(
                src_ref=whole_ref.at[pl.ds(0, rows), pl.ds(first, width)],
                dst_ref=helds[piece].at[k],
                send_sem=sems[4 * piece].at[k],
                recv_sem=sems[4 * piece + 1].at[k],
                device_id=(lax.rem(me + n - k, n), other),
                device_id_type=MESH,
            ).wait_recv()
            total = total + helds[piece][k].astype(jnp.float32)
        mines[piece][...] = total.astype(mines[piece].dtype)
        for k in _shifts(n):
            copy = pltpu.make_async_remote_copy(
                src_ref=mines[piece],
                dst_ref=out_ref.at[own_rows, pl.ds(first, width)],
                send_sem=sems[4 * piece + 2].at[k],
                recv_sem=sems[4 * piece + 3].at[k],
                device_id=(lax.rem(me + k, n), other),
                device_id_type=MESH,
            )
            copy.start()
            sent.append(copy)
        out_ref[own_rows, pl.ds(first, width)] = mines[piece][...]
    extra_total = extra_ref[...]
    for k in _shifts(n):
        pltpu.make_async_remote_copy(
            src_ref=extra_ref,
            dst_ref=extra_held.at[k],
            send_sem=send_extra.at[k],
            recv_sem=recv_extra.at[k],
            device_id=(lax.rem(me + n - k, n), other),
            device_id_type=MESH,
        ).wait_recv()
        extra_total = extra_total + extra_held[k]
    extra_out[...] = extra_total
    for piece, (first, width) in enumerate(spans):
        for k in _shifts(n):
            source = lax.rem(me + n - k, n)
            pltpu.make_async_remote_copy(
                src_ref=mines[piece],
                dst_ref=out_ref.at[
                    pl.ds(pl.multiple_of(source * rows, rows), rows), pl.ds(first, width)
                ],
                send_sem=sems[4 * piece + 2].at[k],
                recv_sem=sems[4 * piece + 3].at[k],
                device_id=(source, other),
                device_id_type=MESH,
            ).wait_recv()
    for copy in sent:
        copy.wait_send()


def ctx_sum(whole, extra, n, collective_id, pieces=8):
    rows, cols = whole.shape[0] // n, whole.shape[1]
    lanes = cols // 128
    edges = [128 * (lanes * p // pieces) for p in range(pieces + 1)]
    spans = tuple((edges[p], edges[p + 1] - edges[p]) for p in range(pieces))
    return pl.pallas_call(
        functools.partial(_sum_kernel, n, spans),
        out_shape=(
            jax.ShapeDtypeStruct(whole.shape, whole.dtype),
            jax.ShapeDtypeStruct(extra.shape, extra.dtype),
        ),
        in_specs=[pl.BlockSpec(memory_space=pltpu.VMEM)] * 2,
        out_specs=(pl.BlockSpec(memory_space=pltpu.VMEM),) * 2,
        scratch_shapes=[pltpu.VMEM((n, rows, width), whole.dtype) for _, width in spans]
        + [pltpu.VMEM((rows, width), whole.dtype) for _, width in spans]
        + [pltpu.VMEM((n,) + extra.shape, extra.dtype)]
        + [pltpu.SemaphoreType.DMA((n,))] * (4 * pieces + 2),
        compiler_params=pltpu.CompilerParams(
            collective_id=collective_id, has_side_effects=True, vmem_limit_bytes=VMEM_LIMIT
        ),
    )(whole, extra)


EPS = 1e-05
THETA = 1000000.0
NEGATIVE = -1e30


def rms_forward(values, norm_gain):
    inverse = lax.rsqrt(jnp.mean(values * values, axis=-1, keepdims=True) + EPS)
    return (values * inverse * norm_gain, inverse)


def rms_backward(values, inverse, norm_gain, upstream):
    scaled = upstream * norm_gain
    inner_mean = jnp.mean(scaled * values, axis=-1, keepdims=True)
    through = inverse * (scaled - values * inverse * inverse * inner_mean)
    return (through, upstream * values * inverse)


def rope_tables(positions, head_dim):
    halfway = head_dim // 2
    frequency = THETA ** (-(jnp.arange(halfway, dtype=jnp.float32) * 2.0 / head_dim))
    angles = positions.astype(jnp.float32)[:, None] * frequency[None, :]
    return (jnp.cos(angles)[:, None, :], jnp.sin(angles)[:, None, :])


def rope_apply(values, cosine, sine_table):
    halfway = values.shape[-1] // 2
    first_half = values[..., :halfway]
    second_half = values[..., halfway:]
    return jnp.concatenate(
        [
            first_half * cosine - second_half * sine_table,
            second_half * cosine + first_half * sine_table,
        ],
        axis=-1,
    )


def rope_back(upstream, cosine, sine_table):
    halfway = upstream.shape[-1] // 2
    first_half = upstream[..., :halfway]
    second_half = upstream[..., halfway:]
    return jnp.concatenate(
        [
            first_half * cosine + second_half * sine_table,
            second_half * cosine - first_half * sine_table,
        ],
        axis=-1,
    )


def row_places(block_map, holder, rows_total, place_count):
    piece_len = rows_total // 4
    within = jnp.arange(rows_total, dtype=jnp.int32)
    picked = jnp.sum(jnp.where(jnp.arange(place_count, dtype=jnp.int32) == holder, block_map, 0))
    later = within // piece_len % 2
    piece_index = jnp.where(later == 1, 2 * place_count - 1 - picked, picked)
    return piece_index * piece_len + within % piece_len


def span_places(block_map, first_anchor, shard_span, seq_rows, place_count):
    piece_len = seq_rows // 2
    anchors = first_anchor + jnp.arange(shard_span, dtype=jnp.int32)
    picked = jnp.sum(
        jnp.where(
            jnp.arange(place_count, dtype=jnp.int32)[None, :] == anchors[:, None],
            block_map[None, :],
            0,
        ),
        axis=1,
    )
    within = jnp.arange(seq_rows, dtype=jnp.int32)
    later = within // piece_len % 2
    piece_index = jnp.where(
        later[None, :] == 1, 2 * place_count - 1 - picked[:, None], picked[:, None]
    )
    return (piece_index * piece_len + (within % piece_len)[None, :]).reshape(shard_span * seq_rows)


def gather_rows(rows_low):
    return lax.all_gather(rows_low, "tp", axis=0, tiled=True)


def reduce_rows(partial_rows):
    return lax.psum_scatter(
        partial_rows.astype(jnp.bfloat16), "tp", scatter_dimension=0, tiled=True
    ).astype(jnp.float32)


def per_device(
    block_input,
    block_map,
    attn_gain,
    query_weight,
    key_weight,
    value_weight,
    query_gain,
    key_gain,
    output_weight,
    ffn_gain,
    gate_weight,
    up_weight,
    down_weight,
    cotangent,
):
    place_count = lax.axis_size("ctx")
    place_index = lax.axis_index("ctx")
    head_dim = query_gain.shape[0]
    query_heads = query_weight.shape[1] // head_dim
    kv_heads = key_weight.shape[1] // head_dim
    group_size = query_heads // kv_heads
    score_scale = 1.0 / math.sqrt(head_dim)
    shard_span = 4
    residual_in = block_input.astype(jnp.float32)
    normed_one, inverse_one = rms_forward(residual_in, attn_gain)
    rows_one = gather_rows(normed_one.astype(jnp.bfloat16))
    rows_total = rows_one.shape[0]
    seq_rows = rows_total // 2
    kv_width = kv_heads * head_dim
    own_places = row_places(block_map, place_index, rows_total, place_count)
    query_raw = jnp.dot(rows_one, query_weight, preferred_element_type=jnp.float32).reshape(
        rows_total, query_heads, head_dim
    )
    key_raw = jnp.dot(rows_one, key_weight, preferred_element_type=jnp.float32).reshape(
        rows_total, kv_heads, head_dim
    )
    values_own = jnp.dot(rows_one, value_weight, preferred_element_type=jnp.float32).astype(
        jnp.bfloat16
    )
    query_normed, query_inverse = rms_forward(query_raw, query_gain)
    key_normed, key_inverse = rms_forward(key_raw, key_gain)
    cosine, sine_table = rope_tables(own_places, head_dim)
    query_rot = rope_apply(query_normed, cosine, sine_table).astype(jnp.bfloat16)
    keys_own = (
        rope_apply(key_normed, cosine, sine_table)
        .astype(jnp.bfloat16)
        .reshape(rows_total, kv_width)
    )
    query_blocks = query_rot.reshape(2, seq_rows, kv_heads, group_size, head_dim)
    query_places = own_places[:seq_rows]

    whole_kv = ctx_gather(jnp.concatenate([keys_own, values_own], axis=1), place_count, 0)
    seq_kv = jnp.transpose(
        whole_kv.reshape(place_count, 2, seq_rows, 2 * kv_width), (1, 0, 2, 3)
    ).reshape(2, place_count * seq_rows, 2 * kv_width)
    key_heads = seq_kv[..., :kv_width].reshape(2, place_count * seq_rows, kv_heads, head_dim)
    value_heads = seq_kv[..., kv_width:].reshape(2, place_count * seq_rows, kv_heads, head_dim)
    key_places = span_places(block_map, 0, place_count, seq_rows, place_count)
    allowed = key_places[None, :] <= query_places[:, None]
    scores = (
        jnp.einsum(
            "sqhgd,skhd->shgqk", query_blocks, key_heads, preferred_element_type=jnp.float32
        )
        * score_scale
    )
    top = jnp.max(jnp.where(allowed, scores, NEGATIVE), axis=-1)
    weights = jnp.where(allowed, jnp.exp(scores - top[..., None]), 0.0)
    weight_total = jnp.sum(weights, axis=-1)
    weighted = jnp.einsum(
        "shgqk,skhd->shgqd",
        weights.astype(jnp.bfloat16),
        value_heads,
        preferred_element_type=jnp.float32,
    )
    log_total = top + jnp.log(weight_total)
    attn_rows = jnp.transpose(weighted / weight_total[..., None], (0, 3, 1, 2, 4))
    attn_low = attn_rows.reshape(rows_total, query_heads * head_dim).astype(jnp.bfloat16)
    residual_mid = residual_in + reduce_rows(
        jnp.dot(attn_low, output_weight, preferred_element_type=jnp.float32)
    )
    normed_two, inverse_two = rms_forward(residual_mid, ffn_gain)
    rows_two = gather_rows(normed_two.astype(jnp.bfloat16))
    gate_pre = jnp.dot(rows_two, gate_weight, preferred_element_type=jnp.float32)
    up_pre = jnp.dot(rows_two, up_weight, preferred_element_type=jnp.float32)
    gate_sig = jax.nn.sigmoid(gate_pre)
    activated = (gate_pre * gate_sig * up_pre).astype(jnp.bfloat16)
    block_output = residual_mid + reduce_rows(
        jnp.dot(activated, down_weight, preferred_element_type=jnp.float32)
    )
    grad_rows = gather_rows(cotangent)
    grad_down_t = jnp.dot(grad_rows.T, activated, preferred_element_type=jnp.float32)
    grad_act = jnp.dot(grad_rows, down_weight.T, preferred_element_type=jnp.float32)
    grad_gate_pre = (grad_act * up_pre * gate_sig * (1.0 + gate_pre * (1.0 - gate_sig))).astype(
        jnp.bfloat16
    )
    grad_up_pre = (grad_act * gate_pre * gate_sig).astype(jnp.bfloat16)
    grad_gate = jnp.dot(rows_two.T, grad_gate_pre, preferred_element_type=jnp.float32)
    grad_up = jnp.dot(rows_two.T, grad_up_pre, preferred_element_type=jnp.float32)
    grad_normed_two = reduce_rows(
        jnp.dot(grad_gate_pre, gate_weight.T, preferred_element_type=jnp.float32)
        + jnp.dot(grad_up_pre, up_weight.T, preferred_element_type=jnp.float32)
    )
    through_two, ffn_terms = rms_backward(residual_mid, inverse_two, ffn_gain, grad_normed_two)
    grad_mid = cotangent.astype(jnp.float32) + through_two
    grad_mid_rows = gather_rows(grad_mid.astype(jnp.bfloat16))
    grad_output_t = jnp.dot(grad_mid_rows.T, attn_low, preferred_element_type=jnp.float32)
    grad_attn = jnp.dot(grad_mid_rows, output_weight.T, preferred_element_type=jnp.float32).astype(
        jnp.bfloat16
    )
    grad_attn_blocks = grad_attn.reshape(2, seq_rows, kv_heads, group_size, head_dim)
    delta_rows = jnp.sum(grad_attn_blocks.astype(jnp.float32) * attn_rows, axis=-1)
    delta_rows = jnp.transpose(delta_rows, (0, 2, 3, 1))

    probs = jnp.where(allowed, jnp.exp(scores - log_total[..., None]), 0.0)
    grad_value_seq = jnp.einsum(
        "shgqk,sqhgd->skhd",
        probs.astype(jnp.bfloat16),
        grad_attn_blocks,
        preferred_element_type=jnp.float32,
    )
    grad_probs = jnp.einsum(
        "sqhgd,skhd->shgqk", grad_attn_blocks, value_heads, preferred_element_type=jnp.float32
    )
    grad_scores = (score_scale * probs * (grad_probs - delta_rows[..., None])).astype(jnp.bfloat16)
    query_acc = jnp.einsum(
        "shgqk,skhd->sqhgd", grad_scores, key_heads, preferred_element_type=jnp.float32
    )
    grad_key_seq = jnp.einsum(
        "shgqk,sqhgd->skhd", grad_scores, query_blocks, preferred_element_type=jnp.float32
    )
    grad_kv_seq = jnp.concatenate(
        [
            grad_key_seq.reshape(2, place_count, seq_rows, kv_width),
            grad_value_seq.reshape(2, place_count, seq_rows, kv_width),
        ],
        axis=-1,
    )
    grad_kv_all = jnp.transpose(grad_kv_seq, (1, 0, 2, 3)).reshape(
        place_count * rows_total, 2 * kv_width
    )
    grad_kv_flat = ctx_scatter(
        grad_kv_all.astype(jnp.bfloat16),
        place_count,
        1,
    )
    grad_keys_flat, grad_values_flat = grad_kv_flat[:, :kv_width], grad_kv_flat[:, kv_width:]
    grad_query_rot = query_acc.reshape(rows_total, query_heads, head_dim)
    grad_key_rot = grad_keys_flat.reshape(rows_total, kv_heads, head_dim)
    grad_query_raw, query_terms = rms_backward(
        query_raw, query_inverse, query_gain, rope_back(grad_query_rot, cosine, sine_table)
    )
    grad_key_raw, key_terms = rms_backward(
        key_raw, key_inverse, key_gain, rope_back(grad_key_rot, cosine, sine_table)
    )
    grad_query_low = grad_query_raw.reshape(rows_total, query_heads * head_dim).astype(jnp.bfloat16)
    grad_key_low = grad_key_raw.reshape(rows_total, kv_width).astype(jnp.bfloat16)
    grad_value_low = grad_values_flat.astype(jnp.bfloat16)
    grad_query = jnp.dot(rows_one.T, grad_query_low, preferred_element_type=jnp.float32)
    grad_key = jnp.dot(rows_one.T, grad_key_low, preferred_element_type=jnp.float32)
    grad_value = jnp.dot(rows_one.T, grad_value_low, preferred_element_type=jnp.float32)
    grad_normed_one = reduce_rows(
        jnp.dot(grad_query_low, query_weight.T, preferred_element_type=jnp.float32)
        + jnp.dot(grad_key_low, key_weight.T, preferred_element_type=jnp.float32)
        + jnp.dot(grad_value_low, value_weight.T, preferred_element_type=jnp.float32)
    )
    through_one, attn_terms = rms_backward(residual_in, inverse_one, attn_gain, grad_normed_one)
    input_grad = grad_mid + through_one
    weight_parts = (grad_query, grad_key, grad_value, grad_output_t, grad_gate, grad_up, grad_down_t)
    widths = [part.shape[1] for part in weight_parts]
    gain_parts = (
        jnp.sum(attn_terms, axis=0),
        jnp.sum(query_terms, axis=(0, 1)),
        jnp.sum(key_terms, axis=(0, 1)),
        jnp.sum(ffn_terms, axis=0),
    )
    gain_sizes = [part.shape[0] for part in gain_parts]
    gain_flat = lax.psum(jnp.concatenate(gain_parts), "tp")
    gain_pad = -gain_flat.shape[0] % 1024
    summed, gains = ctx_sum(
        jnp.concatenate([part.astype(jnp.bfloat16) for part in weight_parts], axis=1),
        jnp.pad(gain_flat, (0, gain_pad)).reshape(8, -1),
        place_count,
        2,
    )
    summed = summed.astype(jnp.float32)
    gains = gains.reshape(-1)
    offsets = [sum(widths[:k]) for k in range(len(widths) + 1)]
    shared_query, shared_key, shared_value, output_t, shared_gate, shared_up, down_t = (
        summed[:, offsets[k] : offsets[k + 1]] for k in range(len(widths))
    )
    shared_output = output_t.T
    shared_down = down_t.T
    gain_attn = gains[: gain_sizes[0]]
    gain_query = gains[gain_sizes[0] : gain_sizes[0] + gain_sizes[1]]
    gain_key = gains[gain_sizes[0] + gain_sizes[1] : gain_sizes[0] + gain_sizes[1] + gain_sizes[2]]
    gain_ffn = gains[gain_sizes[0] + gain_sizes[1] + gain_sizes[2] : sum(gain_sizes)]
    return (
        block_output,
        input_grad,
        gain_attn,
        shared_query,
        shared_key,
        shared_value,
        gain_query,
        gain_key,
        shared_output,
        gain_ffn,
        shared_gate,
        shared_up,
        shared_down,
    )


def solution(mesh):
    return jax.shard_map(
        per_device,
        mesh=mesh,
        in_specs=(
            P(("ctx", "tp"), None),
            P(),
            P(),
            P(None, "tp"),
            P(None, "tp"),
            P(None, "tp"),
            P(),
            P(),
            P("tp", None),
            P(),
            P(None, "tp"),
            P(None, "tp"),
            P("tp", None),
            P(("ctx", "tp"), None),
        ),
        out_specs=(
            P(("ctx", "tp"), None),
            P(("ctx", "tp"), None),
            P(),
            P(None, "tp"),
            P(None, "tp"),
            P(None, "tp"),
            P(),
            P(),
            P("tp", None),
            P(),
            P(None, "tp"),
            P(None, "tp"),
            P("tp", None),
        ),
        check_vma=False,
    )
```

```python
import functools
import math

import jax
import jax.numpy as jnp
from jax import lax
from jax.experimental import pallas as pl
from jax.experimental.pallas import tpu as pltpu
from jax.sharding import PartitionSpec as P

MESH = pl.DeviceIdType.MESH
VMEM_LIMIT = 60 * 1024 * 1024


def _shifts(n):
    order = []
    for k in range(1, n // 2 + 1):
        order.append(k)
        if n - k != k:
            order.append(n - k)
    return order


def _enter(n, me, peer_axis):
    barrier = pltpu.get_barrier_semaphore()
    for k in _shifts(n):
        pl.semaphore_signal(
            barrier, 1, device_id=(lax.rem(me + k, n), peer_axis), device_id_type=MESH
        )
    pl.semaphore_wait(barrier, n - 1)


def _gather_kernel(n, part_ref, out_ref, send_sem, recv_sem):
    me = lax.axis_index("ctx")
    other = lax.axis_index("tp")
    rows = part_ref.shape[0]
    _enter(n, me, other)
    copies = []
    for k in _shifts(n):
        copy = pltpu.make_async_remote_copy(
            src_ref=part_ref,
            dst_ref=out_ref.at[pl.ds(pl.multiple_of(me * rows, rows), rows)],
            send_sem=send_sem.at[k],
            recv_sem=recv_sem.at[k],
            device_id=(lax.rem(me + k, n), other),
            device_id_type=MESH,
        )
        copy.start()
        copies.append(copy)
    out_ref[pl.ds(pl.multiple_of(me * rows, rows), rows), :] = part_ref[...]
    for k in _shifts(n):
        source = lax.rem(me + n - k, n)
        pltpu.make_async_remote_copy(
            src_ref=part_ref,
            dst_ref=out_ref.at[pl.ds(pl.multiple_of(source * rows, rows), rows)],
            send_sem=send_sem.at[k],
            recv_sem=recv_sem.at[k],
            device_id=(source, other),
            device_id_type=MESH,
        ).wait_recv()
    for copy in copies:
        copy.wait_send()


def ctx_gather(part, n, collective_id):
    rows, cols = part.shape
    return pl.pallas_call(
        functools.partial(_gather_kernel, n),
        out_shape=jax.ShapeDtypeStruct((n * rows, cols), part.dtype),
        in_specs=[pl.BlockSpec(memory_space=pltpu.VMEM)],
        out_specs=pl.BlockSpec(memory_space=pltpu.VMEM),
        scratch_shapes=[pltpu.SemaphoreType.DMA((n,)), pltpu.SemaphoreType.DMA((n,))],
        compiler_params=pltpu.CompilerParams(
            collective_id=collective_id, has_side_effects=True, vmem_limit_bytes=VMEM_LIMIT
        ),
    )(part)


def _scatter_sum(n, me, other, whole_ref, held, send_sem, recv_sem, rows):
    copies = []
    for k in _shifts(n):
        target = lax.rem(me + k, n)
        copy = pltpu.make_async_remote_copy(
            src_ref=whole_ref.at[pl.ds(pl.multiple_of(target * rows, rows), rows)],
            dst_ref=held.at[k],
            send_sem=send_sem.at[k],
            recv_sem=recv_sem.at[k],
            device_id=(target, other),
            device_id_type=MESH,
        )
        copy.start()
        copies.append(copy)
    total = whole_ref[pl.ds(pl.multiple_of(me * rows, rows), rows), :].astype(jnp.float32)
    for k in _shifts(n):
        source = lax.rem(me + n - k, n)
        pltpu.make_async_remote_copy(
            src_ref=whole_ref.at[pl.ds(0, rows)],
            dst_ref=held.at[k],
            send_sem=send_sem.at[k],
            recv_sem=recv_sem.at[k],
            device_id=(source, other),
            device_id_type=MESH,
        ).wait_recv()
        total = total + held[k].astype(jnp.float32)
    for copy in copies:
        copy.wait_send()
    return total


def _scatter_kernel(n, whole_ref, out_ref, held, send_sem, recv_sem):
    me = lax.axis_index("ctx")
    other = lax.axis_index("tp")
    rows = out_ref.shape[0]
    _enter(n, me, other)
    out_ref[...] = _scatter_sum(n, me, other, whole_ref, held, send_sem, recv_sem, rows)


def ctx_scatter(whole, n, collective_id):
    rows, cols = whole.shape[0] // n, whole.shape[1]
    return pl.pallas_call(
        functools.partial(_scatter_kernel, n),
        out_shape=jax.ShapeDtypeStruct((rows, cols), jnp.float32),
        in_specs=[pl.BlockSpec(memory_space=pltpu.VMEM)],
        out_specs=pl.BlockSpec(memory_space=pltpu.VMEM),
        scratch_shapes=[
            pltpu.VMEM((n, rows, cols), whole.dtype),
            pltpu.SemaphoreType.DMA((n,)),
            pltpu.SemaphoreType.DMA((n,)),
        ],
        compiler_params=pltpu.CompilerParams(
            collective_id=collective_id, has_side_effects=True, vmem_limit_bytes=VMEM_LIMIT
        ),
    )(whole)


def _shift_at(n, step):
    half = step // 2 + 1
    return jnp.where(step % 2 == 0, half, n - half)


def _sum_kernel(n, spans, whole_ref, extra_ref, out_ref, extra_out, *scratch):
    pieces = len(spans)
    helds, mines, extra_held = scratch[:pieces], scratch[pieces : 2 * pieces], scratch[2 * pieces]
    sems = scratch[2 * pieces + 1 :]
    send_extra, recv_extra = sems[4 * pieces], sems[4 * pieces + 1]
    me = lax.axis_index("ctx")
    other = lax.axis_index("tp")
    rows = whole_ref.shape[0] // n
    own_rows = pl.ds(pl.multiple_of(me * rows, rows), rows)
    _enter(n, me, other)

    def extra_copy(k, peer):
        return pltpu.make_async_remote_copy(
            src_ref=extra_ref,
            dst_ref=extra_held.at[k],
            send_sem=send_extra.at[k],
            recv_sem=recv_extra.at[k],
            device_id=(peer, other),
            device_id_type=MESH,
        )

    def scatter_copy(piece, k, peer, block):
        first, width = spans[piece]
        return pltpu.make_async_remote_copy(
            src_ref=whole_ref.at[pl.ds(pl.multiple_of(block * rows, rows), rows), pl.ds(first, width)],
            dst_ref=helds[piece].at[k],
            send_sem=sems[4 * piece].at[k],
            recv_sem=sems[4 * piece + 1].at[k],
            device_id=(peer, other),
            device_id_type=MESH,
        )

    def gather_copy(piece, k, peer, block):
        first, width = spans[piece]
        return pltpu.make_async_remote_copy(
            src_ref=mines[piece],
            dst_ref=out_ref.at[pl.ds(pl.multiple_of(block * rows, rows), rows), pl.ds(first, width)],
            send_sem=sems[4 * piece + 2].at[k],
            recv_sem=sems[4 * piece + 3].at[k],
            device_id=(peer, other),
            device_id_type=MESH,
        )

    def each_peer(body):
        def step(index, carry):
            k = _shift_at(n, index)
            return body(k, lax.rem(me + k, n), lax.rem(me + n - k, n), carry)

        return lax.fori_loop(0, n - 1, step, 0)

    def start_extra(k, target, source, carry):
        extra_copy(k, target).start()
        return carry

    each_peer(start_extra)
    for piece in range(pieces):

        def start_scatter(k, target, source, carry, piece=piece):
            scatter_copy(piece, k, target, target).start()
            return carry

        each_peer(start_scatter)
    for piece, (first, width) in enumerate(spans):

        def add_block(index, total, piece=piece):
            k = _shift_at(n, index)
            scatter_copy(piece, k, lax.rem(me + n - k, n), me).wait_recv()
            return total + helds[piece][k].astype(jnp.float32)

        total = lax.fori_loop(
            0, n - 1, add_block, whole_ref[own_rows, pl.ds(first, width)].astype(jnp.float32)
        )
        mines[piece][...] = total.astype(mines[piece].dtype)

        def start_gather(k, target, source, carry, piece=piece):
            gather_copy(piece, k, target, me).start()
            return carry

        each_peer(start_gather)
        out_ref[own_rows, pl.ds(first, width)] = mines[piece][...]

    def add_extra(index, total):
        k = _shift_at(n, index)
        extra_copy(k, lax.rem(me + n - k, n)).wait_recv()
        return total + extra_held[k]

    extra_out[...] = lax.fori_loop(0, n - 1, add_extra, extra_ref[...])
    for piece in range(pieces):

        def finish(k, target, source, carry, piece=piece):
            gather_copy(piece, k, source, source).wait_recv()
            gather_copy(piece, k, target, me).wait_send()
            scatter_copy(piece, k, target, target).wait_send()
            return carry

        each_peer(finish)

    def finish_extra(k, target, source, carry):
        extra_copy(k, target).wait_send()
        return carry

    each_peer(finish_extra)


def ctx_sum(whole, extra, n, collective_id, pieces=8):
    rows, cols = whole.shape[0] // n, whole.shape[1]
    lanes = cols // 128
    edges = [128 * (lanes * p // pieces) for p in range(pieces + 1)]
    spans = tuple((edges[p], edges[p + 1] - edges[p]) for p in range(pieces))
    return pl.pallas_call(
        functools.partial(_sum_kernel, n, spans),
        out_shape=(
            jax.ShapeDtypeStruct(whole.shape, whole.dtype),
            jax.ShapeDtypeStruct(extra.shape, extra.dtype),
        ),
        in_specs=[pl.BlockSpec(memory_space=pltpu.VMEM)] * 2,
        out_specs=(pl.BlockSpec(memory_space=pltpu.VMEM),) * 2,
        scratch_shapes=[pltpu.VMEM((n, rows, width), whole.dtype) for _, width in spans]
        + [pltpu.VMEM((rows, width), whole.dtype) for _, width in spans]
        + [pltpu.VMEM((n,) + extra.shape, extra.dtype)]
        + [pltpu.SemaphoreType.DMA((n,))] * (4 * pieces + 2),
        compiler_params=pltpu.CompilerParams(
            collective_id=collective_id, has_side_effects=True, vmem_limit_bytes=VMEM_LIMIT
        ),
    )(whole, extra)


EPS = 1e-05
THETA = 1000000.0
NEGATIVE = -1e30


def rms_forward(values, norm_gain):
    inverse = lax.rsqrt(jnp.mean(values * values, axis=-1, keepdims=True) + EPS)
    return (values * inverse * norm_gain, inverse)


def rms_backward(values, inverse, norm_gain, upstream):
    scaled = upstream * norm_gain
    inner_mean = jnp.mean(scaled * values, axis=-1, keepdims=True)
    through = inverse * (scaled - values * inverse * inverse * inner_mean)
    return (through, upstream * values * inverse)


def rope_tables(positions, head_dim):
    halfway = head_dim // 2
    frequency = THETA ** (-(jnp.arange(halfway, dtype=jnp.float32) * 2.0 / head_dim))
    angles = positions.astype(jnp.float32)[:, None] * frequency[None, :]
    return (jnp.cos(angles)[:, None, :], jnp.sin(angles)[:, None, :])


def rope_apply(values, cosine, sine_table):
    halfway = values.shape[-1] // 2
    first_half = values[..., :halfway]
    second_half = values[..., halfway:]
    return jnp.concatenate(
        [
            first_half * cosine - second_half * sine_table,
            second_half * cosine + first_half * sine_table,
        ],
        axis=-1,
    )


def rope_back(upstream, cosine, sine_table):
    halfway = upstream.shape[-1] // 2
    first_half = upstream[..., :halfway]
    second_half = upstream[..., halfway:]
    return jnp.concatenate(
        [
            first_half * cosine + second_half * sine_table,
            second_half * cosine - first_half * sine_table,
        ],
        axis=-1,
    )


def row_places(block_map, holder, rows_total, place_count):
    piece_len = rows_total // 4
    within = jnp.arange(rows_total, dtype=jnp.int32)
    picked = jnp.sum(jnp.where(jnp.arange(place_count, dtype=jnp.int32) == holder, block_map, 0))
    later = within // piece_len % 2
    piece_index = jnp.where(later == 1, 2 * place_count - 1 - picked, picked)
    return piece_index * piece_len + within % piece_len


def span_places(block_map, first_anchor, shard_span, seq_rows, place_count):
    piece_len = seq_rows // 2
    anchors = first_anchor + jnp.arange(shard_span, dtype=jnp.int32)
    picked = jnp.sum(
        jnp.where(
            jnp.arange(place_count, dtype=jnp.int32)[None, :] == anchors[:, None],
            block_map[None, :],
            0,
        ),
        axis=1,
    )
    within = jnp.arange(seq_rows, dtype=jnp.int32)
    later = within // piece_len % 2
    piece_index = jnp.where(
        later[None, :] == 1, 2 * place_count - 1 - picked[:, None], picked[:, None]
    )
    return (piece_index * piece_len + (within % piece_len)[None, :]).reshape(shard_span * seq_rows)


def gather_rows(rows_low):
    return lax.all_gather(rows_low, "tp", axis=0, tiled=True)


def reduce_rows(partial_rows):
    return lax.psum_scatter(
        partial_rows.astype(jnp.bfloat16), "tp", scatter_dimension=0, tiled=True
    ).astype(jnp.float32)


def per_device(
    block_input,
    block_map,
    attn_gain,
    query_weight,
    key_weight,
    value_weight,
    query_gain,
    key_gain,
    output_weight,
    ffn_gain,
    gate_weight,
    up_weight,
    down_weight,
    cotangent,
):
    place_count = lax.axis_size("ctx")
    place_index = lax.axis_index("ctx")
    head_dim = query_gain.shape[0]
    query_heads = query_weight.shape[1] // head_dim
    kv_heads = key_weight.shape[1] // head_dim
    group_size = query_heads // kv_heads
    score_scale = 1.0 / math.sqrt(head_dim)
    shard_span = 4
    residual_in = block_input.astype(jnp.float32)
    normed_one, inverse_one = rms_forward(residual_in, attn_gain)
    rows_one = gather_rows(normed_one.astype(jnp.bfloat16))
    rows_total = rows_one.shape[0]
    seq_rows = rows_total // 2
    kv_width = kv_heads * head_dim
    own_places = row_places(block_map, place_index, rows_total, place_count)
    query_raw = jnp.dot(rows_one, query_weight, preferred_element_type=jnp.float32).reshape(
        rows_total, query_heads, head_dim
    )
    key_raw = jnp.dot(rows_one, key_weight, preferred_element_type=jnp.float32).reshape(
        rows_total, kv_heads, head_dim
    )
    values_own = jnp.dot(rows_one, value_weight, preferred_element_type=jnp.float32).astype(
        jnp.bfloat16
    )
    query_normed, query_inverse = rms_forward(query_raw, query_gain)
    key_normed, key_inverse = rms_forward(key_raw, key_gain)
    cosine, sine_table = rope_tables(own_places, head_dim)
    query_rot = rope_apply(query_normed, cosine, sine_table).astype(jnp.bfloat16)
    keys_own = (
        rope_apply(key_normed, cosine, sine_table)
        .astype(jnp.bfloat16)
        .reshape(rows_total, kv_width)
    )
    query_blocks = query_rot.reshape(2, seq_rows, kv_heads, group_size, head_dim)
    query_places = own_places[:seq_rows]

    whole_kv = ctx_gather(jnp.concatenate([keys_own, values_own], axis=1), place_count, 0)
    seq_kv = jnp.transpose(
        whole_kv.reshape(place_count, 2, seq_rows, 2 * kv_width), (1, 0, 2, 3)
    ).reshape(2, place_count * seq_rows, 2 * kv_width)
    key_heads = seq_kv[..., :kv_width].reshape(2, place_count * seq_rows, kv_heads, head_dim)
    value_heads = seq_kv[..., kv_width:].reshape(2, place_count * seq_rows, kv_heads, head_dim)
    key_places = span_places(block_map, 0, place_count, seq_rows, place_count)
    allowed = key_places[None, :] <= query_places[:, None]
    scores = (
        jnp.einsum(
            "sqhgd,skhd->shgqk", query_blocks, key_heads, preferred_element_type=jnp.float32
        )
        * score_scale
    )
    top = jnp.max(jnp.where(allowed, scores, NEGATIVE), axis=-1)
    weights = jnp.where(allowed, jnp.exp(scores - top[..., None]), 0.0)
    weight_total = jnp.sum(weights, axis=-1)
    weighted = jnp.einsum(
        "shgqk,skhd->shgqd",
        weights.astype(jnp.bfloat16),
        value_heads,
        preferred_element_type=jnp.float32,
    )
    log_total = top + jnp.log(weight_total)
    attn_rows = jnp.transpose(weighted / weight_total[..., None], (0, 3, 1, 2, 4))
    attn_low = attn_rows.reshape(rows_total, query_heads * head_dim).astype(jnp.bfloat16)
    residual_mid = residual_in + reduce_rows(
        jnp.dot(attn_low, output_weight, preferred_element_type=jnp.float32)
    )
    normed_two, inverse_two = rms_forward(residual_mid, ffn_gain)
    rows_two = gather_rows(normed_two.astype(jnp.bfloat16))
    gate_pre = jnp.dot(rows_two, gate_weight, preferred_element_type=jnp.float32)
    up_pre = jnp.dot(rows_two, up_weight, preferred_element_type=jnp.float32)
    gate_sig = jax.nn.sigmoid(gate_pre)
    activated = (gate_pre * gate_sig * up_pre).astype(jnp.bfloat16)
    block_output = residual_mid + reduce_rows(
        jnp.dot(activated, down_weight, preferred_element_type=jnp.float32)
    )
    grad_rows = gather_rows(cotangent)
    grad_down_t = jnp.dot(grad_rows.T, activated, preferred_element_type=jnp.float32)
    grad_act = jnp.dot(grad_rows, down_weight.T, preferred_element_type=jnp.float32)
    grad_gate_pre = (grad_act * up_pre * gate_sig * (1.0 + gate_pre * (1.0 - gate_sig))).astype(
        jnp.bfloat16
    )
    grad_up_pre = (grad_act * gate_pre * gate_sig).astype(jnp.bfloat16)
    grad_gate = jnp.dot(rows_two.T, grad_gate_pre, preferred_element_type=jnp.float32)
    grad_up = jnp.dot(rows_two.T, grad_up_pre, preferred_element_type=jnp.float32)
    grad_normed_two = reduce_rows(
        jnp.dot(grad_gate_pre, gate_weight.T, preferred_element_type=jnp.float32)
        + jnp.dot(grad_up_pre, up_weight.T, preferred_element_type=jnp.float32)
    )
    through_two, ffn_terms = rms_backward(residual_mid, inverse_two, ffn_gain, grad_normed_two)
    grad_mid = cotangent.astype(jnp.float32) + through_two
    grad_mid_rows = gather_rows(grad_mid.astype(jnp.bfloat16))
    grad_output_t = jnp.dot(grad_mid_rows.T, attn_low, preferred_element_type=jnp.float32)
    grad_attn = jnp.dot(grad_mid_rows, output_weight.T, preferred_element_type=jnp.float32).astype(
        jnp.bfloat16
    )
    grad_attn_blocks = grad_attn.reshape(2, seq_rows, kv_heads, group_size, head_dim)
    delta_rows = jnp.sum(grad_attn_blocks.astype(jnp.float32) * attn_rows, axis=-1)
    delta_rows = jnp.transpose(delta_rows, (0, 2, 3, 1))

    probs = jnp.where(allowed, jnp.exp(scores - log_total[..., None]), 0.0)
    grad_value_seq = jnp.einsum(
        "shgqk,sqhgd->skhd",
        probs.astype(jnp.bfloat16),
        grad_attn_blocks,
        preferred_element_type=jnp.float32,
    )
    grad_probs = jnp.einsum(
        "sqhgd,skhd->shgqk", grad_attn_blocks, value_heads, preferred_element_type=jnp.float32
    )
    grad_scores = (score_scale * probs * (grad_probs - delta_rows[..., None])).astype(jnp.bfloat16)
    query_acc = jnp.einsum(
        "shgqk,skhd->sqhgd", grad_scores, key_heads, preferred_element_type=jnp.float32
    )
    grad_key_seq = jnp.einsum(
        "shgqk,sqhgd->skhd", grad_scores, query_blocks, preferred_element_type=jnp.float32
    )
    grad_kv_seq = jnp.concatenate(
        [
            grad_key_seq.reshape(2, place_count, seq_rows, kv_width),
            grad_value_seq.reshape(2, place_count, seq_rows, kv_width),
        ],
        axis=-1,
    )
    grad_kv_all = jnp.transpose(grad_kv_seq, (1, 0, 2, 3)).reshape(
        place_count * rows_total, 2 * kv_width
    )
    grad_kv_flat = ctx_scatter(
        grad_kv_all.astype(jnp.bfloat16),
        place_count,
        1,
    )
    grad_keys_flat, grad_values_flat = grad_kv_flat[:, :kv_width], grad_kv_flat[:, kv_width:]
    grad_query_rot = query_acc.reshape(rows_total, query_heads, head_dim)
    grad_key_rot = grad_keys_flat.reshape(rows_total, kv_heads, head_dim)
    grad_query_raw, query_terms = rms_backward(
        query_raw, query_inverse, query_gain, rope_back(grad_query_rot, cosine, sine_table)
    )
    grad_key_raw, key_terms = rms_backward(
        key_raw, key_inverse, key_gain, rope_back(grad_key_rot, cosine, sine_table)
    )
    grad_query_low = grad_query_raw.reshape(rows_total, query_heads * head_dim).astype(jnp.bfloat16)
    grad_key_low = grad_key_raw.reshape(rows_total, kv_width).astype(jnp.bfloat16)
    grad_value_low = grad_values_flat.astype(jnp.bfloat16)
    grad_query = jnp.dot(rows_one.T, grad_query_low, preferred_element_type=jnp.float32)
    grad_key = jnp.dot(rows_one.T, grad_key_low, preferred_element_type=jnp.float32)
    grad_value = jnp.dot(rows_one.T, grad_value_low, preferred_element_type=jnp.float32)
    grad_normed_one = reduce_rows(
        jnp.dot(grad_query_low, query_weight.T, preferred_element_type=jnp.float32)
        + jnp.dot(grad_key_low, key_weight.T, preferred_element_type=jnp.float32)
        + jnp.dot(grad_value_low, value_weight.T, preferred_element_type=jnp.float32)
    )
    through_one, attn_terms = rms_backward(residual_in, inverse_one, attn_gain, grad_normed_one)
    input_grad = grad_mid + through_one
    weight_parts = (grad_query, grad_key, grad_value, grad_output_t, grad_gate, grad_up, grad_down_t)
    widths = [part.shape[1] for part in weight_parts]
    gain_parts = (
        jnp.sum(attn_terms, axis=0),
        jnp.sum(query_terms, axis=(0, 1)),
        jnp.sum(key_terms, axis=(0, 1)),
        jnp.sum(ffn_terms, axis=0),
    )
    gain_sizes = [part.shape[0] for part in gain_parts]
    gain_flat = lax.psum(jnp.concatenate(gain_parts), "tp")
    gain_pad = -gain_flat.shape[0] % 1024
    summed, gains = ctx_sum(
        jnp.concatenate([part.astype(jnp.bfloat16) for part in weight_parts], axis=1),
        jnp.pad(gain_flat, (0, gain_pad)).reshape(8, -1),
        place_count,
        2,
    )
    summed = summed.astype(jnp.float32)
    gains = gains.reshape(-1)
    offsets = [sum(widths[:k]) for k in range(len(widths) + 1)]
    shared_query, shared_key, shared_value, output_t, shared_gate, shared_up, down_t = (
        summed[:, offsets[k] : offsets[k + 1]] for k in range(len(widths))
    )
    shared_output = output_t.T
    shared_down = down_t.T
    gain_attn = gains[: gain_sizes[0]]
    gain_query = gains[gain_sizes[0] : gain_sizes[0] + gain_sizes[1]]
    gain_key = gains[gain_sizes[0] + gain_sizes[1] : gain_sizes[0] + gain_sizes[1] + gain_sizes[2]]
    gain_ffn = gains[gain_sizes[0] + gain_sizes[1] + gain_sizes[2] : sum(gain_sizes)]
    return (
        block_output,
        input_grad,
        gain_attn,
        shared_query,
        shared_key,
        shared_value,
        gain_query,
        gain_key,
        shared_output,
        gain_ffn,
        shared_gate,
        shared_up,
        shared_down,
    )


def solution(mesh):
    return jax.shard_map(
        per_device,
        mesh=mesh,
        in_specs=(
            P(("ctx", "tp"), None),
            P(),
            P(),
            P(None, "tp"),
            P(None, "tp"),
            P(None, "tp"),
            P(),
            P(),
            P("tp", None),
            P(),
            P(None, "tp"),
            P(None, "tp"),
            P("tp", None),
            P(("ctx", "tp"), None),
        ),
        out_specs=(
            P(("ctx", "tp"), None),
            P(("ctx", "tp"), None),
            P(),
            P(None, "tp"),
            P(None, "tp"),
            P(None, "tp"),
            P(),
            P(),
            P("tp", None),
            P(),
            P(None, "tp"),
            P(None, "tp"),
            P("tp", None),
        ),
        check_vma=False,
    )
```

```python
import functools
import math

import jax
import jax.numpy as jnp
from jax import lax
from jax.experimental import pallas as pl
from jax.experimental.pallas import tpu as pltpu
from jax.sharding import PartitionSpec as P

MESH = pl.DeviceIdType.MESH
VMEM_LIMIT = 60 * 1024 * 1024


def _shifts(n):
    order = []
    for k in range(1, n // 2 + 1):
        order.append(k)
        if n - k != k:
            order.append(n - k)
    return order


def _shift_at(n, step):
    half = step // 2 + 1
    return jnp.where(step % 2 == 0, half, n - half)


def _enter(n, me, peer_axis):
    barrier = pltpu.get_barrier_semaphore()
    for k in _shifts(n):
        pl.semaphore_signal(
            barrier, 1, device_id=(lax.rem(me + k, n), peer_axis), device_id_type=MESH
        )
    pl.semaphore_wait(barrier, n - 1)


def _gather_kernel(n, part_ref, out_ref, send_sem, recv_sem):
    me = lax.axis_index("ctx")
    other = lax.axis_index("tp")
    rows = part_ref.shape[0]
    _enter(n, me, other)

    def block_copy(k, peer, block):
        return pltpu.make_async_remote_copy(
            src_ref=part_ref,
            dst_ref=out_ref.at[pl.ds(pl.multiple_of(block * rows, rows), rows)],
            send_sem=send_sem.at[k],
            recv_sem=recv_sem.at[k],
            device_id=(peer, other),
            device_id_type=MESH,
        )

    def start(index, carry):
        k = _shift_at(n, index)
        block_copy(k, lax.rem(me + k, n), me).start()
        return carry

    lax.fori_loop(0, n - 1, start, 0)
    out_ref[pl.ds(pl.multiple_of(me * rows, rows), rows), :] = part_ref[...]

    def finish(index, carry):
        k = _shift_at(n, index)
        source = lax.rem(me + n - k, n)
        block_copy(k, source, source).wait_recv()
        block_copy(k, lax.rem(me + k, n), me).wait_send()
        return carry

    lax.fori_loop(0, n - 1, finish, 0)


def ctx_gather(part, n, collective_id):
    rows, cols = part.shape
    return pl.pallas_call(
        functools.partial(_gather_kernel, n),
        out_shape=jax.ShapeDtypeStruct((n * rows, cols), part.dtype),
        in_specs=[pl.BlockSpec(memory_space=pltpu.VMEM)],
        out_specs=pl.BlockSpec(memory_space=pltpu.VMEM),
        scratch_shapes=[pltpu.SemaphoreType.DMA((n,)), pltpu.SemaphoreType.DMA((n,))],
        compiler_params=pltpu.CompilerParams(
            collective_id=collective_id, has_side_effects=True, vmem_limit_bytes=VMEM_LIMIT
        ),
    )(part)


def _scatter_sum(n, me, other, whole_ref, held, send_sem, recv_sem, rows):
    def block_copy(k, peer, block):
        return pltpu.make_async_remote_copy(
            src_ref=whole_ref.at[pl.ds(pl.multiple_of(block * rows, rows), rows)],
            dst_ref=held.at[k],
            send_sem=send_sem.at[k],
            recv_sem=recv_sem.at[k],
            device_id=(peer, other),
            device_id_type=MESH,
        )

    def start(index, carry):
        k = _shift_at(n, index)
        target = lax.rem(me + k, n)
        block_copy(k, target, target).start()
        return carry

    lax.fori_loop(0, n - 1, start, 0)

    def add_block(index, total):
        k = _shift_at(n, index)
        block_copy(k, lax.rem(me + n - k, n), me).wait_recv()
        return total + held[k].astype(jnp.float32)

    total = lax.fori_loop(
        0,
        n - 1,
        add_block,
        whole_ref[pl.ds(pl.multiple_of(me * rows, rows), rows), :].astype(jnp.float32),
    )

    def finish(index, carry):
        k = _shift_at(n, index)
        target = lax.rem(me + k, n)
        block_copy(k, target, target).wait_send()
        return carry

    lax.fori_loop(0, n - 1, finish, 0)
    return total


def _scatter_kernel(n, whole_ref, out_ref, held, send_sem, recv_sem):
    me = lax.axis_index("ctx")
    other = lax.axis_index("tp")
    rows = out_ref.shape[0]
    _enter(n, me, other)
    out_ref[...] = _scatter_sum(n, me, other, whole_ref, held, send_sem, recv_sem, rows)


def ctx_scatter(whole, n, collective_id):
    rows, cols = whole.shape[0] // n, whole.shape[1]
    return pl.pallas_call(
        functools.partial(_scatter_kernel, n),
        out_shape=jax.ShapeDtypeStruct((rows, cols), jnp.float32),
        in_specs=[pl.BlockSpec(memory_space=pltpu.VMEM)],
        out_specs=pl.BlockSpec(memory_space=pltpu.VMEM),
        scratch_shapes=[
            pltpu.VMEM((n, rows, cols), whole.dtype),
            pltpu.SemaphoreType.DMA((n,)),
            pltpu.SemaphoreType.DMA((n,)),
        ],
        compiler_params=pltpu.CompilerParams(
            collective_id=collective_id, has_side_effects=True, vmem_limit_bytes=VMEM_LIMIT
        ),
    )(whole)


def _sum_kernel(n, spans, whole_ref, extra_ref, out_ref, extra_out, *scratch):
    pieces = len(spans)
    helds, mines, extra_held = scratch[:pieces], scratch[pieces : 2 * pieces], scratch[2 * pieces]
    sems = scratch[2 * pieces + 1 :]
    send_extra, recv_extra = sems[4 * pieces], sems[4 * pieces + 1]
    me = lax.axis_index("ctx")
    other = lax.axis_index("tp")
    rows = whole_ref.shape[0] // n
    own_rows = pl.ds(pl.multiple_of(me * rows, rows), rows)
    _enter(n, me, other)

    def extra_copy(k, peer):
        return pltpu.make_async_remote_copy(
            src_ref=extra_ref,
            dst_ref=extra_held.at[k],
            send_sem=send_extra.at[k],
            recv_sem=recv_extra.at[k],
            device_id=(peer, other),
            device_id_type=MESH,
        )

    def scatter_copy(piece, k, peer, block):
        first, width = spans[piece]
        return pltpu.make_async_remote_copy(
            src_ref=whole_ref.at[pl.ds(pl.multiple_of(block * rows, rows), rows), pl.ds(first, width)],
            dst_ref=helds[piece].at[k],
            send_sem=sems[4 * piece].at[k],
            recv_sem=sems[4 * piece + 1].at[k],
            device_id=(peer, other),
            device_id_type=MESH,
        )

    def gather_copy(piece, k, peer, block):
        first, width = spans[piece]
        return pltpu.make_async_remote_copy(
            src_ref=mines[piece],
            dst_ref=out_ref.at[pl.ds(pl.multiple_of(block * rows, rows), rows), pl.ds(first, width)],
            send_sem=sems[4 * piece + 2].at[k],
            recv_sem=sems[4 * piece + 3].at[k],
            device_id=(peer, other),
            device_id_type=MESH,
        )

    def each_peer(body):
        def step(index, carry):
            k = _shift_at(n, index)
            return body(k, lax.rem(me + k, n), lax.rem(me + n - k, n), carry)

        return lax.fori_loop(0, n - 1, step, 0)

    def start_extra(k, target, source, carry):
        extra_copy(k, target).start()
        return carry

    each_peer(start_extra)
    for piece in range(pieces):

        def start_scatter(k, target, source, carry, piece=piece):
            scatter_copy(piece, k, target, target).start()
            return carry

        each_peer(start_scatter)
    for piece, (first, width) in enumerate(spans):

        def add_block(index, total, piece=piece):
            k = _shift_at(n, index)
            scatter_copy(piece, k, lax.rem(me + n - k, n), me).wait_recv()
            return total + helds[piece][k].astype(jnp.float32)

        total = lax.fori_loop(
            0, n - 1, add_block, whole_ref[own_rows, pl.ds(first, width)].astype(jnp.float32)
        )
        mines[piece][...] = total.astype(mines[piece].dtype)

        def start_gather(k, target, source, carry, piece=piece):
            gather_copy(piece, k, target, me).start()
            return carry

        each_peer(start_gather)
        out_ref[own_rows, pl.ds(first, width)] = mines[piece][...]

    def add_extra(index, total):
        k = _shift_at(n, index)
        extra_copy(k, lax.rem(me + n - k, n)).wait_recv()
        return total + extra_held[k]

    extra_out[...] = lax.fori_loop(0, n - 1, add_extra, extra_ref[...])
    for piece in range(pieces):

        def finish(k, target, source, carry, piece=piece):
            gather_copy(piece, k, source, source).wait_recv()
            gather_copy(piece, k, target, me).wait_send()
            scatter_copy(piece, k, target, target).wait_send()
            return carry

        each_peer(finish)

    def finish_extra(k, target, source, carry):
        extra_copy(k, target).wait_send()
        return carry

    each_peer(finish_extra)


def ctx_sum(whole, extra, n, collective_id, pieces=8):
    rows, cols = whole.shape[0] // n, whole.shape[1]
    lanes = cols // 128
    edges = [128 * (lanes * p // pieces) for p in range(pieces + 1)]
    spans = tuple((edges[p], edges[p + 1] - edges[p]) for p in range(pieces))
    return pl.pallas_call(
        functools.partial(_sum_kernel, n, spans),
        out_shape=(
            jax.ShapeDtypeStruct(whole.shape, whole.dtype),
            jax.ShapeDtypeStruct(extra.shape, extra.dtype),
        ),
        in_specs=[pl.BlockSpec(memory_space=pltpu.VMEM)] * 2,
        out_specs=(pl.BlockSpec(memory_space=pltpu.VMEM),) * 2,
        scratch_shapes=[pltpu.VMEM((n, rows, width), whole.dtype) for _, width in spans]
        + [pltpu.VMEM((rows, width), whole.dtype) for _, width in spans]
        + [pltpu.VMEM((n,) + extra.shape, extra.dtype)]
        + [pltpu.SemaphoreType.DMA((n,))] * (4 * pieces + 2),
        compiler_params=pltpu.CompilerParams(
            collective_id=collective_id, has_side_effects=True, vmem_limit_bytes=VMEM_LIMIT
        ),
    )(whole, extra)


EPS = 1e-05
THETA = 1000000.0
NEGATIVE = -1e30


def rms_forward(values, norm_gain):
    inverse = lax.rsqrt(jnp.mean(values * values, axis=-1, keepdims=True) + EPS)
    return (values * inverse * norm_gain, inverse)


def rms_backward(values, inverse, norm_gain, upstream):
    scaled = upstream * norm_gain
    inner_mean = jnp.mean(scaled * values, axis=-1, keepdims=True)
    through = inverse * (scaled - values * inverse * inverse * inner_mean)
    return (through, upstream * values * inverse)


def rope_tables(positions, head_dim):
    halfway = head_dim // 2
    frequency = THETA ** (-(jnp.arange(halfway, dtype=jnp.float32) * 2.0 / head_dim))
    angles = positions.astype(jnp.float32)[:, None] * frequency[None, :]
    return (jnp.cos(angles)[:, None, :], jnp.sin(angles)[:, None, :])


def rope_apply(values, cosine, sine_table):
    halfway = values.shape[-1] // 2
    first_half = values[..., :halfway]
    second_half = values[..., halfway:]
    return jnp.concatenate(
        [
            first_half * cosine - second_half * sine_table,
            second_half * cosine + first_half * sine_table,
        ],
        axis=-1,
    )


def rope_back(upstream, cosine, sine_table):
    halfway = upstream.shape[-1] // 2
    first_half = upstream[..., :halfway]
    second_half = upstream[..., halfway:]
    return jnp.concatenate(
        [
            first_half * cosine + second_half * sine_table,
            second_half * cosine - first_half * sine_table,
        ],
        axis=-1,
    )


def row_places(block_map, holder, rows_total, place_count):
    piece_len = rows_total // 4
    within = jnp.arange(rows_total, dtype=jnp.int32)
    picked = jnp.sum(jnp.where(jnp.arange(place_count, dtype=jnp.int32) == holder, block_map, 0))
    later = within // piece_len % 2
    piece_index = jnp.where(later == 1, 2 * place_count - 1 - picked, picked)
    return piece_index * piece_len + within % piece_len


def span_places(block_map, first_anchor, shard_span, seq_rows, place_count):
    piece_len = seq_rows // 2
    anchors = first_anchor + jnp.arange(shard_span, dtype=jnp.int32)
    picked = jnp.sum(
        jnp.where(
            jnp.arange(place_count, dtype=jnp.int32)[None, :] == anchors[:, None],
            block_map[None, :],
            0,
        ),
        axis=1,
    )
    within = jnp.arange(seq_rows, dtype=jnp.int32)
    later = within // piece_len % 2
    piece_index = jnp.where(
        later[None, :] == 1, 2 * place_count - 1 - picked[:, None], picked[:, None]
    )
    return (piece_index * piece_len + (within % piece_len)[None, :]).reshape(shard_span * seq_rows)


def gather_rows(rows_low):
    return lax.all_gather(rows_low, "tp", axis=0, tiled=True)


def reduce_rows(partial_rows):
    return lax.psum_scatter(
        partial_rows.astype(jnp.bfloat16), "tp", scatter_dimension=0, tiled=True
    ).astype(jnp.float32)


def per_device(
    block_input,
    block_map,
    attn_gain,
    query_weight,
    key_weight,
    value_weight,
    query_gain,
    key_gain,
    output_weight,
    ffn_gain,
    gate_weight,
    up_weight,
    down_weight,
    cotangent,
):
    place_count = lax.axis_size("ctx")
    place_index = lax.axis_index("ctx")
    head_dim = query_gain.shape[0]
    query_heads = query_weight.shape[1] // head_dim
    kv_heads = key_weight.shape[1] // head_dim
    group_size = query_heads // kv_heads
    score_scale = 1.0 / math.sqrt(head_dim)
    shard_span = 4
    residual_in = block_input.astype(jnp.float32)
    normed_one, inverse_one = rms_forward(residual_in, attn_gain)
    rows_one = gather_rows(normed_one.astype(jnp.bfloat16))
    rows_total = rows_one.shape[0]
    seq_rows = rows_total // 2
    kv_width = kv_heads * head_dim
    own_places = row_places(block_map, place_index, rows_total, place_count)
    query_raw = jnp.dot(rows_one, query_weight, preferred_element_type=jnp.float32).reshape(
        rows_total, query_heads, head_dim
    )
    key_raw = jnp.dot(rows_one, key_weight, preferred_element_type=jnp.float32).reshape(
        rows_total, kv_heads, head_dim
    )
    values_own = jnp.dot(rows_one, value_weight, preferred_element_type=jnp.float32).astype(
        jnp.bfloat16
    )
    query_normed, query_inverse = rms_forward(query_raw, query_gain)
    key_normed, key_inverse = rms_forward(key_raw, key_gain)
    cosine, sine_table = rope_tables(own_places, head_dim)
    query_rot = rope_apply(query_normed, cosine, sine_table).astype(jnp.bfloat16)
    keys_own = (
        rope_apply(key_normed, cosine, sine_table)
        .astype(jnp.bfloat16)
        .reshape(rows_total, kv_width)
    )
    query_blocks = query_rot.reshape(2, seq_rows, kv_heads, group_size, head_dim)
    query_places = own_places[:seq_rows]

    whole_kv = ctx_gather(jnp.concatenate([keys_own, values_own], axis=1), place_count, 0)
    seq_kv = jnp.transpose(
        whole_kv.reshape(place_count, 2, seq_rows, 2 * kv_width), (1, 0, 2, 3)
    ).reshape(2, place_count * seq_rows, 2 * kv_width)
    key_heads = seq_kv[..., :kv_width].reshape(2, place_count * seq_rows, kv_heads, head_dim)
    value_heads = seq_kv[..., kv_width:].reshape(2, place_count * seq_rows, kv_heads, head_dim)
    key_places = span_places(block_map, 0, place_count, seq_rows, place_count)
    allowed = key_places[None, :] <= query_places[:, None]
    scores = (
        jnp.einsum(
            "sqhgd,skhd->shgqk", query_blocks, key_heads, preferred_element_type=jnp.float32
        )
        * score_scale
    )
    top = jnp.max(jnp.where(allowed, scores, NEGATIVE), axis=-1)
    weights = jnp.where(allowed, jnp.exp(scores - top[..., None]), 0.0)
    weight_total = jnp.sum(weights, axis=-1)
    weighted = jnp.einsum(
        "shgqk,skhd->shgqd",
        weights.astype(jnp.bfloat16),
        value_heads,
        preferred_element_type=jnp.float32,
    )
    log_total = top + jnp.log(weight_total)
    attn_rows = jnp.transpose(weighted / weight_total[..., None], (0, 3, 1, 2, 4))
    attn_low = attn_rows.reshape(rows_total, query_heads * head_dim).astype(jnp.bfloat16)
    residual_mid = residual_in + reduce_rows(
        jnp.dot(attn_low, output_weight, preferred_element_type=jnp.float32)
    )
    normed_two, inverse_two = rms_forward(residual_mid, ffn_gain)
    rows_two = gather_rows(normed_two.astype(jnp.bfloat16))
    gate_pre = jnp.dot(rows_two, gate_weight, preferred_element_type=jnp.float32)
    up_pre = jnp.dot(rows_two, up_weight, preferred_element_type=jnp.float32)
    gate_sig = jax.nn.sigmoid(gate_pre)
    activated = (gate_pre * gate_sig * up_pre).astype(jnp.bfloat16)
    block_output = residual_mid + reduce_rows(
        jnp.dot(activated, down_weight, preferred_element_type=jnp.float32)
    )
    grad_rows = gather_rows(cotangent)
    grad_down_t = jnp.dot(grad_rows.T, activated, preferred_element_type=jnp.float32)
    grad_act = jnp.dot(grad_rows, down_weight.T, preferred_element_type=jnp.float32)
    grad_gate_pre = (grad_act * up_pre * gate_sig * (1.0 + gate_pre * (1.0 - gate_sig))).astype(
        jnp.bfloat16
    )
    grad_up_pre = (grad_act * gate_pre * gate_sig).astype(jnp.bfloat16)
    grad_gate = jnp.dot(rows_two.T, grad_gate_pre, preferred_element_type=jnp.float32)
    grad_up = jnp.dot(rows_two.T, grad_up_pre, preferred_element_type=jnp.float32)
    grad_normed_two = reduce_rows(
        jnp.dot(grad_gate_pre, gate_weight.T, preferred_element_type=jnp.float32)
        + jnp.dot(grad_up_pre, up_weight.T, preferred_element_type=jnp.float32)
    )
    through_two, ffn_terms = rms_backward(residual_mid, inverse_two, ffn_gain, grad_normed_two)
    grad_mid = cotangent.astype(jnp.float32) + through_two
    grad_mid_rows = gather_rows(grad_mid.astype(jnp.bfloat16))
    grad_output_t = jnp.dot(grad_mid_rows.T, attn_low, preferred_element_type=jnp.float32)
    grad_attn = jnp.dot(grad_mid_rows, output_weight.T, preferred_element_type=jnp.float32).astype(
        jnp.bfloat16
    )
    grad_attn_blocks = grad_attn.reshape(2, seq_rows, kv_heads, group_size, head_dim)
    delta_rows = jnp.sum(grad_attn_blocks.astype(jnp.float32) * attn_rows, axis=-1)
    delta_rows = jnp.transpose(delta_rows, (0, 2, 3, 1))

    probs = jnp.where(allowed, jnp.exp(scores - log_total[..., None]), 0.0)
    grad_value_seq = jnp.einsum(
        "shgqk,sqhgd->skhd",
        probs.astype(jnp.bfloat16),
        grad_attn_blocks,
        preferred_element_type=jnp.float32,
    )
    grad_probs = jnp.einsum(
        "sqhgd,skhd->shgqk", grad_attn_blocks, value_heads, preferred_element_type=jnp.float32
    )
    grad_scores = (score_scale * probs * (grad_probs - delta_rows[..., None])).astype(jnp.bfloat16)
    query_acc = jnp.einsum(
        "shgqk,skhd->sqhgd", grad_scores, key_heads, preferred_element_type=jnp.float32
    )
    grad_key_seq = jnp.einsum(
        "shgqk,sqhgd->skhd", grad_scores, query_blocks, preferred_element_type=jnp.float32
    )
    grad_kv_seq = jnp.concatenate(
        [
            grad_key_seq.reshape(2, place_count, seq_rows, kv_width),
            grad_value_seq.reshape(2, place_count, seq_rows, kv_width),
        ],
        axis=-1,
    )
    grad_kv_all = jnp.transpose(grad_kv_seq, (1, 0, 2, 3)).reshape(
        place_count * rows_total, 2 * kv_width
    )
    grad_kv_flat = ctx_scatter(
        grad_kv_all.astype(jnp.bfloat16),
        place_count,
        1,
    )
    grad_keys_flat, grad_values_flat = grad_kv_flat[:, :kv_width], grad_kv_flat[:, kv_width:]
    grad_query_rot = query_acc.reshape(rows_total, query_heads, head_dim)
    grad_key_rot = grad_keys_flat.reshape(rows_total, kv_heads, head_dim)
    grad_query_raw, query_terms = rms_backward(
        query_raw, query_inverse, query_gain, rope_back(grad_query_rot, cosine, sine_table)
    )
    grad_key_raw, key_terms = rms_backward(
        key_raw, key_inverse, key_gain, rope_back(grad_key_rot, cosine, sine_table)
    )
    grad_query_low = grad_query_raw.reshape(rows_total, query_heads * head_dim).astype(jnp.bfloat16)
    grad_key_low = grad_key_raw.reshape(rows_total, kv_width).astype(jnp.bfloat16)
    grad_value_low = grad_values_flat.astype(jnp.bfloat16)
    grad_query = jnp.dot(rows_one.T, grad_query_low, preferred_element_type=jnp.float32)
    grad_key = jnp.dot(rows_one.T, grad_key_low, preferred_element_type=jnp.float32)
    grad_value = jnp.dot(rows_one.T, grad_value_low, preferred_element_type=jnp.float32)
    grad_normed_one = reduce_rows(
        jnp.dot(grad_query_low, query_weight.T, preferred_element_type=jnp.float32)
        + jnp.dot(grad_key_low, key_weight.T, preferred_element_type=jnp.float32)
        + jnp.dot(grad_value_low, value_weight.T, preferred_element_type=jnp.float32)
    )
    through_one, attn_terms = rms_backward(residual_in, inverse_one, attn_gain, grad_normed_one)
    input_grad = grad_mid + through_one
    weight_parts = (grad_query, grad_key, grad_value, grad_output_t, grad_gate, grad_up, grad_down_t)
    widths = [part.shape[1] for part in weight_parts]
    gain_parts = (
        jnp.sum(attn_terms, axis=0),
        jnp.sum(query_terms, axis=(0, 1)),
        jnp.sum(key_terms, axis=(0, 1)),
        jnp.sum(ffn_terms, axis=0),
    )
    gain_sizes = [part.shape[0] for part in gain_parts]
    gain_flat = lax.psum(jnp.concatenate(gain_parts), "tp")
    gain_pad = -gain_flat.shape[0] % 1024
    summed, gains = ctx_sum(
        jnp.concatenate([part.astype(jnp.bfloat16) for part in weight_parts], axis=1),
        jnp.pad(gain_flat, (0, gain_pad)).reshape(8, -1),
        place_count,
        2,
    )
    summed = summed.astype(jnp.float32)
    gains = gains.reshape(-1)
    offsets = [sum(widths[:k]) for k in range(len(widths) + 1)]
    shared_query, shared_key, shared_value, output_t, shared_gate, shared_up, down_t = (
        summed[:, offsets[k] : offsets[k + 1]] for k in range(len(widths))
    )
    shared_output = output_t.T
    shared_down = down_t.T
    gain_attn = gains[: gain_sizes[0]]
    gain_query = gains[gain_sizes[0] : gain_sizes[0] + gain_sizes[1]]
    gain_key = gains[gain_sizes[0] + gain_sizes[1] : gain_sizes[0] + gain_sizes[1] + gain_sizes[2]]
    gain_ffn = gains[gain_sizes[0] + gain_sizes[1] + gain_sizes[2] : sum(gain_sizes)]
    return (
        block_output,
        input_grad,
        gain_attn,
        shared_query,
        shared_key,
        shared_value,
        gain_query,
        gain_key,
        shared_output,
        gain_ffn,
        shared_gate,
        shared_up,
        shared_down,
    )


def solution(mesh):
    return jax.shard_map(
        per_device,
        mesh=mesh,
        in_specs=(
            P(("ctx", "tp"), None),
            P(),
            P(),
            P(None, "tp"),
            P(None, "tp"),
            P(None, "tp"),
            P(),
            P(),
            P("tp", None),
            P(),
            P(None, "tp"),
            P(None, "tp"),
            P("tp", None),
            P(("ctx", "tp"), None),
        ),
        out_specs=(
            P(("ctx", "tp"), None),
            P(("ctx", "tp"), None),
            P(),
            P(None, "tp"),
            P(None, "tp"),
            P(None, "tp"),
            P(),
            P(),
            P("tp", None),
            P(),
            P(None, "tp"),
            P(None, "tp"),
            P("tp", None),
        ),
        check_vma=False,
    )
```

```python
import functools
import math

import jax
import jax.numpy as jnp
from jax import lax
from jax.experimental import pallas as pl
from jax.experimental.pallas import tpu as pltpu
from jax.sharding import PartitionSpec as P

MESH = pl.DeviceIdType.MESH
VMEM_LIMIT = 60 * 1024 * 1024


def _shifts(n):
    order = []
    for k in range(1, n // 2 + 1):
        order.append(k)
        if n - k != k:
            order.append(n - k)
    return order


def _enter(n, me, peer_axis):
    barrier = pltpu.get_barrier_semaphore()
    for k in _shifts(n):
        pl.semaphore_signal(
            barrier, 1, device_id=(lax.rem(me + k, n), peer_axis), device_id_type=MESH
        )
    pl.semaphore_wait(barrier, n - 1)


def _gather_kernel(n, part_ref, out_ref, send_sem, recv_sem):
    me = lax.axis_index("ctx")
    other = lax.axis_index("tp")
    rows = part_ref.shape[0]
    _enter(n, me, other)
    copies = []
    for k in _shifts(n):
        copy = pltpu.make_async_remote_copy(
            src_ref=part_ref,
            dst_ref=out_ref.at[pl.ds(pl.multiple_of(me * rows, rows), rows)],
            send_sem=send_sem.at[k],
            recv_sem=recv_sem.at[k],
            device_id=(lax.rem(me + k, n), other),
            device_id_type=MESH,
        )
        copy.start()
        copies.append(copy)
    out_ref[pl.ds(pl.multiple_of(me * rows, rows), rows), :] = part_ref[...]
    for k in _shifts(n):
        source = lax.rem(me + n - k, n)
        pltpu.make_async_remote_copy(
            src_ref=part_ref,
            dst_ref=out_ref.at[pl.ds(pl.multiple_of(source * rows, rows), rows)],
            send_sem=send_sem.at[k],
            recv_sem=recv_sem.at[k],
            device_id=(source, other),
            device_id_type=MESH,
        ).wait_recv()
    for copy in copies:
        copy.wait_send()


def ctx_gather(part, n, collective_id):
    rows, cols = part.shape
    return pl.pallas_call(
        functools.partial(_gather_kernel, n),
        out_shape=jax.ShapeDtypeStruct((n * rows, cols), part.dtype),
        in_specs=[pl.BlockSpec(memory_space=pltpu.VMEM)],
        out_specs=pl.BlockSpec(memory_space=pltpu.VMEM),
        scratch_shapes=[pltpu.SemaphoreType.DMA((n,)), pltpu.SemaphoreType.DMA((n,))],
        compiler_params=pltpu.CompilerParams(
            collective_id=collective_id, has_side_effects=True, vmem_limit_bytes=VMEM_LIMIT
        ),
    )(part)


def _scatter_sum(n, me, other, whole_ref, held, send_sem, recv_sem, rows):
    copies = []
    for k in _shifts(n):
        target = lax.rem(me + k, n)
        copy = pltpu.make_async_remote_copy(
            src_ref=whole_ref.at[pl.ds(pl.multiple_of(target * rows, rows), rows)],
            dst_ref=held.at[k],
            send_sem=send_sem.at[k],
            recv_sem=recv_sem.at[k],
            device_id=(target, other),
            device_id_type=MESH,
        )
        copy.start()
        copies.append(copy)
    total = whole_ref[pl.ds(pl.multiple_of(me * rows, rows), rows), :].astype(jnp.float32)
    for k in _shifts(n):
        source = lax.rem(me + n - k, n)
        pltpu.make_async_remote_copy(
            src_ref=whole_ref.at[pl.ds(0, rows)],
            dst_ref=held.at[k],
            send_sem=send_sem.at[k],
            recv_sem=recv_sem.at[k],
            device_id=(source, other),
            device_id_type=MESH,
        ).wait_recv()
        total = total + held[k].astype(jnp.float32)
    for copy in copies:
        copy.wait_send()
    return total


def _scatter_kernel(n, whole_ref, out_ref, held, send_sem, recv_sem):
    me = lax.axis_index("ctx")
    other = lax.axis_index("tp")
    rows = out_ref.shape[0]
    _enter(n, me, other)
    out_ref[...] = _scatter_sum(n, me, other, whole_ref, held, send_sem, recv_sem, rows)


def ctx_scatter(whole, n, collective_id):
    rows, cols = whole.shape[0] // n, whole.shape[1]
    return pl.pallas_call(
        functools.partial(_scatter_kernel, n),
        out_shape=jax.ShapeDtypeStruct((rows, cols), jnp.float32),
        in_specs=[pl.BlockSpec(memory_space=pltpu.VMEM)],
        out_specs=pl.BlockSpec(memory_space=pltpu.VMEM),
        scratch_shapes=[
            pltpu.VMEM((n, rows, cols), whole.dtype),
            pltpu.SemaphoreType.DMA((n,)),
            pltpu.SemaphoreType.DMA((n,)),
        ],
        compiler_params=pltpu.CompilerParams(
            collective_id=collective_id, has_side_effects=True, vmem_limit_bytes=VMEM_LIMIT
        ),
    )(whole)


def _shift_at(n, step):
    half = step // 2 + 1
    return jnp.where(step % 2 == 0, half, n - half)


def _sum_kernel(n, spans, whole_ref, extra_ref, out_ref, extra_out, *scratch):
    pieces = len(spans)
    helds, mines, extra_held = scratch[:pieces], scratch[pieces : 2 * pieces], scratch[2 * pieces]
    sems = scratch[2 * pieces + 1 :]
    send_extra, recv_extra = sems[4 * pieces], sems[4 * pieces + 1]
    me = lax.axis_index("ctx")
    other = lax.axis_index("tp")
    rows = whole_ref.shape[0] // n
    own_rows = pl.ds(pl.multiple_of(me * rows, rows), rows)
    _enter(n, me, other)

    def extra_copy(k, peer):
        return pltpu.make_async_remote_copy(
            src_ref=extra_ref,
            dst_ref=extra_held.at[k],
            send_sem=send_extra.at[k],
            recv_sem=recv_extra.at[k],
            device_id=(peer, other),
            device_id_type=MESH,
        )

    def scatter_copy(piece, k, peer, block):
        first, width = spans[piece]
        return pltpu.make_async_remote_copy(
            src_ref=whole_ref.at[pl.ds(pl.multiple_of(block * rows, rows), rows), pl.ds(first, width)],
            dst_ref=helds[piece].at[k],
            send_sem=sems[4 * piece].at[k],
            recv_sem=sems[4 * piece + 1].at[k],
            device_id=(peer, other),
            device_id_type=MESH,
        )

    def gather_copy(piece, k, peer, block):
        first, width = spans[piece]
        return pltpu.make_async_remote_copy(
            src_ref=mines[piece],
            dst_ref=out_ref.at[pl.ds(pl.multiple_of(block * rows, rows), rows), pl.ds(first, width)],
            send_sem=sems[4 * piece + 2].at[k],
            recv_sem=sems[4 * piece + 3].at[k],
            device_id=(peer, other),
            device_id_type=MESH,
        )

    def each_peer(body):
        def step(index, carry):
            k = _shift_at(n, index)
            return body(k, lax.rem(me + k, n), lax.rem(me + n - k, n), carry)

        return lax.fori_loop(0, n - 1, step, 0)

    def start_extra(k, target, source, carry):
        extra_copy(k, target).start()
        return carry

    each_peer(start_extra)
    for piece in range(pieces):

        def start_scatter(k, target, source, carry, piece=piece):
            scatter_copy(piece, k, target, target).start()
            return carry

        each_peer(start_scatter)
    for piece, (first, width) in enumerate(spans):

        def add_block(index, total, piece=piece):
            k = _shift_at(n, index)
            scatter_copy(piece, k, lax.rem(me + n - k, n), me).wait_recv()
            return total + helds[piece][k].astype(jnp.float32)

        total = lax.fori_loop(
            0, n - 1, add_block, whole_ref[own_rows, pl.ds(first, width)].astype(jnp.float32)
        )
        mines[piece][...] = total.astype(mines[piece].dtype)

        def start_gather(k, target, source, carry, piece=piece):
            gather_copy(piece, k, target, me).start()
            return carry

        each_peer(start_gather)
        out_ref[own_rows, pl.ds(first, width)] = mines[piece][...]

    def add_extra(index, total):
        k = _shift_at(n, index)
        extra_copy(k, lax.rem(me + n - k, n)).wait_recv()
        return total + extra_held[k]

    extra_out[...] = lax.fori_loop(0, n - 1, add_extra, extra_ref[...])
    for piece in range(pieces):

        def finish(k, target, source, carry, piece=piece):
            gather_copy(piece, k, source, source).wait_recv()
            gather_copy(piece, k, target, me).wait_send()
            scatter_copy(piece, k, target, target).wait_send()
            return carry

        each_peer(finish)

    def finish_extra(k, target, source, carry):
        extra_copy(k, target).wait_send()
        return carry

    each_peer(finish_extra)


def ctx_sum(whole, extra, n, collective_id, pieces=11):
    rows, cols = whole.shape[0] // n, whole.shape[1]
    lanes = cols // 128
    edges = [128 * (lanes * p // pieces) for p in range(pieces + 1)]
    spans = tuple((edges[p], edges[p + 1] - edges[p]) for p in range(pieces))
    return pl.pallas_call(
        functools.partial(_sum_kernel, n, spans),
        out_shape=(
            jax.ShapeDtypeStruct(whole.shape, whole.dtype),
            jax.ShapeDtypeStruct(extra.shape, extra.dtype),
        ),
        in_specs=[pl.BlockSpec(memory_space=pltpu.VMEM)] * 2,
        out_specs=(pl.BlockSpec(memory_space=pltpu.VMEM),) * 2,
        scratch_shapes=[pltpu.VMEM((n, rows, width), whole.dtype) for _, width in spans]
        + [pltpu.VMEM((rows, width), whole.dtype) for _, width in spans]
        + [pltpu.VMEM((n,) + extra.shape, extra.dtype)]
        + [pltpu.SemaphoreType.DMA((n,))] * (4 * pieces + 2),
        compiler_params=pltpu.CompilerParams(
            collective_id=collective_id, has_side_effects=True, vmem_limit_bytes=VMEM_LIMIT
        ),
    )(whole, extra)


EPS = 1e-05
THETA = 1000000.0
NEGATIVE = -1e30


def rms_forward(values, norm_gain):
    inverse = lax.rsqrt(jnp.mean(values * values, axis=-1, keepdims=True) + EPS)
    return (values * inverse * norm_gain, inverse)


def rms_backward(values, inverse, norm_gain, upstream):
    scaled = upstream * norm_gain
    inner_mean = jnp.mean(scaled * values, axis=-1, keepdims=True)
    through = inverse * (scaled - values * inverse * inverse * inner_mean)
    return (through, upstream * values * inverse)


def rope_tables(positions, head_dim):
    halfway = head_dim // 2
    frequency = THETA ** (-(jnp.arange(halfway, dtype=jnp.float32) * 2.0 / head_dim))
    angles = positions.astype(jnp.float32)[:, None] * frequency[None, :]
    return (jnp.cos(angles)[:, None, :], jnp.sin(angles)[:, None, :])


def rope_apply(values, cosine, sine_table):
    halfway = values.shape[-1] // 2
    first_half = values[..., :halfway]
    second_half = values[..., halfway:]
    return jnp.concatenate(
        [
            first_half * cosine - second_half * sine_table,
            second_half * cosine + first_half * sine_table,
        ],
        axis=-1,
    )


def rope_back(upstream, cosine, sine_table):
    halfway = upstream.shape[-1] // 2
    first_half = upstream[..., :halfway]
    second_half = upstream[..., halfway:]
    return jnp.concatenate(
        [
            first_half * cosine + second_half * sine_table,
            second_half * cosine - first_half * sine_table,
        ],
        axis=-1,
    )


def row_places(block_map, holder, rows_total, place_count):
    piece_len = rows_total // 4
    within = jnp.arange(rows_total, dtype=jnp.int32)
    picked = jnp.sum(jnp.where(jnp.arange(place_count, dtype=jnp.int32) == holder, block_map, 0))
    later = within // piece_len % 2
    piece_index = jnp.where(later == 1, 2 * place_count - 1 - picked, picked)
    return piece_index * piece_len + within % piece_len


def span_places(block_map, first_anchor, shard_span, seq_rows, place_count):
    piece_len = seq_rows // 2
    anchors = first_anchor + jnp.arange(shard_span, dtype=jnp.int32)
    picked = jnp.sum(
        jnp.where(
            jnp.arange(place_count, dtype=jnp.int32)[None, :] == anchors[:, None],
            block_map[None, :],
            0,
        ),
        axis=1,
    )
    within = jnp.arange(seq_rows, dtype=jnp.int32)
    later = within // piece_len % 2
    piece_index = jnp.where(
        later[None, :] == 1, 2 * place_count - 1 - picked[:, None], picked[:, None]
    )
    return (piece_index * piece_len + (within % piece_len)[None, :]).reshape(shard_span * seq_rows)


def gather_rows(rows_low):
    return lax.all_gather(rows_low, "tp", axis=0, tiled=True)


def reduce_rows(partial_rows):
    return lax.psum_scatter(
        partial_rows.astype(jnp.bfloat16), "tp", scatter_dimension=0, tiled=True
    ).astype(jnp.float32)


def per_device(
    block_input,
    block_map,
    attn_gain,
    query_weight,
    key_weight,
    value_weight,
    query_gain,
    key_gain,
    output_weight,
    ffn_gain,
    gate_weight,
    up_weight,
    down_weight,
    cotangent,
):
    place_count = lax.axis_size("ctx")
    place_index = lax.axis_index("ctx")
    head_dim = query_gain.shape[0]
    query_heads = query_weight.shape[1] // head_dim
    kv_heads = key_weight.shape[1] // head_dim
    group_size = query_heads // kv_heads
    score_scale = 1.0 / math.sqrt(head_dim)
    shard_span = 4
    residual_in = block_input.astype(jnp.float32)
    normed_one, inverse_one = rms_forward(residual_in, attn_gain)
    rows_one = gather_rows(normed_one.astype(jnp.bfloat16))
    rows_total = rows_one.shape[0]
    seq_rows = rows_total // 2
    kv_width = kv_heads * head_dim
    own_places = row_places(block_map, place_index, rows_total, place_count)
    query_raw = jnp.dot(rows_one, query_weight, preferred_element_type=jnp.float32).reshape(
        rows_total, query_heads, head_dim
    )
    key_raw = jnp.dot(rows_one, key_weight, preferred_element_type=jnp.float32).reshape(
        rows_total, kv_heads, head_dim
    )
    values_own = jnp.dot(rows_one, value_weight, preferred_element_type=jnp.float32).astype(
        jnp.bfloat16
    )
    query_normed, query_inverse = rms_forward(query_raw, query_gain)
    key_normed, key_inverse = rms_forward(key_raw, key_gain)
    cosine, sine_table = rope_tables(own_places, head_dim)
    query_rot = rope_apply(query_normed, cosine, sine_table).astype(jnp.bfloat16)
    keys_own = (
        rope_apply(key_normed, cosine, sine_table)
        .astype(jnp.bfloat16)
        .reshape(rows_total, kv_width)
    )
    query_blocks = query_rot.reshape(2, seq_rows, kv_heads, group_size, head_dim)
    query_places = own_places[:seq_rows]

    whole_kv = ctx_gather(jnp.concatenate([keys_own, values_own], axis=1), place_count, 0)
    seq_kv = jnp.transpose(
        whole_kv.reshape(place_count, 2, seq_rows, 2 * kv_width), (1, 0, 2, 3)
    ).reshape(2, place_count * seq_rows, 2 * kv_width)
    key_heads = seq_kv[..., :kv_width].reshape(2, place_count * seq_rows, kv_heads, head_dim)
    value_heads = seq_kv[..., kv_width:].reshape(2, place_count * seq_rows, kv_heads, head_dim)
    key_places = span_places(block_map, 0, place_count, seq_rows, place_count)
    allowed = key_places[None, :] <= query_places[:, None]
    scores = (
        jnp.einsum(
            "sqhgd,skhd->shgqk", query_blocks, key_heads, preferred_element_type=jnp.float32
        )
        * score_scale
    )
    top = jnp.max(jnp.where(allowed, scores, NEGATIVE), axis=-1)
    weights = jnp.where(allowed, jnp.exp(scores - top[..., None]), 0.0)
    weight_total = jnp.sum(weights, axis=-1)
    weighted = jnp.einsum(
        "shgqk,skhd->shgqd",
        weights.astype(jnp.bfloat16),
        value_heads,
        preferred_element_type=jnp.float32,
    )
    log_total = top + jnp.log(weight_total)
    attn_rows = jnp.transpose(weighted / weight_total[..., None], (0, 3, 1, 2, 4))
    attn_low = attn_rows.reshape(rows_total, query_heads * head_dim).astype(jnp.bfloat16)
    residual_mid = residual_in + reduce_rows(
        jnp.dot(attn_low, output_weight, preferred_element_type=jnp.float32)
    )
    normed_two, inverse_two = rms_forward(residual_mid, ffn_gain)
    rows_two = gather_rows(normed_two.astype(jnp.bfloat16))
    gate_pre = jnp.dot(rows_two, gate_weight, preferred_element_type=jnp.float32)
    up_pre = jnp.dot(rows_two, up_weight, preferred_element_type=jnp.float32)
    gate_sig = jax.nn.sigmoid(gate_pre)
    activated = (gate_pre * gate_sig * up_pre).astype(jnp.bfloat16)
    block_output = residual_mid + reduce_rows(
        jnp.dot(activated, down_weight, preferred_element_type=jnp.float32)
    )
    grad_rows = gather_rows(cotangent)
    grad_down_t = jnp.dot(grad_rows.T, activated, preferred_element_type=jnp.float32)
    grad_act = jnp.dot(grad_rows, down_weight.T, preferred_element_type=jnp.float32)
    grad_gate_pre = (grad_act * up_pre * gate_sig * (1.0 + gate_pre * (1.0 - gate_sig))).astype(
        jnp.bfloat16
    )
    grad_up_pre = (grad_act * gate_pre * gate_sig).astype(jnp.bfloat16)
    grad_gate = jnp.dot(rows_two.T, grad_gate_pre, preferred_element_type=jnp.float32)
    grad_up = jnp.dot(rows_two.T, grad_up_pre, preferred_element_type=jnp.float32)
    grad_normed_two = reduce_rows(
        jnp.dot(grad_gate_pre, gate_weight.T, preferred_element_type=jnp.float32)
        + jnp.dot(grad_up_pre, up_weight.T, preferred_element_type=jnp.float32)
    )
    through_two, ffn_terms = rms_backward(residual_mid, inverse_two, ffn_gain, grad_normed_two)
    grad_mid = cotangent.astype(jnp.float32) + through_two
    grad_mid_rows = gather_rows(grad_mid.astype(jnp.bfloat16))
    grad_output_t = jnp.dot(grad_mid_rows.T, attn_low, preferred_element_type=jnp.float32)
    grad_attn = jnp.dot(grad_mid_rows, output_weight.T, preferred_element_type=jnp.float32).astype(
        jnp.bfloat16
    )
    grad_attn_blocks = grad_attn.reshape(2, seq_rows, kv_heads, group_size, head_dim)
    delta_rows = jnp.sum(grad_attn_blocks.astype(jnp.float32) * attn_rows, axis=-1)
    delta_rows = jnp.transpose(delta_rows, (0, 2, 3, 1))

    probs = jnp.where(allowed, jnp.exp(scores - log_total[..., None]), 0.0)
    grad_value_seq = jnp.einsum(
        "shgqk,sqhgd->skhd",
        probs.astype(jnp.bfloat16),
        grad_attn_blocks,
        preferred_element_type=jnp.float32,
    )
    grad_probs = jnp.einsum(
        "sqhgd,skhd->shgqk", grad_attn_blocks, value_heads, preferred_element_type=jnp.float32
    )
    grad_scores = (score_scale * probs * (grad_probs - delta_rows[..., None])).astype(jnp.bfloat16)
    query_acc = jnp.einsum(
        "shgqk,skhd->sqhgd", grad_scores, key_heads, preferred_element_type=jnp.float32
    )
    grad_key_seq = jnp.einsum(
        "shgqk,sqhgd->skhd", grad_scores, query_blocks, preferred_element_type=jnp.float32
    )
    grad_kv_seq = jnp.concatenate(
        [
            grad_key_seq.reshape(2, place_count, seq_rows, kv_width),
            grad_value_seq.reshape(2, place_count, seq_rows, kv_width),
        ],
        axis=-1,
    )
    grad_kv_all = jnp.transpose(grad_kv_seq, (1, 0, 2, 3)).reshape(
        place_count * rows_total, 2 * kv_width
    )
    grad_kv_flat = ctx_scatter(
        grad_kv_all.astype(jnp.bfloat16),
        place_count,
        1,
    )
    grad_keys_flat, grad_values_flat = grad_kv_flat[:, :kv_width], grad_kv_flat[:, kv_width:]
    grad_query_rot = query_acc.reshape(rows_total, query_heads, head_dim)
    grad_key_rot = grad_keys_flat.reshape(rows_total, kv_heads, head_dim)
    grad_query_raw, query_terms = rms_backward(
        query_raw, query_inverse, query_gain, rope_back(grad_query_rot, cosine, sine_table)
    )
    grad_key_raw, key_terms = rms_backward(
        key_raw, key_inverse, key_gain, rope_back(grad_key_rot, cosine, sine_table)
    )
    grad_query_low = grad_query_raw.reshape(rows_total, query_heads * head_dim).astype(jnp.bfloat16)
    grad_key_low = grad_key_raw.reshape(rows_total, kv_width).astype(jnp.bfloat16)
    grad_value_low = grad_values_flat.astype(jnp.bfloat16)
    grad_query = jnp.dot(rows_one.T, grad_query_low, preferred_element_type=jnp.float32)
    grad_key = jnp.dot(rows_one.T, grad_key_low, preferred_element_type=jnp.float32)
    grad_value = jnp.dot(rows_one.T, grad_value_low, preferred_element_type=jnp.float32)
    grad_normed_one = reduce_rows(
        jnp.dot(grad_query_low, query_weight.T, preferred_element_type=jnp.float32)
        + jnp.dot(grad_key_low, key_weight.T, preferred_element_type=jnp.float32)
        + jnp.dot(grad_value_low, value_weight.T, preferred_element_type=jnp.float32)
    )
    through_one, attn_terms = rms_backward(residual_in, inverse_one, attn_gain, grad_normed_one)
    input_grad = grad_mid + through_one
    weight_parts = (grad_query, grad_key, grad_value, grad_output_t, grad_gate, grad_up, grad_down_t)
    widths = [part.shape[1] for part in weight_parts]
    gain_parts = (
        jnp.sum(attn_terms, axis=0),
        jnp.sum(query_terms, axis=(0, 1)),
        jnp.sum(key_terms, axis=(0, 1)),
        jnp.sum(ffn_terms, axis=0),
    )
    gain_sizes = [part.shape[0] for part in gain_parts]
    gain_flat = lax.psum(jnp.concatenate(gain_parts), "tp")
    gain_pad = -gain_flat.shape[0] % 1024
    summed, gains = ctx_sum(
        jnp.concatenate([part.astype(jnp.bfloat16) for part in weight_parts], axis=1),
        jnp.pad(gain_flat, (0, gain_pad)).reshape(8, -1),
        place_count,
        2,
    )
    summed = summed.astype(jnp.float32)
    gains = gains.reshape(-1)
    offsets = [sum(widths[:k]) for k in range(len(widths) + 1)]
    shared_query, shared_key, shared_value, output_t, shared_gate, shared_up, down_t = (
        summed[:, offsets[k] : offsets[k + 1]] for k in range(len(widths))
    )
    shared_output = output_t.T
    shared_down = down_t.T
    gain_attn = gains[: gain_sizes[0]]
    gain_query = gains[gain_sizes[0] : gain_sizes[0] + gain_sizes[1]]
    gain_key = gains[gain_sizes[0] + gain_sizes[1] : gain_sizes[0] + gain_sizes[1] + gain_sizes[2]]
    gain_ffn = gains[gain_sizes[0] + gain_sizes[1] + gain_sizes[2] : sum(gain_sizes)]
    return (
        block_output,
        input_grad,
        gain_attn,
        shared_query,
        shared_key,
        shared_value,
        gain_query,
        gain_key,
        shared_output,
        gain_ffn,
        shared_gate,
        shared_up,
        shared_down,
    )


def solution(mesh):
    return jax.shard_map(
        per_device,
        mesh=mesh,
        in_specs=(
            P(("ctx", "tp"), None),
            P(),
            P(),
            P(None, "tp"),
            P(None, "tp"),
            P(None, "tp"),
            P(),
            P(),
            P("tp", None),
            P(),
            P(None, "tp"),
            P(None, "tp"),
            P("tp", None),
            P(("ctx", "tp"), None),
        ),
        out_specs=(
            P(("ctx", "tp"), None),
            P(("ctx", "tp"), None),
            P(),
            P(None, "tp"),
            P(None, "tp"),
            P(None, "tp"),
            P(),
            P(),
            P("tp", None),
            P(),
            P(None, "tp"),
            P(None, "tp"),
            P("tp", None),
        ),
        check_vma=False,
    )
```

```python
import functools
import math

import jax
import jax.numpy as jnp
from jax import lax
from jax.experimental import pallas as pl
from jax.experimental.pallas import tpu as pltpu
from jax.sharding import PartitionSpec as P

MESH = pl.DeviceIdType.MESH
VMEM_LIMIT = 60 * 1024 * 1024


def _shifts(n):
    order = []
    for k in range(1, n // 2 + 1):
        order.append(k)
        if n - k != k:
            order.append(n - k)
    return order


def _place(axis, peer, other):
    return (peer, other) if axis == "ctx" else (other, peer)


def _enter(n, me, peer_axis, axis="ctx"):
    barrier = pltpu.get_barrier_semaphore()
    for k in _shifts(n):
        pl.semaphore_signal(
            barrier,
            1,
            device_id=_place(axis, lax.rem(me + k, n), peer_axis),
            device_id_type=MESH,
        )
    pl.semaphore_wait(barrier, n - 1)


def _gather_kernel(n, part_ref, out_ref, send_sem, recv_sem):
    me = lax.axis_index("ctx")
    other = lax.axis_index("tp")
    rows = part_ref.shape[0]
    _enter(n, me, other)
    copies = []
    for k in _shifts(n):
        copy = pltpu.make_async_remote_copy(
            src_ref=part_ref,
            dst_ref=out_ref.at[pl.ds(pl.multiple_of(me * rows, rows), rows)],
            send_sem=send_sem.at[k],
            recv_sem=recv_sem.at[k],
            device_id=(lax.rem(me + k, n), other),
            device_id_type=MESH,
        )
        copy.start()
        copies.append(copy)
    out_ref[pl.ds(pl.multiple_of(me * rows, rows), rows), :] = part_ref[...]
    for k in _shifts(n):
        source = lax.rem(me + n - k, n)
        pltpu.make_async_remote_copy(
            src_ref=part_ref,
            dst_ref=out_ref.at[pl.ds(pl.multiple_of(source * rows, rows), rows)],
            send_sem=send_sem.at[k],
            recv_sem=recv_sem.at[k],
            device_id=(source, other),
            device_id_type=MESH,
        ).wait_recv()
    for copy in copies:
        copy.wait_send()


def ctx_gather(part, n, collective_id):
    rows, cols = part.shape
    return pl.pallas_call(
        functools.partial(_gather_kernel, n),
        out_shape=jax.ShapeDtypeStruct((n * rows, cols), part.dtype),
        in_specs=[pl.BlockSpec(memory_space=pltpu.VMEM)],
        out_specs=pl.BlockSpec(memory_space=pltpu.VMEM),
        scratch_shapes=[pltpu.SemaphoreType.DMA((n,)), pltpu.SemaphoreType.DMA((n,))],
        compiler_params=pltpu.CompilerParams(
            collective_id=collective_id, has_side_effects=True, vmem_limit_bytes=VMEM_LIMIT
        ),
    )(part)


def _scatter_sum(n, me, other, whole_ref, held, send_sem, recv_sem, rows, axis="ctx"):
    copies = []
    for k in _shifts(n):
        target = lax.rem(me + k, n)
        copy = pltpu.make_async_remote_copy(
            src_ref=whole_ref.at[pl.ds(pl.multiple_of(target * rows, rows), rows)],
            dst_ref=held.at[k],
            send_sem=send_sem.at[k],
            recv_sem=recv_sem.at[k],
            device_id=_place(axis, target, other),
            device_id_type=MESH,
        )
        copy.start()
        copies.append(copy)
    total = whole_ref[pl.ds(pl.multiple_of(me * rows, rows), rows), :].astype(jnp.float32)
    for k in _shifts(n):
        source = lax.rem(me + n - k, n)
        pltpu.make_async_remote_copy(
            src_ref=whole_ref.at[pl.ds(0, rows)],
            dst_ref=held.at[k],
            send_sem=send_sem.at[k],
            recv_sem=recv_sem.at[k],
            device_id=_place(axis, source, other),
            device_id_type=MESH,
        ).wait_recv()
        total = total + held[k].astype(jnp.float32)
    for copy in copies:
        copy.wait_send()
    return total


def _scatter_kernel(n, axis, whole_ref, out_ref, held, send_sem, recv_sem):
    me = lax.axis_index(axis)
    other = lax.axis_index("tp" if axis == "ctx" else "ctx")
    rows = out_ref.shape[0]
    _enter(n, me, other, axis)
    out_ref[...] = _scatter_sum(n, me, other, whole_ref, held, send_sem, recv_sem, rows, axis)


def ctx_scatter(whole, n, collective_id, axis="ctx"):
    rows, cols = whole.shape[0] // n, whole.shape[1]
    return pl.pallas_call(
        functools.partial(_scatter_kernel, n, axis),
        out_shape=jax.ShapeDtypeStruct((rows, cols), jnp.float32),
        in_specs=[pl.BlockSpec(memory_space=pltpu.VMEM)],
        out_specs=pl.BlockSpec(memory_space=pltpu.VMEM),
        scratch_shapes=[
            pltpu.VMEM((n, rows, cols), whole.dtype),
            pltpu.SemaphoreType.DMA((n,)),
            pltpu.SemaphoreType.DMA((n,)),
        ],
        compiler_params=pltpu.CompilerParams(
            collective_id=collective_id, has_side_effects=True, vmem_limit_bytes=VMEM_LIMIT
        ),
    )(whole)


def _shift_at(n, step):
    half = step // 2 + 1
    return jnp.where(step % 2 == 0, half, n - half)


def _sum_kernel(n, spans, whole_ref, extra_ref, out_ref, extra_out, *scratch):
    pieces = len(spans)
    helds, mines, extra_held = scratch[:pieces], scratch[pieces : 2 * pieces], scratch[2 * pieces]
    sems = scratch[2 * pieces + 1 :]
    send_extra, recv_extra = sems[4 * pieces], sems[4 * pieces + 1]
    me = lax.axis_index("ctx")
    other = lax.axis_index("tp")
    rows = whole_ref.shape[0] // n
    own_rows = pl.ds(pl.multiple_of(me * rows, rows), rows)
    _enter(n, me, other)

    def extra_copy(k, peer):
        return pltpu.make_async_remote_copy(
            src_ref=extra_ref,
            dst_ref=extra_held.at[k],
            send_sem=send_extra.at[k],
            recv_sem=recv_extra.at[k],
            device_id=(peer, other),
            device_id_type=MESH,
        )

    def scatter_copy(piece, k, peer, block):
        first, width = spans[piece]
        return pltpu.make_async_remote_copy(
            src_ref=whole_ref.at[pl.ds(pl.multiple_of(block * rows, rows), rows), pl.ds(first, width)],
            dst_ref=helds[piece].at[k],
            send_sem=sems[4 * piece].at[k],
            recv_sem=sems[4 * piece + 1].at[k],
            device_id=(peer, other),
            device_id_type=MESH,
        )

    def gather_copy(piece, k, peer, block):
        first, width = spans[piece]
        return pltpu.make_async_remote_copy(
            src_ref=mines[piece],
            dst_ref=out_ref.at[pl.ds(pl.multiple_of(block * rows, rows), rows), pl.ds(first, width)],
            send_sem=sems[4 * piece + 2].at[k],
            recv_sem=sems[4 * piece + 3].at[k],
            device_id=(peer, other),
            device_id_type=MESH,
        )

    def each_peer(body):
        def step(index, carry):
            k = _shift_at(n, index)
            return body(k, lax.rem(me + k, n), lax.rem(me + n - k, n), carry)

        return lax.fori_loop(0, n - 1, step, 0)

    def start_extra(k, target, source, carry):
        extra_copy(k, target).start()
        return carry

    each_peer(start_extra)
    for piece in range(pieces):

        def start_scatter(k, target, source, carry, piece=piece):
            scatter_copy(piece, k, target, target).start()
            return carry

        each_peer(start_scatter)
    for piece, (first, width) in enumerate(spans):

        def add_block(index, total, piece=piece):
            k = _shift_at(n, index)
            scatter_copy(piece, k, lax.rem(me + n - k, n), me).wait_recv()
            return total + helds[piece][k].astype(jnp.float32)

        total = lax.fori_loop(
            0, n - 1, add_block, whole_ref[own_rows, pl.ds(first, width)].astype(jnp.float32)
        )
        mines[piece][...] = total.astype(mines[piece].dtype)

        def start_gather(k, target, source, carry, piece=piece):
            gather_copy(piece, k, target, me).start()
            return carry

        each_peer(start_gather)
        out_ref[own_rows, pl.ds(first, width)] = mines[piece][...]

    def add_extra(index, total):
        k = _shift_at(n, index)
        extra_copy(k, lax.rem(me + n - k, n)).wait_recv()
        return total + extra_held[k]

    extra_out[...] = lax.fori_loop(0, n - 1, add_extra, extra_ref[...])
    for piece in range(pieces):

        def finish(k, target, source, carry, piece=piece):
            gather_copy(piece, k, source, source).wait_recv()
            gather_copy(piece, k, target, me).wait_send()
            scatter_copy(piece, k, target, target).wait_send()
            return carry

        each_peer(finish)

    def finish_extra(k, target, source, carry):
        extra_copy(k, target).wait_send()
        return carry

    each_peer(finish_extra)


def ctx_sum(whole, extra, n, collective_id, pieces=8):
    rows, cols = whole.shape[0] // n, whole.shape[1]
    lanes = cols // 128
    edges = [128 * (lanes * p // pieces) for p in range(pieces + 1)]
    spans = tuple((edges[p], edges[p + 1] - edges[p]) for p in range(pieces))
    return pl.pallas_call(
        functools.partial(_sum_kernel, n, spans),
        out_shape=(
            jax.ShapeDtypeStruct(whole.shape, whole.dtype),
            jax.ShapeDtypeStruct(extra.shape, extra.dtype),
        ),
        in_specs=[pl.BlockSpec(memory_space=pltpu.VMEM)] * 2,
        out_specs=(pl.BlockSpec(memory_space=pltpu.VMEM),) * 2,
        scratch_shapes=[pltpu.VMEM((n, rows, width), whole.dtype) for _, width in spans]
        + [pltpu.VMEM((rows, width), whole.dtype) for _, width in spans]
        + [pltpu.VMEM((n,) + extra.shape, extra.dtype)]
        + [pltpu.SemaphoreType.DMA((n,))] * (4 * pieces + 2),
        compiler_params=pltpu.CompilerParams(
            collective_id=collective_id, has_side_effects=True, vmem_limit_bytes=VMEM_LIMIT
        ),
    )(whole, extra)


EPS = 1e-05
THETA = 1000000.0
NEGATIVE = -1e30


def rms_forward(values, norm_gain):
    inverse = lax.rsqrt(jnp.mean(values * values, axis=-1, keepdims=True) + EPS)
    return (values * inverse * norm_gain, inverse)


def rms_backward(values, inverse, norm_gain, upstream):
    scaled = upstream * norm_gain
    inner_mean = jnp.mean(scaled * values, axis=-1, keepdims=True)
    through = inverse * (scaled - values * inverse * inverse * inner_mean)
    return (through, upstream * values * inverse)


def rope_tables(positions, head_dim):
    halfway = head_dim // 2
    frequency = THETA ** (-(jnp.arange(halfway, dtype=jnp.float32) * 2.0 / head_dim))
    angles = positions.astype(jnp.float32)[:, None] * frequency[None, :]
    return (jnp.cos(angles)[:, None, :], jnp.sin(angles)[:, None, :])


def rope_apply(values, cosine, sine_table):
    halfway = values.shape[-1] // 2
    first_half = values[..., :halfway]
    second_half = values[..., halfway:]
    return jnp.concatenate(
        [
            first_half * cosine - second_half * sine_table,
            second_half * cosine + first_half * sine_table,
        ],
        axis=-1,
    )


def rope_back(upstream, cosine, sine_table):
    halfway = upstream.shape[-1] // 2
    first_half = upstream[..., :halfway]
    second_half = upstream[..., halfway:]
    return jnp.concatenate(
        [
            first_half * cosine + second_half * sine_table,
            second_half * cosine - first_half * sine_table,
        ],
        axis=-1,
    )


def row_places(block_map, holder, rows_total, place_count):
    piece_len = rows_total // 4
    within = jnp.arange(rows_total, dtype=jnp.int32)
    picked = jnp.sum(jnp.where(jnp.arange(place_count, dtype=jnp.int32) == holder, block_map, 0))
    later = within // piece_len % 2
    piece_index = jnp.where(later == 1, 2 * place_count - 1 - picked, picked)
    return piece_index * piece_len + within % piece_len


def span_places(block_map, first_anchor, shard_span, seq_rows, place_count):
    piece_len = seq_rows // 2
    anchors = first_anchor + jnp.arange(shard_span, dtype=jnp.int32)
    picked = jnp.sum(
        jnp.where(
            jnp.arange(place_count, dtype=jnp.int32)[None, :] == anchors[:, None],
            block_map[None, :],
            0,
        ),
        axis=1,
    )
    within = jnp.arange(seq_rows, dtype=jnp.int32)
    later = within // piece_len % 2
    piece_index = jnp.where(
        later[None, :] == 1, 2 * place_count - 1 - picked[:, None], picked[:, None]
    )
    return (piece_index * piece_len + (within % piece_len)[None, :]).reshape(shard_span * seq_rows)


def gather_rows(rows_low):
    return lax.all_gather(rows_low, "tp", axis=0, tiled=True)


def reduce_rows(partial_rows, collective_id):
    return ctx_scatter(
        partial_rows.astype(jnp.bfloat16), lax.axis_size("tp"), collective_id, "tp"
    )


def per_device(
    block_input,
    block_map,
    attn_gain,
    query_weight,
    key_weight,
    value_weight,
    query_gain,
    key_gain,
    output_weight,
    ffn_gain,
    gate_weight,
    up_weight,
    down_weight,
    cotangent,
):
    place_count = lax.axis_size("ctx")
    place_index = lax.axis_index("ctx")
    head_dim = query_gain.shape[0]
    query_heads = query_weight.shape[1] // head_dim
    kv_heads = key_weight.shape[1] // head_dim
    group_size = query_heads // kv_heads
    score_scale = 1.0 / math.sqrt(head_dim)
    shard_span = 4
    residual_in = block_input.astype(jnp.float32)
    normed_one, inverse_one = rms_forward(residual_in, attn_gain)
    rows_one = gather_rows(normed_one.astype(jnp.bfloat16))
    rows_total = rows_one.shape[0]
    seq_rows = rows_total // 2
    kv_width = kv_heads * head_dim
    own_places = row_places(block_map, place_index, rows_total, place_count)
    query_raw = jnp.dot(rows_one, query_weight, preferred_element_type=jnp.float32).reshape(
        rows_total, query_heads, head_dim
    )
    key_raw = jnp.dot(rows_one, key_weight, preferred_element_type=jnp.float32).reshape(
        rows_total, kv_heads, head_dim
    )
    values_own = jnp.dot(rows_one, value_weight, preferred_element_type=jnp.float32).astype(
        jnp.bfloat16
    )
    query_normed, query_inverse = rms_forward(query_raw, query_gain)
    key_normed, key_inverse = rms_forward(key_raw, key_gain)
    cosine, sine_table = rope_tables(own_places, head_dim)
    query_rot = rope_apply(query_normed, cosine, sine_table).astype(jnp.bfloat16)
    keys_own = (
        rope_apply(key_normed, cosine, sine_table)
        .astype(jnp.bfloat16)
        .reshape(rows_total, kv_width)
    )
    query_blocks = query_rot.reshape(2, seq_rows, kv_heads, group_size, head_dim)
    query_places = own_places[:seq_rows]

    whole_kv = ctx_gather(jnp.concatenate([keys_own, values_own], axis=1), place_count, 0)
    seq_kv = jnp.transpose(
        whole_kv.reshape(place_count, 2, seq_rows, 2 * kv_width), (1, 0, 2, 3)
    ).reshape(2, place_count * seq_rows, 2 * kv_width)
    key_heads = seq_kv[..., :kv_width].reshape(2, place_count * seq_rows, kv_heads, head_dim)
    value_heads = seq_kv[..., kv_width:].reshape(2, place_count * seq_rows, kv_heads, head_dim)
    key_places = span_places(block_map, 0, place_count, seq_rows, place_count)
    allowed = key_places[None, :] <= query_places[:, None]
    scores = (
        jnp.einsum(
            "sqhgd,skhd->shgqk", query_blocks, key_heads, preferred_element_type=jnp.float32
        )
        * score_scale
    )
    top = jnp.max(jnp.where(allowed, scores, NEGATIVE), axis=-1)
    weights = jnp.where(allowed, jnp.exp(scores - top[..., None]), 0.0)
    weight_total = jnp.sum(weights, axis=-1)
    weighted = jnp.einsum(
        "shgqk,skhd->shgqd",
        weights.astype(jnp.bfloat16),
        value_heads,
        preferred_element_type=jnp.float32,
    )
    log_total = top + jnp.log(weight_total)
    attn_rows = jnp.transpose(weighted / weight_total[..., None], (0, 3, 1, 2, 4))
    attn_low = attn_rows.reshape(rows_total, query_heads * head_dim).astype(jnp.bfloat16)
    residual_mid = residual_in + reduce_rows(
        jnp.dot(attn_low, output_weight, preferred_element_type=jnp.float32),
        3
    )
    normed_two, inverse_two = rms_forward(residual_mid, ffn_gain)
    rows_two = gather_rows(normed_two.astype(jnp.bfloat16))
    gate_pre = jnp.dot(rows_two, gate_weight, preferred_element_type=jnp.float32)
    up_pre = jnp.dot(rows_two, up_weight, preferred_element_type=jnp.float32)
    gate_sig = jax.nn.sigmoid(gate_pre)
    activated = (gate_pre * gate_sig * up_pre).astype(jnp.bfloat16)
    block_output = residual_mid + reduce_rows(
        jnp.dot(activated, down_weight, preferred_element_type=jnp.float32),
        4
    )
    grad_rows = gather_rows(cotangent)
    grad_down_t = jnp.dot(grad_rows.T, activated, preferred_element_type=jnp.float32)
    grad_act = jnp.dot(grad_rows, down_weight.T, preferred_element_type=jnp.float32)
    grad_gate_pre = (grad_act * up_pre * gate_sig * (1.0 + gate_pre * (1.0 - gate_sig))).astype(
        jnp.bfloat16
    )
    grad_up_pre = (grad_act * gate_pre * gate_sig).astype(jnp.bfloat16)
    grad_gate = jnp.dot(rows_two.T, grad_gate_pre, preferred_element_type=jnp.float32)
    grad_up = jnp.dot(rows_two.T, grad_up_pre, preferred_element_type=jnp.float32)
    grad_normed_two = reduce_rows(
        jnp.dot(grad_gate_pre, gate_weight.T, preferred_element_type=jnp.float32)
        + jnp.dot(grad_up_pre, up_weight.T, preferred_element_type=jnp.float32),
        5
    )
    through_two, ffn_terms = rms_backward(residual_mid, inverse_two, ffn_gain, grad_normed_two)
    grad_mid = cotangent.astype(jnp.float32) + through_two
    grad_mid_rows = gather_rows(grad_mid.astype(jnp.bfloat16))
    grad_output_t = jnp.dot(grad_mid_rows.T, attn_low, preferred_element_type=jnp.float32)
    grad_attn = jnp.dot(grad_mid_rows, output_weight.T, preferred_element_type=jnp.float32).astype(
        jnp.bfloat16
    )
    grad_attn_blocks = grad_attn.reshape(2, seq_rows, kv_heads, group_size, head_dim)
    delta_rows = jnp.sum(grad_attn_blocks.astype(jnp.float32) * attn_rows, axis=-1)
    delta_rows = jnp.transpose(delta_rows, (0, 2, 3, 1))

    probs = jnp.where(allowed, jnp.exp(scores - log_total[..., None]), 0.0)
    grad_value_seq = jnp.einsum(
        "shgqk,sqhgd->skhd",
        probs.astype(jnp.bfloat16),
        grad_attn_blocks,
        preferred_element_type=jnp.float32,
    )
    grad_probs = jnp.einsum(
        "sqhgd,skhd->shgqk", grad_attn_blocks, value_heads, preferred_element_type=jnp.float32
    )
    grad_scores = (score_scale * probs * (grad_probs - delta_rows[..., None])).astype(jnp.bfloat16)
    query_acc = jnp.einsum(
        "shgqk,skhd->sqhgd", grad_scores, key_heads, preferred_element_type=jnp.float32
    )
    grad_key_seq = jnp.einsum(
        "shgqk,sqhgd->skhd", grad_scores, query_blocks, preferred_element_type=jnp.float32
    )
    grad_kv_seq = jnp.concatenate(
        [
            grad_key_seq.reshape(2, place_count, seq_rows, kv_width),
            grad_value_seq.reshape(2, place_count, seq_rows, kv_width),
        ],
        axis=-1,
    )
    grad_kv_all = jnp.transpose(grad_kv_seq, (1, 0, 2, 3)).reshape(
        place_count * rows_total, 2 * kv_width
    )
    grad_kv_flat = ctx_scatter(
        grad_kv_all.astype(jnp.bfloat16),
        place_count,
        1,
    )
    grad_keys_flat, grad_values_flat = grad_kv_flat[:, :kv_width], grad_kv_flat[:, kv_width:]
    grad_query_rot = query_acc.reshape(rows_total, query_heads, head_dim)
    grad_key_rot = grad_keys_flat.reshape(rows_total, kv_heads, head_dim)
    grad_query_raw, query_terms = rms_backward(
        query_raw, query_inverse, query_gain, rope_back(grad_query_rot, cosine, sine_table)
    )
    grad_key_raw, key_terms = rms_backward(
        key_raw, key_inverse, key_gain, rope_back(grad_key_rot, cosine, sine_table)
    )
    grad_query_low = grad_query_raw.reshape(rows_total, query_heads * head_dim).astype(jnp.bfloat16)
    grad_key_low = grad_key_raw.reshape(rows_total, kv_width).astype(jnp.bfloat16)
    grad_value_low = grad_values_flat.astype(jnp.bfloat16)
    grad_query = jnp.dot(rows_one.T, grad_query_low, preferred_element_type=jnp.float32)
    grad_key = jnp.dot(rows_one.T, grad_key_low, preferred_element_type=jnp.float32)
    grad_value = jnp.dot(rows_one.T, grad_value_low, preferred_element_type=jnp.float32)
    grad_normed_one = reduce_rows(
        jnp.dot(grad_query_low, query_weight.T, preferred_element_type=jnp.float32)
        + jnp.dot(grad_key_low, key_weight.T, preferred_element_type=jnp.float32)
        + jnp.dot(grad_value_low, value_weight.T, preferred_element_type=jnp.float32),
        6
    )
    through_one, attn_terms = rms_backward(residual_in, inverse_one, attn_gain, grad_normed_one)
    input_grad = grad_mid + through_one
    weight_parts = (grad_query, grad_key, grad_value, grad_output_t, grad_gate, grad_up, grad_down_t)
    widths = [part.shape[1] for part in weight_parts]
    gain_parts = (
        jnp.sum(attn_terms, axis=0),
        jnp.sum(query_terms, axis=(0, 1)),
        jnp.sum(key_terms, axis=(0, 1)),
        jnp.sum(ffn_terms, axis=0),
    )
    gain_sizes = [part.shape[0] for part in gain_parts]
    gain_flat = lax.psum(jnp.concatenate(gain_parts), "tp")
    gain_pad = -gain_flat.shape[0] % 1024
    summed, gains = ctx_sum(
        jnp.concatenate([part.astype(jnp.bfloat16) for part in weight_parts], axis=1),
        jnp.pad(gain_flat, (0, gain_pad)).reshape(8, -1),
        place_count,
        2,
    )
    summed = summed.astype(jnp.float32)
    gains = gains.reshape(-1)
    offsets = [sum(widths[:k]) for k in range(len(widths) + 1)]
    shared_query, shared_key, shared_value, output_t, shared_gate, shared_up, down_t = (
        summed[:, offsets[k] : offsets[k + 1]] for k in range(len(widths))
    )
    shared_output = output_t.T
    shared_down = down_t.T
    gain_attn = gains[: gain_sizes[0]]
    gain_query = gains[gain_sizes[0] : gain_sizes[0] + gain_sizes[1]]
    gain_key = gains[gain_sizes[0] + gain_sizes[1] : gain_sizes[0] + gain_sizes[1] + gain_sizes[2]]
    gain_ffn = gains[gain_sizes[0] + gain_sizes[1] + gain_sizes[2] : sum(gain_sizes)]
    return (
        block_output,
        input_grad,
        gain_attn,
        shared_query,
        shared_key,
        shared_value,
        gain_query,
        gain_key,
        shared_output,
        gain_ffn,
        shared_gate,
        shared_up,
        shared_down,
    )


def solution(mesh):
    return jax.shard_map(
        per_device,
        mesh=mesh,
        in_specs=(
            P(("ctx", "tp"), None),
            P(),
            P(),
            P(None, "tp"),
            P(None, "tp"),
            P(None, "tp"),
            P(),
            P(),
            P("tp", None),
            P(),
            P(None, "tp"),
            P(None, "tp"),
            P("tp", None),
            P(("ctx", "tp"), None),
        ),
        out_specs=(
            P(("ctx", "tp"), None),
            P(("ctx", "tp"), None),
            P(),
            P(None, "tp"),
            P(None, "tp"),
            P(None, "tp"),
            P(),
            P(),
            P("tp", None),
            P(),
            P(None, "tp"),
            P(None, "tp"),
            P("tp", None),
        ),
        check_vma=False,
    )
```

```python
import functools
import math

import jax
import jax.numpy as jnp
from jax import lax
from jax.experimental import pallas as pl
from jax.experimental.pallas import tpu as pltpu
from jax.sharding import PartitionSpec as P

MESH = pl.DeviceIdType.MESH
VMEM_LIMIT = 60 * 1024 * 1024


def _shifts(n):
    order = []
    for k in range(1, n // 2 + 1):
        order.append(k)
        if n - k != k:
            order.append(n - k)
    return order


def _place(axis, peer, other):
    return (peer, other) if axis == "ctx" else (other, peer)


def _enter(n, me, peer_axis, axis="ctx"):
    barrier = pltpu.get_barrier_semaphore()
    for k in _shifts(n):
        pl.semaphore_signal(
            barrier,
            1,
            device_id=_place(axis, lax.rem(me + k, n), peer_axis),
            device_id_type=MESH,
        )
    pl.semaphore_wait(barrier, n - 1)


def _gather_kernel(n, part_ref, out_ref, send_sem, recv_sem):
    me = lax.axis_index("ctx")
    other = lax.axis_index("tp")
    rows = part_ref.shape[0]
    _enter(n, me, other)
    copies = []
    for k in _shifts(n):
        copy = pltpu.make_async_remote_copy(
            src_ref=part_ref,
            dst_ref=out_ref.at[pl.ds(pl.multiple_of(me * rows, rows), rows)],
            send_sem=send_sem.at[k],
            recv_sem=recv_sem.at[k],
            device_id=(lax.rem(me + k, n), other),
            device_id_type=MESH,
        )
        copy.start()
        copies.append(copy)
    out_ref[pl.ds(pl.multiple_of(me * rows, rows), rows), :] = part_ref[...]
    for k in _shifts(n):
        source = lax.rem(me + n - k, n)
        pltpu.make_async_remote_copy(
            src_ref=part_ref,
            dst_ref=out_ref.at[pl.ds(pl.multiple_of(source * rows, rows), rows)],
            send_sem=send_sem.at[k],
            recv_sem=recv_sem.at[k],
            device_id=(source, other),
            device_id_type=MESH,
        ).wait_recv()
    for copy in copies:
        copy.wait_send()


def ctx_gather(part, n, collective_id):
    rows, cols = part.shape
    return pl.pallas_call(
        functools.partial(_gather_kernel, n),
        out_shape=jax.ShapeDtypeStruct((n * rows, cols), part.dtype),
        in_specs=[pl.BlockSpec(memory_space=pltpu.VMEM)],
        out_specs=pl.BlockSpec(memory_space=pltpu.VMEM),
        scratch_shapes=[pltpu.SemaphoreType.DMA((n,)), pltpu.SemaphoreType.DMA((n,))],
        compiler_params=pltpu.CompilerParams(
            collective_id=collective_id, has_side_effects=True, vmem_limit_bytes=VMEM_LIMIT
        ),
    )(part)


def _scatter_sum(n, me, other, whole_ref, held, send_sem, recv_sem, rows, axis="ctx"):
    copies = []
    for k in _shifts(n):
        target = lax.rem(me + k, n)
        copy = pltpu.make_async_remote_copy(
            src_ref=whole_ref.at[pl.ds(pl.multiple_of(target * rows, rows), rows)],
            dst_ref=held.at[k],
            send_sem=send_sem.at[k],
            recv_sem=recv_sem.at[k],
            device_id=_place(axis, target, other),
            device_id_type=MESH,
        )
        copy.start()
        copies.append(copy)
    total = whole_ref[pl.ds(pl.multiple_of(me * rows, rows), rows), :].astype(jnp.float32)
    for k in _shifts(n):
        source = lax.rem(me + n - k, n)
        pltpu.make_async_remote_copy(
            src_ref=whole_ref.at[pl.ds(0, rows)],
            dst_ref=held.at[k],
            send_sem=send_sem.at[k],
            recv_sem=recv_sem.at[k],
            device_id=_place(axis, source, other),
            device_id_type=MESH,
        ).wait_recv()
        total = total + held[k].astype(jnp.float32)
    for copy in copies:
        copy.wait_send()
    return total


def _scatter_kernel(n, axis, whole_ref, out_ref, held, send_sem, recv_sem):
    me = lax.axis_index(axis)
    other = lax.axis_index("tp" if axis == "ctx" else "ctx")
    rows = out_ref.shape[0]
    _enter(n, me, other, axis)
    out_ref[...] = _scatter_sum(n, me, other, whole_ref, held, send_sem, recv_sem, rows, axis)


def ctx_scatter(whole, n, collective_id, axis="ctx"):
    rows, cols = whole.shape[0] // n, whole.shape[1]
    return pl.pallas_call(
        functools.partial(_scatter_kernel, n, axis),
        out_shape=jax.ShapeDtypeStruct((rows, cols), jnp.float32),
        in_specs=[pl.BlockSpec(memory_space=pltpu.VMEM)],
        out_specs=pl.BlockSpec(memory_space=pltpu.VMEM),
        scratch_shapes=[
            pltpu.VMEM((n, rows, cols), whole.dtype),
            pltpu.SemaphoreType.DMA((n,)),
            pltpu.SemaphoreType.DMA((n,)),
        ],
        compiler_params=pltpu.CompilerParams(
            collective_id=collective_id, has_side_effects=True, vmem_limit_bytes=VMEM_LIMIT
        ),
    )(whole)


def _shift_at(n, step):
    half = step // 2 + 1
    return jnp.where(step % 2 == 0, half, n - half)


def _sum_kernel(n, spans, whole_ref, extra_ref, out_ref, extra_out, *scratch):
    pieces = len(spans)
    helds, mines, extra_held = scratch[:pieces], scratch[pieces : 2 * pieces], scratch[2 * pieces]
    sems = scratch[2 * pieces + 1 :]
    send_extra, recv_extra = sems[4 * pieces], sems[4 * pieces + 1]
    me = lax.axis_index("ctx")
    other = lax.axis_index("tp")
    rows = whole_ref.shape[0] // n
    own_rows = pl.ds(pl.multiple_of(me * rows, rows), rows)
    _enter(n, me, other)

    def extra_copy(k, peer):
        return pltpu.make_async_remote_copy(
            src_ref=extra_ref,
            dst_ref=extra_held.at[k],
            send_sem=send_extra.at[k],
            recv_sem=recv_extra.at[k],
            device_id=(peer, other),
            device_id_type=MESH,
        )

    def scatter_copy(piece, k, peer, block):
        first, width = spans[piece]
        return pltpu.make_async_remote_copy(
            src_ref=whole_ref.at[pl.ds(pl.multiple_of(block * rows, rows), rows), pl.ds(first, width)],
            dst_ref=helds[piece].at[k],
            send_sem=sems[4 * piece].at[k],
            recv_sem=sems[4 * piece + 1].at[k],
            device_id=(peer, other),
            device_id_type=MESH,
        )

    def gather_copy(piece, k, peer, block):
        first, width = spans[piece]
        return pltpu.make_async_remote_copy(
            src_ref=mines[piece],
            dst_ref=out_ref.at[pl.ds(pl.multiple_of(block * rows, rows), rows), pl.ds(first, width)],
            send_sem=sems[4 * piece + 2].at[k],
            recv_sem=sems[4 * piece + 3].at[k],
            device_id=(peer, other),
            device_id_type=MESH,
        )

    def each_peer(body):
        def step(index, carry):
            k = _shift_at(n, index)
            return body(k, lax.rem(me + k, n), lax.rem(me + n - k, n), carry)

        return lax.fori_loop(0, n - 1, step, 0)

    def start_extra(k, target, source, carry):
        extra_copy(k, target).start()
        return carry

    each_peer(start_extra)
    for piece in range(pieces):

        def start_scatter(k, target, source, carry, piece=piece):
            scatter_copy(piece, k, target, target).start()
            return carry

        each_peer(start_scatter)
    for piece, (first, width) in enumerate(spans):

        def add_block(index, total, piece=piece):
            k = _shift_at(n, index)
            scatter_copy(piece, k, lax.rem(me + n - k, n), me).wait_recv()
            return total + helds[piece][k].astype(jnp.float32)

        total = lax.fori_loop(
            0, n - 1, add_block, whole_ref[own_rows, pl.ds(first, width)].astype(jnp.float32)
        )
        mines[piece][...] = total.astype(mines[piece].dtype)

        def start_gather(k, target, source, carry, piece=piece):
            gather_copy(piece, k, target, me).start()
            return carry

        each_peer(start_gather)
        out_ref[own_rows, pl.ds(first, width)] = mines[piece][...]

    def add_extra(index, total):
        k = _shift_at(n, index)
        extra_copy(k, lax.rem(me + n - k, n)).wait_recv()
        return total + extra_held[k]

    extra_out[...] = lax.fori_loop(0, n - 1, add_extra, extra_ref[...])
    for piece in range(pieces):

        def finish(k, target, source, carry, piece=piece):
            gather_copy(piece, k, source, source).wait_recv()
            gather_copy(piece, k, target, me).wait_send()
            scatter_copy(piece, k, target, target).wait_send()
            return carry

        each_peer(finish)

    def finish_extra(k, target, source, carry):
        extra_copy(k, target).wait_send()
        return carry

    each_peer(finish_extra)


def ctx_sum(whole, extra, n, collective_id, pieces=8):
    rows, cols = whole.shape[0] // n, whole.shape[1]
    lanes = cols // 128
    edges = [128 * (lanes * p // pieces) for p in range(pieces + 1)]
    spans = tuple((edges[p], edges[p + 1] - edges[p]) for p in range(pieces))
    return pl.pallas_call(
        functools.partial(_sum_kernel, n, spans),
        out_shape=(
            jax.ShapeDtypeStruct(whole.shape, whole.dtype),
            jax.ShapeDtypeStruct(extra.shape, extra.dtype),
        ),
        in_specs=[pl.BlockSpec(memory_space=pltpu.VMEM)] * 2,
        out_specs=(pl.BlockSpec(memory_space=pltpu.VMEM),) * 2,
        scratch_shapes=[pltpu.VMEM((n, rows, width), whole.dtype) for _, width in spans]
        + [pltpu.VMEM((rows, width), whole.dtype) for _, width in spans]
        + [pltpu.VMEM((n,) + extra.shape, extra.dtype)]
        + [pltpu.SemaphoreType.DMA((n,))] * (4 * pieces + 2),
        compiler_params=pltpu.CompilerParams(
            collective_id=collective_id, has_side_effects=True, vmem_limit_bytes=VMEM_LIMIT
        ),
    )(whole, extra)


EPS = 1e-05
THETA = 1000000.0
NEGATIVE = -1e30


def rms_forward(values, norm_gain):
    inverse = lax.rsqrt(jnp.mean(values * values, axis=-1, keepdims=True) + EPS)
    return (values * inverse * norm_gain, inverse)


def rms_backward(values, inverse, norm_gain, upstream):
    scaled = upstream * norm_gain
    inner_mean = jnp.mean(scaled * values, axis=-1, keepdims=True)
    through = inverse * (scaled - values * inverse * inverse * inner_mean)
    return (through, upstream * values * inverse)


def rope_tables(positions, head_dim):
    halfway = head_dim // 2
    frequency = THETA ** (-(jnp.arange(halfway, dtype=jnp.float32) * 2.0 / head_dim))
    angles = positions.astype(jnp.float32)[:, None] * frequency[None, :]
    return (jnp.cos(angles)[:, None, :], jnp.sin(angles)[:, None, :])


def rope_apply(values, cosine, sine_table):
    halfway = values.shape[-1] // 2
    first_half = values[..., :halfway]
    second_half = values[..., halfway:]
    return jnp.concatenate(
        [
            first_half * cosine - second_half * sine_table,
            second_half * cosine + first_half * sine_table,
        ],
        axis=-1,
    )


def rope_back(upstream, cosine, sine_table):
    halfway = upstream.shape[-1] // 2
    first_half = upstream[..., :halfway]
    second_half = upstream[..., halfway:]
    return jnp.concatenate(
        [
            first_half * cosine + second_half * sine_table,
            second_half * cosine - first_half * sine_table,
        ],
        axis=-1,
    )


def row_places(block_map, holder, rows_total, place_count):
    piece_len = rows_total // 4
    within = jnp.arange(rows_total, dtype=jnp.int32)
    picked = jnp.sum(jnp.where(jnp.arange(place_count, dtype=jnp.int32) == holder, block_map, 0))
    later = within // piece_len % 2
    piece_index = jnp.where(later == 1, 2 * place_count - 1 - picked, picked)
    return piece_index * piece_len + within % piece_len


def span_places(block_map, first_anchor, shard_span, seq_rows, place_count):
    piece_len = seq_rows // 2
    anchors = first_anchor + jnp.arange(shard_span, dtype=jnp.int32)
    picked = jnp.sum(
        jnp.where(
            jnp.arange(place_count, dtype=jnp.int32)[None, :] == anchors[:, None],
            block_map[None, :],
            0,
        ),
        axis=1,
    )
    within = jnp.arange(seq_rows, dtype=jnp.int32)
    later = within // piece_len % 2
    piece_index = jnp.where(
        later[None, :] == 1, 2 * place_count - 1 - picked[:, None], picked[:, None]
    )
    return (piece_index * piece_len + (within % piece_len)[None, :]).reshape(shard_span * seq_rows)


def gather_rows(rows_low):
    return lax.all_gather(rows_low, "tp", axis=0, tiled=True)


def reduce_rows(partial_rows, collective_id):
    return ctx_scatter(
        partial_rows.astype(jnp.bfloat16), lax.axis_size("tp"), collective_id, "tp"
    )


def per_device(
    block_input,
    block_map,
    attn_gain,
    query_weight,
    key_weight,
    value_weight,
    query_gain,
    key_gain,
    output_weight,
    ffn_gain,
    gate_weight,
    up_weight,
    down_weight,
    cotangent,
):
    place_count = lax.axis_size("ctx")
    place_index = lax.axis_index("ctx")
    head_dim = query_gain.shape[0]
    query_heads = query_weight.shape[1] // head_dim
    kv_heads = key_weight.shape[1] // head_dim
    group_size = query_heads // kv_heads
    score_scale = 1.0 / math.sqrt(head_dim)
    shard_span = 4
    residual_in = block_input.astype(jnp.float32)
    normed_one, inverse_one = rms_forward(residual_in, attn_gain)
    rows_one = gather_rows(normed_one.astype(jnp.bfloat16))
    rows_total = rows_one.shape[0]
    seq_rows = rows_total // 2
    kv_width = kv_heads * head_dim
    own_places = row_places(block_map, place_index, rows_total, place_count)
    query_raw = jnp.dot(rows_one, query_weight, preferred_element_type=jnp.float32).reshape(
        rows_total, query_heads, head_dim
    )
    key_raw = jnp.dot(rows_one, key_weight, preferred_element_type=jnp.float32).reshape(
        rows_total, kv_heads, head_dim
    )
    values_own = jnp.dot(rows_one, value_weight, preferred_element_type=jnp.float32).astype(
        jnp.bfloat16
    )
    query_normed, query_inverse = rms_forward(query_raw, query_gain)
    key_normed, key_inverse = rms_forward(key_raw, key_gain)
    cosine, sine_table = rope_tables(own_places, head_dim)
    query_rot = rope_apply(query_normed, cosine, sine_table).astype(jnp.bfloat16)
    keys_own = (
        rope_apply(key_normed, cosine, sine_table)
        .astype(jnp.bfloat16)
        .reshape(rows_total, kv_width)
    )
    query_blocks = query_rot.reshape(2, seq_rows, kv_heads, group_size, head_dim)
    query_places = own_places[:seq_rows]

    whole_kv = ctx_gather(jnp.concatenate([keys_own, values_own], axis=1), place_count, 0)
    seq_kv = jnp.transpose(
        whole_kv.reshape(place_count, 2, seq_rows, 2 * kv_width), (1, 0, 2, 3)
    ).reshape(2, place_count * seq_rows, 2 * kv_width)
    key_heads = seq_kv[..., :kv_width].reshape(2, place_count * seq_rows, kv_heads, head_dim)
    value_heads = seq_kv[..., kv_width:].reshape(2, place_count * seq_rows, kv_heads, head_dim)
    key_places = span_places(block_map, 0, place_count, seq_rows, place_count)
    allowed = key_places[None, :] <= query_places[:, None]
    scores = (
        jnp.einsum(
            "sqhgd,skhd->shgqk", query_blocks, key_heads, preferred_element_type=jnp.float32
        )
        * score_scale
    )
    top = jnp.max(jnp.where(allowed, scores, NEGATIVE), axis=-1)
    weights = jnp.where(allowed, jnp.exp(scores - top[..., None]), 0.0)
    weight_total = jnp.sum(weights, axis=-1)
    weighted = jnp.einsum(
        "shgqk,skhd->shgqd",
        weights.astype(jnp.bfloat16),
        value_heads,
        preferred_element_type=jnp.float32,
    )
    log_total = top + jnp.log(weight_total)
    attn_rows = jnp.transpose(weighted / weight_total[..., None], (0, 3, 1, 2, 4))
    attn_low = attn_rows.reshape(rows_total, query_heads * head_dim).astype(jnp.bfloat16)
    residual_mid = residual_in + reduce_rows(
        jnp.dot(attn_low, output_weight, preferred_element_type=jnp.float32),
        3
    )
    normed_two, inverse_two = rms_forward(residual_mid, ffn_gain)
    rows_two = gather_rows(normed_two.astype(jnp.bfloat16))
    gate_pre = jnp.dot(rows_two, gate_weight, preferred_element_type=jnp.float32)
    up_pre = jnp.dot(rows_two, up_weight, preferred_element_type=jnp.float32)
    gate_sig = jax.nn.sigmoid(gate_pre)
    activated = (gate_pre * gate_sig * up_pre).astype(jnp.bfloat16)
    block_output = residual_mid + reduce_rows(
        jnp.dot(activated, down_weight, preferred_element_type=jnp.float32),
        4
    )
    grad_rows = gather_rows(cotangent)
    grad_down_t = jnp.dot(grad_rows.T, activated, preferred_element_type=jnp.float32)
    grad_act = jnp.dot(grad_rows, down_weight.T, preferred_element_type=jnp.float32)
    grad_gate_pre = (grad_act * up_pre * gate_sig * (1.0 + gate_pre * (1.0 - gate_sig))).astype(
        jnp.bfloat16
    )
    grad_up_pre = (grad_act * gate_pre * gate_sig).astype(jnp.bfloat16)
    grad_gate = jnp.dot(rows_two.T, grad_gate_pre, preferred_element_type=jnp.float32)
    grad_up = jnp.dot(rows_two.T, grad_up_pre, preferred_element_type=jnp.float32)
    grad_normed_two = reduce_rows(
        jnp.dot(grad_gate_pre, gate_weight.T, preferred_element_type=jnp.float32)
        + jnp.dot(grad_up_pre, up_weight.T, preferred_element_type=jnp.float32),
        5
    )
    through_two, ffn_terms = rms_backward(residual_mid, inverse_two, ffn_gain, grad_normed_two)
    grad_mid = cotangent.astype(jnp.float32) + through_two
    grad_mid_rows = gather_rows(grad_mid.astype(jnp.bfloat16))
    grad_output_t = jnp.dot(grad_mid_rows.T, attn_low, preferred_element_type=jnp.float32)
    grad_attn = jnp.dot(grad_mid_rows, output_weight.T, preferred_element_type=jnp.float32).astype(
        jnp.bfloat16
    )
    grad_attn_blocks = grad_attn.reshape(2, seq_rows, kv_heads, group_size, head_dim)
    delta_rows = jnp.sum(grad_attn_blocks.astype(jnp.float32) * attn_rows, axis=-1)
    delta_rows = jnp.transpose(delta_rows, (0, 2, 3, 1))

    probs = jnp.where(allowed, jnp.exp(scores - log_total[..., None]), 0.0)
    grad_value_seq = jnp.einsum(
        "shgqk,sqhgd->skhd",
        probs.astype(jnp.bfloat16),
        grad_attn_blocks,
        preferred_element_type=jnp.float32,
    )
    grad_probs = jnp.einsum(
        "sqhgd,skhd->shgqk", grad_attn_blocks, value_heads, preferred_element_type=jnp.float32
    )
    grad_scores = (score_scale * probs * (grad_probs - delta_rows[..., None])).astype(jnp.bfloat16)
    query_acc = jnp.einsum(
        "shgqk,skhd->sqhgd", grad_scores, key_heads, preferred_element_type=jnp.float32
    )
    grad_key_seq = jnp.einsum(
        "shgqk,sqhgd->skhd", grad_scores, query_blocks, preferred_element_type=jnp.float32
    )
    grad_kv_seq = jnp.concatenate(
        [
            grad_key_seq.reshape(2, place_count, seq_rows, kv_width),
            grad_value_seq.reshape(2, place_count, seq_rows, kv_width),
        ],
        axis=-1,
    )
    grad_kv_all = jnp.transpose(grad_kv_seq, (1, 0, 2, 3)).reshape(
        place_count * rows_total, 2 * kv_width
    )
    grad_kv_flat = ctx_scatter(
        grad_kv_all.astype(jnp.bfloat16),
        place_count,
        1,
    )
    grad_keys_flat, grad_values_flat = grad_kv_flat[:, :kv_width], grad_kv_flat[:, kv_width:]
    grad_query_rot = query_acc.reshape(rows_total, query_heads, head_dim)
    grad_key_rot = grad_keys_flat.reshape(rows_total, kv_heads, head_dim)
    grad_query_raw, query_terms = rms_backward(
        query_raw, query_inverse, query_gain, rope_back(grad_query_rot, cosine, sine_table)
    )
    grad_key_raw, key_terms = rms_backward(
        key_raw, key_inverse, key_gain, rope_back(grad_key_rot, cosine, sine_table)
    )
    grad_query_low = grad_query_raw.reshape(rows_total, query_heads * head_dim).astype(jnp.bfloat16)
    grad_key_low = grad_key_raw.reshape(rows_total, kv_width).astype(jnp.bfloat16)
    grad_value_low = grad_values_flat.astype(jnp.bfloat16)
    grad_query = jnp.dot(rows_one.T, grad_query_low, preferred_element_type=jnp.float32)
    grad_key = jnp.dot(rows_one.T, grad_key_low, preferred_element_type=jnp.float32)
    grad_value = jnp.dot(rows_one.T, grad_value_low, preferred_element_type=jnp.float32)
    grad_normed_one = reduce_rows(
        jnp.dot(grad_query_low, query_weight.T, preferred_element_type=jnp.float32)
        + jnp.dot(grad_key_low, key_weight.T, preferred_element_type=jnp.float32)
        + jnp.dot(grad_value_low, value_weight.T, preferred_element_type=jnp.float32),
        6
    )
    through_one, attn_terms = rms_backward(residual_in, inverse_one, attn_gain, grad_normed_one)
    input_grad = grad_mid + through_one
    weight_parts = (grad_query, grad_key, grad_value, grad_output_t, grad_gate, grad_up, grad_down_t)
    widths = [part.shape[1] for part in weight_parts]
    gain_parts = (
        jnp.sum(attn_terms, axis=0),
        jnp.sum(query_terms, axis=(0, 1)),
        jnp.sum(key_terms, axis=(0, 1)),
        jnp.sum(ffn_terms, axis=0),
    )
    gain_sizes = [part.shape[0] for part in gain_parts]
    gain_local = jnp.concatenate(gain_parts)
    gain_pad = -gain_local.shape[0] % 1024
    tp_count = lax.axis_size("tp")
    gain_flat = ctx_scatter(
        jnp.tile(jnp.pad(gain_local, (0, gain_pad)).reshape(8, -1), (tp_count, 1)),
        tp_count,
        7,
        "tp",
    ).reshape(-1)[: gain_local.shape[0]]
    summed, gains = ctx_sum(
        jnp.concatenate([part.astype(jnp.bfloat16) for part in weight_parts], axis=1),
        jnp.pad(gain_flat, (0, gain_pad)).reshape(8, -1),
        place_count,
        2,
    )
    summed = summed.astype(jnp.float32)
    gains = gains.reshape(-1)
    offsets = [sum(widths[:k]) for k in range(len(widths) + 1)]
    shared_query, shared_key, shared_value, output_t, shared_gate, shared_up, down_t = (
        summed[:, offsets[k] : offsets[k + 1]] for k in range(len(widths))
    )
    shared_output = output_t.T
    shared_down = down_t.T
    gain_attn = gains[: gain_sizes[0]]
    gain_query = gains[gain_sizes[0] : gain_sizes[0] + gain_sizes[1]]
    gain_key = gains[gain_sizes[0] + gain_sizes[1] : gain_sizes[0] + gain_sizes[1] + gain_sizes[2]]
    gain_ffn = gains[gain_sizes[0] + gain_sizes[1] + gain_sizes[2] : sum(gain_sizes)]
    return (
        block_output,
        input_grad,
        gain_attn,
        shared_query,
        shared_key,
        shared_value,
        gain_query,
        gain_key,
        shared_output,
        gain_ffn,
        shared_gate,
        shared_up,
        shared_down,
    )


def solution(mesh):
    return jax.shard_map(
        per_device,
        mesh=mesh,
        in_specs=(
            P(("ctx", "tp"), None),
            P(),
            P(),
            P(None, "tp"),
            P(None, "tp"),
            P(None, "tp"),
            P(),
            P(),
            P("tp", None),
            P(),
            P(None, "tp"),
            P(None, "tp"),
            P("tp", None),
            P(("ctx", "tp"), None),
        ),
        out_specs=(
            P(("ctx", "tp"), None),
            P(("ctx", "tp"), None),
            P(),
            P(None, "tp"),
            P(None, "tp"),
            P(None, "tp"),
            P(),
            P(),
            P("tp", None),
            P(),
            P(None, "tp"),
            P(None, "tp"),
            P("tp", None),
        ),
        check_vma=False,
    )
```

```python
import functools
import math

import jax
import jax.numpy as jnp
from jax import lax
from jax.experimental import pallas as pl
from jax.experimental.pallas import tpu as pltpu
from jax.sharding import PartitionSpec as P

MESH = pl.DeviceIdType.MESH
VMEM_LIMIT = 60 * 1024 * 1024


def _shifts(n):
    order = []
    for k in range(1, n // 2 + 1):
        order.append(k)
        if n - k != k:
            order.append(n - k)
    return order


def _place(axis, peer, other):
    return (peer, other) if axis == "ctx" else (other, peer)


def _enter(n, me, peer_axis, axis="ctx"):
    barrier = pltpu.get_barrier_semaphore()
    for k in _shifts(n):
        pl.semaphore_signal(
            barrier,
            1,
            device_id=_place(axis, lax.rem(me + k, n), peer_axis),
            device_id_type=MESH,
        )
    pl.semaphore_wait(barrier, n - 1)


def _gather_kernel(n, part_ref, out_ref, send_sem, recv_sem):
    me = lax.axis_index("ctx")
    other = lax.axis_index("tp")
    rows = part_ref.shape[0]
    _enter(n, me, other)
    copies = []
    for k in _shifts(n):
        copy = pltpu.make_async_remote_copy(
            src_ref=part_ref,
            dst_ref=out_ref.at[pl.ds(pl.multiple_of(me * rows, rows), rows)],
            send_sem=send_sem.at[k],
            recv_sem=recv_sem.at[k],
            device_id=(lax.rem(me + k, n), other),
            device_id_type=MESH,
        )
        copy.start()
        copies.append(copy)
    out_ref[pl.ds(pl.multiple_of(me * rows, rows), rows), :] = part_ref[...]
    for k in _shifts(n):
        source = lax.rem(me + n - k, n)
        pltpu.make_async_remote_copy(
            src_ref=part_ref,
            dst_ref=out_ref.at[pl.ds(pl.multiple_of(source * rows, rows), rows)],
            send_sem=send_sem.at[k],
            recv_sem=recv_sem.at[k],
            device_id=(source, other),
            device_id_type=MESH,
        ).wait_recv()
    for copy in copies:
        copy.wait_send()


def ctx_gather(part, n, collective_id):
    rows, cols = part.shape
    return pl.pallas_call(
        functools.partial(_gather_kernel, n),
        out_shape=jax.ShapeDtypeStruct((n * rows, cols), part.dtype),
        in_specs=[pl.BlockSpec(memory_space=pltpu.VMEM)],
        out_specs=pl.BlockSpec(memory_space=pltpu.VMEM),
        scratch_shapes=[pltpu.SemaphoreType.DMA((n,)), pltpu.SemaphoreType.DMA((n,))],
        compiler_params=pltpu.CompilerParams(
            collective_id=collective_id, has_side_effects=True, vmem_limit_bytes=VMEM_LIMIT
        ),
    )(part)


def _scatter_sum(n, me, other, whole_ref, held, send_sem, recv_sem, rows, axis="ctx"):
    copies = []
    for k in _shifts(n):
        target = lax.rem(me + k, n)
        copy = pltpu.make_async_remote_copy(
            src_ref=whole_ref.at[pl.ds(pl.multiple_of(target * rows, rows), rows)],
            dst_ref=held.at[k],
            send_sem=send_sem.at[k],
            recv_sem=recv_sem.at[k],
            device_id=_place(axis, target, other),
            device_id_type=MESH,
        )
        copy.start()
        copies.append(copy)
    total = whole_ref[pl.ds(pl.multiple_of(me * rows, rows), rows), :].astype(jnp.float32)
    for k in _shifts(n):
        source = lax.rem(me + n - k, n)
        pltpu.make_async_remote_copy(
            src_ref=whole_ref.at[pl.ds(0, rows)],
            dst_ref=held.at[k],
            send_sem=send_sem.at[k],
            recv_sem=recv_sem.at[k],
            device_id=_place(axis, source, other),
            device_id_type=MESH,
        ).wait_recv()
        total = total + held[k].astype(jnp.float32)
    for copy in copies:
        copy.wait_send()
    return total


def _scatter_kernel(n, axis, whole_ref, out_ref, held, send_sem, recv_sem):
    me = lax.axis_index(axis)
    other = lax.axis_index("tp" if axis == "ctx" else "ctx")
    rows = out_ref.shape[0]
    _enter(n, me, other, axis)
    out_ref[...] = _scatter_sum(n, me, other, whole_ref, held, send_sem, recv_sem, rows, axis)


def ctx_scatter(whole, n, collective_id, axis="ctx"):
    rows, cols = whole.shape[0] // n, whole.shape[1]
    return pl.pallas_call(
        functools.partial(_scatter_kernel, n, axis),
        out_shape=jax.ShapeDtypeStruct((rows, cols), jnp.float32),
        in_specs=[pl.BlockSpec(memory_space=pltpu.VMEM)],
        out_specs=pl.BlockSpec(memory_space=pltpu.VMEM),
        scratch_shapes=[
            pltpu.VMEM((n, rows, cols), whole.dtype),
            pltpu.SemaphoreType.DMA((n,)),
            pltpu.SemaphoreType.DMA((n,)),
        ],
        compiler_params=pltpu.CompilerParams(
            collective_id=collective_id, has_side_effects=True, vmem_limit_bytes=VMEM_LIMIT
        ),
    )(whole)


def _shift_at(n, step):
    half = step // 2 + 1
    return jnp.where(step % 2 == 0, half, n - half)


def _sum_kernel(n, spans, whole_ref, extra_ref, out_ref, extra_out, wide_out, *scratch):
    pieces = len(spans)
    helds, mines, extra_held = scratch[:pieces], scratch[pieces : 2 * pieces], scratch[2 * pieces]
    sems = scratch[2 * pieces + 1 :]
    send_extra, recv_extra = sems[4 * pieces], sems[4 * pieces + 1]
    me = lax.axis_index("ctx")
    other = lax.axis_index("tp")
    rows = whole_ref.shape[0] // n
    own_rows = pl.ds(pl.multiple_of(me * rows, rows), rows)
    _enter(n, me, other)

    def extra_copy(k, peer):
        return pltpu.make_async_remote_copy(
            src_ref=extra_ref,
            dst_ref=extra_held.at[k],
            send_sem=send_extra.at[k],
            recv_sem=recv_extra.at[k],
            device_id=(peer, other),
            device_id_type=MESH,
        )

    def scatter_copy(piece, k, peer, block):
        first, width = spans[piece]
        return pltpu.make_async_remote_copy(
            src_ref=whole_ref.at[pl.ds(pl.multiple_of(block * rows, rows), rows), pl.ds(first, width)],
            dst_ref=helds[piece].at[k],
            send_sem=sems[4 * piece].at[k],
            recv_sem=sems[4 * piece + 1].at[k],
            device_id=(peer, other),
            device_id_type=MESH,
        )

    def gather_copy(piece, k, peer, block):
        first, width = spans[piece]
        return pltpu.make_async_remote_copy(
            src_ref=mines[piece],
            dst_ref=out_ref.at[pl.ds(pl.multiple_of(block * rows, rows), rows), pl.ds(first, width)],
            send_sem=sems[4 * piece + 2].at[k],
            recv_sem=sems[4 * piece + 3].at[k],
            device_id=(peer, other),
            device_id_type=MESH,
        )

    def each_peer(body):
        def step(index, carry):
            k = _shift_at(n, index)
            return body(k, lax.rem(me + k, n), lax.rem(me + n - k, n), carry)

        return lax.fori_loop(0, n - 1, step, 0)

    def start_extra(k, target, source, carry):
        extra_copy(k, target).start()
        return carry

    each_peer(start_extra)
    for piece in range(pieces):

        def start_scatter(k, target, source, carry, piece=piece):
            scatter_copy(piece, k, target, target).start()
            return carry

        each_peer(start_scatter)
    for piece, (first, width) in enumerate(spans):

        def add_block(index, total, piece=piece):
            k = _shift_at(n, index)
            scatter_copy(piece, k, lax.rem(me + n - k, n), me).wait_recv()
            return total + helds[piece][k].astype(jnp.float32)

        total = lax.fori_loop(
            0, n - 1, add_block, whole_ref[own_rows, pl.ds(first, width)].astype(jnp.float32)
        )
        mines[piece][...] = total.astype(mines[piece].dtype)

        def start_gather(k, target, source, carry, piece=piece):
            gather_copy(piece, k, target, me).start()
            return carry

        each_peer(start_gather)
        out_ref[own_rows, pl.ds(first, width)] = mines[piece][...]

    def add_extra(index, total):
        k = _shift_at(n, index)
        extra_copy(k, lax.rem(me + n - k, n)).wait_recv()
        return total + extra_held[k]

    extra_out[...] = lax.fori_loop(0, n - 1, add_extra, extra_ref[...])
    for piece in range(pieces):

        def finish(k, target, source, carry, piece=piece):
            gather_copy(piece, k, source, source).wait_recv()
            gather_copy(piece, k, target, me).wait_send()
            scatter_copy(piece, k, target, target).wait_send()
            return carry

        each_peer(finish)
        first, width = spans[piece]
        wide_out[:, pl.ds(first, width)] = out_ref[:, pl.ds(first, width)].astype(wide_out.dtype)

    def finish_extra(k, target, source, carry):
        extra_copy(k, target).wait_send()
        return carry

    each_peer(finish_extra)


def ctx_sum(whole, extra, n, collective_id, pieces=8):
    rows, cols = whole.shape[0] // n, whole.shape[1]
    lanes = cols // 128
    edges = [128 * (lanes * p // pieces) for p in range(pieces + 1)]
    spans = tuple((edges[p], edges[p + 1] - edges[p]) for p in range(pieces))
    return pl.pallas_call(
        functools.partial(_sum_kernel, n, spans),
        out_shape=(
            jax.ShapeDtypeStruct(whole.shape, whole.dtype),
            jax.ShapeDtypeStruct(extra.shape, extra.dtype),
            jax.ShapeDtypeStruct(whole.shape, jnp.float32),
        ),
        in_specs=[pl.BlockSpec(memory_space=pltpu.VMEM)] * 2,
        out_specs=(pl.BlockSpec(memory_space=pltpu.VMEM),) * 3,
        scratch_shapes=[pltpu.VMEM((n, rows, width), whole.dtype) for _, width in spans]
        + [pltpu.VMEM((rows, width), whole.dtype) for _, width in spans]
        + [pltpu.VMEM((n,) + extra.shape, extra.dtype)]
        + [pltpu.SemaphoreType.DMA((n,))] * (4 * pieces + 2),
        compiler_params=pltpu.CompilerParams(
            collective_id=collective_id, has_side_effects=True, vmem_limit_bytes=VMEM_LIMIT
        ),
    )(whole, extra)


EPS = 1e-05
THETA = 1000000.0
NEGATIVE = -1e30


def rms_forward(values, norm_gain):
    inverse = lax.rsqrt(jnp.mean(values * values, axis=-1, keepdims=True) + EPS)
    return (values * inverse * norm_gain, inverse)


def rms_backward(values, inverse, norm_gain, upstream):
    scaled = upstream * norm_gain
    inner_mean = jnp.mean(scaled * values, axis=-1, keepdims=True)
    through = inverse * (scaled - values * inverse * inverse * inner_mean)
    return (through, upstream * values * inverse)


def rope_tables(positions, head_dim):
    halfway = head_dim // 2
    frequency = THETA ** (-(jnp.arange(halfway, dtype=jnp.float32) * 2.0 / head_dim))
    angles = positions.astype(jnp.float32)[:, None] * frequency[None, :]
    return (jnp.cos(angles)[:, None, :], jnp.sin(angles)[:, None, :])


def rope_apply(values, cosine, sine_table):
    halfway = values.shape[-1] // 2
    first_half = values[..., :halfway]
    second_half = values[..., halfway:]
    return jnp.concatenate(
        [
            first_half * cosine - second_half * sine_table,
            second_half * cosine + first_half * sine_table,
        ],
        axis=-1,
    )


def rope_back(upstream, cosine, sine_table):
    halfway = upstream.shape[-1] // 2
    first_half = upstream[..., :halfway]
    second_half = upstream[..., halfway:]
    return jnp.concatenate(
        [
            first_half * cosine + second_half * sine_table,
            second_half * cosine - first_half * sine_table,
        ],
        axis=-1,
    )


def row_places(block_map, holder, rows_total, place_count):
    piece_len = rows_total // 4
    within = jnp.arange(rows_total, dtype=jnp.int32)
    picked = jnp.sum(jnp.where(jnp.arange(place_count, dtype=jnp.int32) == holder, block_map, 0))
    later = within // piece_len % 2
    piece_index = jnp.where(later == 1, 2 * place_count - 1 - picked, picked)
    return piece_index * piece_len + within % piece_len


def span_places(block_map, first_anchor, shard_span, seq_rows, place_count):
    piece_len = seq_rows // 2
    anchors = first_anchor + jnp.arange(shard_span, dtype=jnp.int32)
    picked = jnp.sum(
        jnp.where(
            jnp.arange(place_count, dtype=jnp.int32)[None, :] == anchors[:, None],
            block_map[None, :],
            0,
        ),
        axis=1,
    )
    within = jnp.arange(seq_rows, dtype=jnp.int32)
    later = within // piece_len % 2
    piece_index = jnp.where(
        later[None, :] == 1, 2 * place_count - 1 - picked[:, None], picked[:, None]
    )
    return (piece_index * piece_len + (within % piece_len)[None, :]).reshape(shard_span * seq_rows)


def gather_rows(rows_low):
    return lax.all_gather(rows_low, "tp", axis=0, tiled=True)


def reduce_rows(partial_rows, collective_id):
    return ctx_scatter(
        partial_rows.astype(jnp.bfloat16), lax.axis_size("tp"), collective_id, "tp"
    )


def per_device(
    block_input,
    block_map,
    attn_gain,
    query_weight,
    key_weight,
    value_weight,
    query_gain,
    key_gain,
    output_weight,
    ffn_gain,
    gate_weight,
    up_weight,
    down_weight,
    cotangent,
):
    place_count = lax.axis_size("ctx")
    place_index = lax.axis_index("ctx")
    head_dim = query_gain.shape[0]
    query_heads = query_weight.shape[1] // head_dim
    kv_heads = key_weight.shape[1] // head_dim
    group_size = query_heads // kv_heads
    score_scale = 1.0 / math.sqrt(head_dim)
    shard_span = 4
    residual_in = block_input.astype(jnp.float32)
    normed_one, inverse_one = rms_forward(residual_in, attn_gain)
    rows_one = gather_rows(normed_one.astype(jnp.bfloat16))
    rows_total = rows_one.shape[0]
    seq_rows = rows_total // 2
    kv_width = kv_heads * head_dim
    own_places = row_places(block_map, place_index, rows_total, place_count)
    query_raw = jnp.dot(rows_one, query_weight, preferred_element_type=jnp.float32).reshape(
        rows_total, query_heads, head_dim
    )
    key_raw = jnp.dot(rows_one, key_weight, preferred_element_type=jnp.float32).reshape(
        rows_total, kv_heads, head_dim
    )
    values_own = jnp.dot(rows_one, value_weight, preferred_element_type=jnp.float32).astype(
        jnp.bfloat16
    )
    query_normed, query_inverse = rms_forward(query_raw, query_gain)
    key_normed, key_inverse = rms_forward(key_raw, key_gain)
    cosine, sine_table = rope_tables(own_places, head_dim)
    query_rot = rope_apply(query_normed, cosine, sine_table).astype(jnp.bfloat16)
    keys_own = (
        rope_apply(key_normed, cosine, sine_table)
        .astype(jnp.bfloat16)
        .reshape(rows_total, kv_width)
    )
    query_blocks = query_rot.reshape(2, seq_rows, kv_heads, group_size, head_dim)
    query_places = own_places[:seq_rows]

    whole_kv = ctx_gather(jnp.concatenate([keys_own, values_own], axis=1), place_count, 0)
    seq_kv = jnp.transpose(
        whole_kv.reshape(place_count, 2, seq_rows, 2 * kv_width), (1, 0, 2, 3)
    ).reshape(2, place_count * seq_rows, 2 * kv_width)
    key_heads = seq_kv[..., :kv_width].reshape(2, place_count * seq_rows, kv_heads, head_dim)
    value_heads = seq_kv[..., kv_width:].reshape(2, place_count * seq_rows, kv_heads, head_dim)
    key_places = span_places(block_map, 0, place_count, seq_rows, place_count)
    allowed = key_places[None, :] <= query_places[:, None]
    scores = (
        jnp.einsum(
            "sqhgd,skhd->shgqk", query_blocks, key_heads, preferred_element_type=jnp.float32
        )
        * score_scale
    )
    top = jnp.max(jnp.where(allowed, scores, NEGATIVE), axis=-1)
    weights = jnp.where(allowed, jnp.exp(scores - top[..., None]), 0.0)
    weight_total = jnp.sum(weights, axis=-1)
    weighted = jnp.einsum(
        "shgqk,skhd->shgqd",
        weights.astype(jnp.bfloat16),
        value_heads,
        preferred_element_type=jnp.float32,
    )
    log_total = top + jnp.log(weight_total)
    attn_rows = jnp.transpose(weighted / weight_total[..., None], (0, 3, 1, 2, 4))
    attn_low = attn_rows.reshape(rows_total, query_heads * head_dim).astype(jnp.bfloat16)
    residual_mid = residual_in + reduce_rows(
        jnp.dot(attn_low, output_weight, preferred_element_type=jnp.float32),
        3
    )
    normed_two, inverse_two = rms_forward(residual_mid, ffn_gain)
    rows_two = gather_rows(normed_two.astype(jnp.bfloat16))
    gate_pre = jnp.dot(rows_two, gate_weight, preferred_element_type=jnp.float32)
    up_pre = jnp.dot(rows_two, up_weight, preferred_element_type=jnp.float32)
    gate_sig = jax.nn.sigmoid(gate_pre)
    activated = (gate_pre * gate_sig * up_pre).astype(jnp.bfloat16)
    block_output = residual_mid + reduce_rows(
        jnp.dot(activated, down_weight, preferred_element_type=jnp.float32),
        4
    )
    grad_rows = gather_rows(cotangent)
    grad_down_t = jnp.dot(grad_rows.T, activated, preferred_element_type=jnp.float32)
    grad_act = jnp.dot(grad_rows, down_weight.T, preferred_element_type=jnp.float32)
    grad_gate_pre = (grad_act * up_pre * gate_sig * (1.0 + gate_pre * (1.0 - gate_sig))).astype(
        jnp.bfloat16
    )
    grad_up_pre = (grad_act * gate_pre * gate_sig).astype(jnp.bfloat16)
    grad_gate = jnp.dot(rows_two.T, grad_gate_pre, preferred_element_type=jnp.float32)
    grad_up = jnp.dot(rows_two.T, grad_up_pre, preferred_element_type=jnp.float32)
    grad_normed_two = reduce_rows(
        jnp.dot(grad_gate_pre, gate_weight.T, preferred_element_type=jnp.float32)
        + jnp.dot(grad_up_pre, up_weight.T, preferred_element_type=jnp.float32),
        5
    )
    through_two, ffn_terms = rms_backward(residual_mid, inverse_two, ffn_gain, grad_normed_two)
    grad_mid = cotangent.astype(jnp.float32) + through_two
    grad_mid_rows = gather_rows(grad_mid.astype(jnp.bfloat16))
    grad_output_t = jnp.dot(grad_mid_rows.T, attn_low, preferred_element_type=jnp.float32)
    grad_attn = jnp.dot(grad_mid_rows, output_weight.T, preferred_element_type=jnp.float32).astype(
        jnp.bfloat16
    )
    grad_attn_blocks = grad_attn.reshape(2, seq_rows, kv_heads, group_size, head_dim)
    delta_rows = jnp.sum(grad_attn_blocks.astype(jnp.float32) * attn_rows, axis=-1)
    delta_rows = jnp.transpose(delta_rows, (0, 2, 3, 1))

    probs = jnp.where(allowed, jnp.exp(scores - log_total[..., None]), 0.0)
    grad_value_seq = jnp.einsum(
        "shgqk,sqhgd->skhd",
        probs.astype(jnp.bfloat16),
        grad_attn_blocks,
        preferred_element_type=jnp.float32,
    )
    grad_probs = jnp.einsum(
        "sqhgd,skhd->shgqk", grad_attn_blocks, value_heads, preferred_element_type=jnp.float32
    )
    grad_scores = (score_scale * probs * (grad_probs - delta_rows[..., None])).astype(jnp.bfloat16)
    query_acc = jnp.einsum(
        "shgqk,skhd->sqhgd", grad_scores, key_heads, preferred_element_type=jnp.float32
    )
    grad_key_seq = jnp.einsum(
        "shgqk,sqhgd->skhd", grad_scores, query_blocks, preferred_element_type=jnp.float32
    )
    grad_kv_seq = jnp.concatenate(
        [
            grad_key_seq.reshape(2, place_count, seq_rows, kv_width),
            grad_value_seq.reshape(2, place_count, seq_rows, kv_width),
        ],
        axis=-1,
    )
    grad_kv_all = jnp.transpose(grad_kv_seq, (1, 0, 2, 3)).reshape(
        place_count * rows_total, 2 * kv_width
    )
    grad_kv_flat = ctx_scatter(
        grad_kv_all.astype(jnp.bfloat16),
        place_count,
        1,
    )
    grad_keys_flat, grad_values_flat = grad_kv_flat[:, :kv_width], grad_kv_flat[:, kv_width:]
    grad_query_rot = query_acc.reshape(rows_total, query_heads, head_dim)
    grad_key_rot = grad_keys_flat.reshape(rows_total, kv_heads, head_dim)
    grad_query_raw, query_terms = rms_backward(
        query_raw, query_inverse, query_gain, rope_back(grad_query_rot, cosine, sine_table)
    )
    grad_key_raw, key_terms = rms_backward(
        key_raw, key_inverse, key_gain, rope_back(grad_key_rot, cosine, sine_table)
    )
    grad_query_low = grad_query_raw.reshape(rows_total, query_heads * head_dim).astype(jnp.bfloat16)
    grad_key_low = grad_key_raw.reshape(rows_total, kv_width).astype(jnp.bfloat16)
    grad_value_low = grad_values_flat.astype(jnp.bfloat16)
    grad_query = jnp.dot(rows_one.T, grad_query_low, preferred_element_type=jnp.float32)
    grad_key = jnp.dot(rows_one.T, grad_key_low, preferred_element_type=jnp.float32)
    grad_value = jnp.dot(rows_one.T, grad_value_low, preferred_element_type=jnp.float32)
    grad_normed_one = reduce_rows(
        jnp.dot(grad_query_low, query_weight.T, preferred_element_type=jnp.float32)
        + jnp.dot(grad_key_low, key_weight.T, preferred_element_type=jnp.float32)
        + jnp.dot(grad_value_low, value_weight.T, preferred_element_type=jnp.float32),
        6
    )
    through_one, attn_terms = rms_backward(residual_in, inverse_one, attn_gain, grad_normed_one)
    input_grad = grad_mid + through_one
    weight_parts = (grad_query, grad_key, grad_value, grad_output_t, grad_gate, grad_up, grad_down_t)
    widths = [part.shape[1] for part in weight_parts]
    gain_parts = (
        jnp.sum(attn_terms, axis=0),
        jnp.sum(query_terms, axis=(0, 1)),
        jnp.sum(key_terms, axis=(0, 1)),
        jnp.sum(ffn_terms, axis=0),
    )
    gain_sizes = [part.shape[0] for part in gain_parts]
    gain_local = jnp.concatenate(gain_parts)
    gain_pad = -gain_local.shape[0] % 1024
    tp_count = lax.axis_size("tp")
    gain_flat = ctx_scatter(
        jnp.tile(jnp.pad(gain_local, (0, gain_pad)).reshape(8, -1), (tp_count, 1)),
        tp_count,
        7,
        "tp",
    ).reshape(-1)[: gain_local.shape[0]]
    _, gains, summed = ctx_sum(
        jnp.concatenate([part.astype(jnp.bfloat16) for part in weight_parts], axis=1),
        jnp.pad(gain_flat, (0, gain_pad)).reshape(8, -1),
        place_count,
        2,
    )
    gains = gains.reshape(-1)
    offsets = [sum(widths[:k]) for k in range(len(widths) + 1)]
    shared_query, shared_key, shared_value, output_t, shared_gate, shared_up, down_t = (
        summed[:, offsets[k] : offsets[k + 1]] for k in range(len(widths))
    )
    shared_output = output_t.T
    shared_down = down_t.T
    gain_attn = gains[: gain_sizes[0]]
    gain_query = gains[gain_sizes[0] : gain_sizes[0] + gain_sizes[1]]
    gain_key = gains[gain_sizes[0] + gain_sizes[1] : gain_sizes[0] + gain_sizes[1] + gain_sizes[2]]
    gain_ffn = gains[gain_sizes[0] + gain_sizes[1] + gain_sizes[2] : sum(gain_sizes)]
    return (
        block_output,
        input_grad,
        gain_attn,
        shared_query,
        shared_key,
        shared_value,
        gain_query,
        gain_key,
        shared_output,
        gain_ffn,
        shared_gate,
        shared_up,
        shared_down,
    )


def solution(mesh):
    return jax.shard_map(
        per_device,
        mesh=mesh,
        in_specs=(
            P(("ctx", "tp"), None),
            P(),
            P(),
            P(None, "tp"),
            P(None, "tp"),
            P(None, "tp"),
            P(),
            P(),
            P("tp", None),
            P(),
            P(None, "tp"),
            P(None, "tp"),
            P("tp", None),
            P(("ctx", "tp"), None),
        ),
        out_specs=(
            P(("ctx", "tp"), None),
            P(("ctx", "tp"), None),
            P(),
            P(None, "tp"),
            P(None, "tp"),
            P(None, "tp"),
            P(),
            P(),
            P("tp", None),
            P(),
            P(None, "tp"),
            P(None, "tp"),
            P("tp", None),
        ),
        check_vma=False,
    )
```

```python
import functools
import math

import jax
import jax.numpy as jnp
from jax import lax
from jax.experimental import pallas as pl
from jax.experimental.pallas import tpu as pltpu
from jax.sharding import PartitionSpec as P

MESH = pl.DeviceIdType.MESH
VMEM_LIMIT = 60 * 1024 * 1024


def _shifts(n):
    order = []
    for k in range(1, n // 2 + 1):
        order.append(k)
        if n - k != k:
            order.append(n - k)
    return order


def _place(axis, peer, other):
    return (peer, other) if axis == "ctx" else (other, peer)


def _enter(n, me, peer_axis, axis="ctx"):
    barrier = pltpu.get_barrier_semaphore()
    for k in _shifts(n):
        pl.semaphore_signal(
            barrier,
            1,
            device_id=_place(axis, lax.rem(me + k, n), peer_axis),
            device_id_type=MESH,
        )
    pl.semaphore_wait(barrier, n - 1)


def _gather_kernel(n, part_ref, out_ref, send_sem, recv_sem):
    me = lax.axis_index("ctx")
    other = lax.axis_index("tp")
    rows = part_ref.shape[0]
    _enter(n, me, other)
    copies = []
    for k in _shifts(n):
        copy = pltpu.make_async_remote_copy(
            src_ref=part_ref,
            dst_ref=out_ref.at[pl.ds(pl.multiple_of(me * rows, rows), rows)],
            send_sem=send_sem.at[k],
            recv_sem=recv_sem.at[k],
            device_id=(lax.rem(me + k, n), other),
            device_id_type=MESH,
        )
        copy.start()
        copies.append(copy)
    out_ref[pl.ds(pl.multiple_of(me * rows, rows), rows), :] = part_ref[...]
    for k in _shifts(n):
        source = lax.rem(me + n - k, n)
        pltpu.make_async_remote_copy(
            src_ref=part_ref,
            dst_ref=out_ref.at[pl.ds(pl.multiple_of(source * rows, rows), rows)],
            send_sem=send_sem.at[k],
            recv_sem=recv_sem.at[k],
            device_id=(source, other),
            device_id_type=MESH,
        ).wait_recv()
    for copy in copies:
        copy.wait_send()


def ctx_gather(part, n, collective_id):
    rows, cols = part.shape
    return pl.pallas_call(
        functools.partial(_gather_kernel, n),
        out_shape=jax.ShapeDtypeStruct((n * rows, cols), part.dtype),
        in_specs=[pl.BlockSpec(memory_space=pltpu.VMEM)],
        out_specs=pl.BlockSpec(memory_space=pltpu.VMEM),
        scratch_shapes=[pltpu.SemaphoreType.DMA((n,)), pltpu.SemaphoreType.DMA((n,))],
        compiler_params=pltpu.CompilerParams(
            collective_id=collective_id, has_side_effects=True, vmem_limit_bytes=VMEM_LIMIT
        ),
    )(part)


def _scatter_sum(n, me, other, whole_ref, held, send_sem, recv_sem, rows, axis="ctx"):
    copies = []
    for k in _shifts(n):
        target = lax.rem(me + k, n)
        copy = pltpu.make_async_remote_copy(
            src_ref=whole_ref.at[pl.ds(pl.multiple_of(target * rows, rows), rows)],
            dst_ref=held.at[k],
            send_sem=send_sem.at[k],
            recv_sem=recv_sem.at[k],
            device_id=_place(axis, target, other),
            device_id_type=MESH,
        )
        copy.start()
        copies.append(copy)
    total = whole_ref[pl.ds(pl.multiple_of(me * rows, rows), rows), :].astype(jnp.float32)
    for k in _shifts(n):
        source = lax.rem(me + n - k, n)
        pltpu.make_async_remote_copy(
            src_ref=whole_ref.at[pl.ds(0, rows)],
            dst_ref=held.at[k],
            send_sem=send_sem.at[k],
            recv_sem=recv_sem.at[k],
            device_id=_place(axis, source, other),
            device_id_type=MESH,
        ).wait_recv()
        total = total + held[k].astype(jnp.float32)
    for copy in copies:
        copy.wait_send()
    return total


def _scatter_kernel(n, axis, whole_ref, out_ref, held, send_sem, recv_sem):
    me = lax.axis_index(axis)
    other = lax.axis_index("tp" if axis == "ctx" else "ctx")
    rows = out_ref.shape[0]
    _enter(n, me, other, axis)
    out_ref[...] = _scatter_sum(n, me, other, whole_ref, held, send_sem, recv_sem, rows, axis)


def ctx_scatter(whole, n, collective_id, axis="ctx"):
    rows, cols = whole.shape[0] // n, whole.shape[1]
    return pl.pallas_call(
        functools.partial(_scatter_kernel, n, axis),
        out_shape=jax.ShapeDtypeStruct((rows, cols), jnp.float32),
        in_specs=[pl.BlockSpec(memory_space=pltpu.VMEM)],
        out_specs=pl.BlockSpec(memory_space=pltpu.VMEM),
        scratch_shapes=[
            pltpu.VMEM((n, rows, cols), whole.dtype),
            pltpu.SemaphoreType.DMA((n,)),
            pltpu.SemaphoreType.DMA((n,)),
        ],
        compiler_params=pltpu.CompilerParams(
            collective_id=collective_id, has_side_effects=True, vmem_limit_bytes=VMEM_LIMIT
        ),
    )(whole)


def _shift_at(n, step):
    half = step // 2 + 1
    return jnp.where(step % 2 == 0, half, n - half)


def _sum_kernel(n, spans, whole_ref, extra_ref, out_ref, extra_out, wide_out, *scratch):
    pieces = len(spans)
    helds, mines, extra_held = scratch[:pieces], scratch[pieces : 2 * pieces], scratch[2 * pieces]
    sems = scratch[2 * pieces + 1 :]
    send_extra, recv_extra = sems[4 * pieces], sems[4 * pieces + 1]
    me = lax.axis_index("ctx")
    other = lax.axis_index("tp")
    rows = whole_ref.shape[0] // n
    own_rows = pl.ds(pl.multiple_of(me * rows, rows), rows)
    _enter(n, me, other)

    def extra_copy(k, peer):
        return pltpu.make_async_remote_copy(
            src_ref=extra_ref,
            dst_ref=extra_held.at[k],
            send_sem=send_extra.at[k],
            recv_sem=recv_extra.at[k],
            device_id=(peer, other),
            device_id_type=MESH,
        )

    def scatter_copy(piece, k, peer, block):
        first, width = spans[piece]
        return pltpu.make_async_remote_copy(
            src_ref=whole_ref.at[pl.ds(pl.multiple_of(block * rows, rows), rows), pl.ds(first, width)],
            dst_ref=helds[piece].at[k],
            send_sem=sems[4 * piece].at[k],
            recv_sem=sems[4 * piece + 1].at[k],
            device_id=(peer, other),
            device_id_type=MESH,
        )

    def gather_copy(piece, k, peer, block):
        first, width = spans[piece]
        return pltpu.make_async_remote_copy(
            src_ref=mines[piece],
            dst_ref=out_ref.at[pl.ds(pl.multiple_of(block * rows, rows), rows), pl.ds(first, width)],
            send_sem=sems[4 * piece + 2].at[k],
            recv_sem=sems[4 * piece + 3].at[k],
            device_id=(peer, other),
            device_id_type=MESH,
        )

    def each_peer(body):
        def step(index, carry):
            k = _shift_at(n, index)
            return body(k, lax.rem(me + k, n), lax.rem(me + n - k, n), carry)

        return lax.fori_loop(0, n - 1, step, 0)

    def start_extra(k, target, source, carry):
        extra_copy(k, target).start()
        return carry

    each_peer(start_extra)
    for piece in range(pieces):

        def start_scatter(k, target, source, carry, piece=piece):
            scatter_copy(piece, k, target, target).start()
            return carry

        each_peer(start_scatter)
    for piece, (first, width) in enumerate(spans):

        def add_block(index, total, piece=piece):
            k = _shift_at(n, index)
            scatter_copy(piece, k, lax.rem(me + n - k, n), me).wait_recv()
            return total + helds[piece][k].astype(jnp.float32)

        total = lax.fori_loop(
            0, n - 1, add_block, whole_ref[own_rows, pl.ds(first, width)].astype(jnp.float32)
        )
        mines[piece][...] = total.astype(mines[piece].dtype)

        def start_gather(k, target, source, carry, piece=piece):
            gather_copy(piece, k, target, me).start()
            return carry

        each_peer(start_gather)
        out_ref[own_rows, pl.ds(first, width)] = mines[piece][...]

    def add_extra(index, total):
        k = _shift_at(n, index)
        extra_copy(k, lax.rem(me + n - k, n)).wait_recv()
        return total + extra_held[k]

    extra_out[...] = lax.fori_loop(0, n - 1, add_extra, extra_ref[...])
    for piece in range(pieces):

        def finish(k, target, source, carry, piece=piece):
            gather_copy(piece, k, source, source).wait_recv()
            gather_copy(piece, k, target, me).wait_send()
            scatter_copy(piece, k, target, target).wait_send()
            return carry

        each_peer(finish)
        first, width = spans[piece]
        wide_out[:, pl.ds(first, width)] = out_ref[:, pl.ds(first, width)].astype(wide_out.dtype)

    def finish_extra(k, target, source, carry):
        extra_copy(k, target).wait_send()
        return carry

    each_peer(finish_extra)


def ctx_sum(whole, extra, n, collective_id, pieces=11):
    rows, cols = whole.shape[0] // n, whole.shape[1]
    lanes = cols // 128
    edges = [128 * (lanes * p // pieces) for p in range(pieces + 1)]
    spans = tuple((edges[p], edges[p + 1] - edges[p]) for p in range(pieces))
    return pl.pallas_call(
        functools.partial(_sum_kernel, n, spans),
        out_shape=(
            jax.ShapeDtypeStruct(whole.shape, whole.dtype),
            jax.ShapeDtypeStruct(extra.shape, extra.dtype),
            jax.ShapeDtypeStruct(whole.shape, jnp.float32),
        ),
        in_specs=[pl.BlockSpec(memory_space=pltpu.VMEM)] * 2,
        out_specs=(pl.BlockSpec(memory_space=pltpu.VMEM),) * 3,
        scratch_shapes=[pltpu.VMEM((n, rows, width), whole.dtype) for _, width in spans]
        + [pltpu.VMEM((rows, width), whole.dtype) for _, width in spans]
        + [pltpu.VMEM((n,) + extra.shape, extra.dtype)]
        + [pltpu.SemaphoreType.DMA((n,))] * (4 * pieces + 2),
        compiler_params=pltpu.CompilerParams(
            collective_id=collective_id, has_side_effects=True, vmem_limit_bytes=VMEM_LIMIT
        ),
    )(whole, extra)


EPS = 1e-05
THETA = 1000000.0
NEGATIVE = -1e30


def rms_forward(values, norm_gain):
    inverse = lax.rsqrt(jnp.mean(values * values, axis=-1, keepdims=True) + EPS)
    return (values * inverse * norm_gain, inverse)


def rms_backward(values, inverse, norm_gain, upstream):
    scaled = upstream * norm_gain
    inner_mean = jnp.mean(scaled * values, axis=-1, keepdims=True)
    through = inverse * (scaled - values * inverse * inverse * inner_mean)
    return (through, upstream * values * inverse)


def rope_tables(positions, head_dim):
    halfway = head_dim // 2
    frequency = THETA ** (-(jnp.arange(halfway, dtype=jnp.float32) * 2.0 / head_dim))
    angles = positions.astype(jnp.float32)[:, None] * frequency[None, :]
    return (jnp.cos(angles)[:, None, :], jnp.sin(angles)[:, None, :])


def rope_apply(values, cosine, sine_table):
    halfway = values.shape[-1] // 2
    first_half = values[..., :halfway]
    second_half = values[..., halfway:]
    return jnp.concatenate(
        [
            first_half * cosine - second_half * sine_table,
            second_half * cosine + first_half * sine_table,
        ],
        axis=-1,
    )


def rope_back(upstream, cosine, sine_table):
    halfway = upstream.shape[-1] // 2
    first_half = upstream[..., :halfway]
    second_half = upstream[..., halfway:]
    return jnp.concatenate(
        [
            first_half * cosine + second_half * sine_table,
            second_half * cosine - first_half * sine_table,
        ],
        axis=-1,
    )


def row_places(block_map, holder, rows_total, place_count):
    piece_len = rows_total // 4
    within = jnp.arange(rows_total, dtype=jnp.int32)
    picked = jnp.sum(jnp.where(jnp.arange(place_count, dtype=jnp.int32) == holder, block_map, 0))
    later = within // piece_len % 2
    piece_index = jnp.where(later == 1, 2 * place_count - 1 - picked, picked)
    return piece_index * piece_len + within % piece_len


def span_places(block_map, first_anchor, shard_span, seq_rows, place_count):
    piece_len = seq_rows // 2
    anchors = first_anchor + jnp.arange(shard_span, dtype=jnp.int32)
    picked = jnp.sum(
        jnp.where(
            jnp.arange(place_count, dtype=jnp.int32)[None, :] == anchors[:, None],
            block_map[None, :],
            0,
        ),
        axis=1,
    )
    within = jnp.arange(seq_rows, dtype=jnp.int32)
    later = within // piece_len % 2
    piece_index = jnp.where(
        later[None, :] == 1, 2 * place_count - 1 - picked[:, None], picked[:, None]
    )
    return (piece_index * piece_len + (within % piece_len)[None, :]).reshape(shard_span * seq_rows)


def gather_rows(rows_low):
    return lax.all_gather(rows_low, "tp", axis=0, tiled=True)


def reduce_rows(partial_rows, collective_id):
    return ctx_scatter(
        partial_rows.astype(jnp.bfloat16), lax.axis_size("tp"), collective_id, "tp"
    )


def per_device(
    block_input,
    block_map,
    attn_gain,
    query_weight,
    key_weight,
    value_weight,
    query_gain,
    key_gain,
    output_weight,
    ffn_gain,
    gate_weight,
    up_weight,
    down_weight,
    cotangent,
):
    place_count = lax.axis_size("ctx")
    place_index = lax.axis_index("ctx")
    head_dim = query_gain.shape[0]
    query_heads = query_weight.shape[1] // head_dim
    kv_heads = key_weight.shape[1] // head_dim
    group_size = query_heads // kv_heads
    score_scale = 1.0 / math.sqrt(head_dim)
    shard_span = 4
    residual_in = block_input.astype(jnp.float32)
    normed_one, inverse_one = rms_forward(residual_in, attn_gain)
    rows_one = gather_rows(normed_one.astype(jnp.bfloat16))
    rows_total = rows_one.shape[0]
    seq_rows = rows_total // 2
    kv_width = kv_heads * head_dim
    own_places = row_places(block_map, place_index, rows_total, place_count)
    query_raw = jnp.dot(rows_one, query_weight, preferred_element_type=jnp.float32).reshape(
        rows_total, query_heads, head_dim
    )
    key_raw = jnp.dot(rows_one, key_weight, preferred_element_type=jnp.float32).reshape(
        rows_total, kv_heads, head_dim
    )
    values_own = jnp.dot(rows_one, value_weight, preferred_element_type=jnp.float32).astype(
        jnp.bfloat16
    )
    query_normed, query_inverse = rms_forward(query_raw, query_gain)
    key_normed, key_inverse = rms_forward(key_raw, key_gain)
    cosine, sine_table = rope_tables(own_places, head_dim)
    query_rot = rope_apply(query_normed, cosine, sine_table).astype(jnp.bfloat16)
    keys_own = (
        rope_apply(key_normed, cosine, sine_table)
        .astype(jnp.bfloat16)
        .reshape(rows_total, kv_width)
    )
    query_blocks = query_rot.reshape(2, seq_rows, kv_heads, group_size, head_dim)
    query_places = own_places[:seq_rows]

    whole_kv = ctx_gather(jnp.concatenate([keys_own, values_own], axis=1), place_count, 0)
    seq_kv = jnp.transpose(
        whole_kv.reshape(place_count, 2, seq_rows, 2 * kv_width), (1, 0, 2, 3)
    ).reshape(2, place_count * seq_rows, 2 * kv_width)
    key_heads = seq_kv[..., :kv_width].reshape(2, place_count * seq_rows, kv_heads, head_dim)
    value_heads = seq_kv[..., kv_width:].reshape(2, place_count * seq_rows, kv_heads, head_dim)
    key_places = span_places(block_map, 0, place_count, seq_rows, place_count)
    allowed = key_places[None, :] <= query_places[:, None]
    scores = (
        jnp.einsum(
            "sqhgd,skhd->shgqk", query_blocks, key_heads, preferred_element_type=jnp.float32
        )
        * score_scale
    )
    top = jnp.max(jnp.where(allowed, scores, NEGATIVE), axis=-1)
    weights = jnp.where(allowed, jnp.exp(scores - top[..., None]), 0.0)
    weight_total = jnp.sum(weights, axis=-1)
    weighted = jnp.einsum(
        "shgqk,skhd->shgqd",
        weights.astype(jnp.bfloat16),
        value_heads,
        preferred_element_type=jnp.float32,
    )
    log_total = top + jnp.log(weight_total)
    attn_rows = jnp.transpose(weighted / weight_total[..., None], (0, 3, 1, 2, 4))
    attn_low = attn_rows.reshape(rows_total, query_heads * head_dim).astype(jnp.bfloat16)
    residual_mid = residual_in + reduce_rows(
        jnp.dot(attn_low, output_weight, preferred_element_type=jnp.float32),
        3
    )
    normed_two, inverse_two = rms_forward(residual_mid, ffn_gain)
    rows_two = gather_rows(normed_two.astype(jnp.bfloat16))
    gate_pre = jnp.dot(rows_two, gate_weight, preferred_element_type=jnp.float32)
    up_pre = jnp.dot(rows_two, up_weight, preferred_element_type=jnp.float32)
    gate_sig = jax.nn.sigmoid(gate_pre)
    activated = (gate_pre * gate_sig * up_pre).astype(jnp.bfloat16)
    block_output = residual_mid + reduce_rows(
        jnp.dot(activated, down_weight, preferred_element_type=jnp.float32),
        4
    )
    grad_rows = gather_rows(cotangent)
    grad_down_t = jnp.dot(grad_rows.T, activated, preferred_element_type=jnp.float32)
    grad_act = jnp.dot(grad_rows, down_weight.T, preferred_element_type=jnp.float32)
    grad_gate_pre = (grad_act * up_pre * gate_sig * (1.0 + gate_pre * (1.0 - gate_sig))).astype(
        jnp.bfloat16
    )
    grad_up_pre = (grad_act * gate_pre * gate_sig).astype(jnp.bfloat16)
    grad_gate = jnp.dot(rows_two.T, grad_gate_pre, preferred_element_type=jnp.float32)
    grad_up = jnp.dot(rows_two.T, grad_up_pre, preferred_element_type=jnp.float32)
    grad_normed_two = reduce_rows(
        jnp.dot(grad_gate_pre, gate_weight.T, preferred_element_type=jnp.float32)
        + jnp.dot(grad_up_pre, up_weight.T, preferred_element_type=jnp.float32),
        5
    )
    through_two, ffn_terms = rms_backward(residual_mid, inverse_two, ffn_gain, grad_normed_two)
    grad_mid = cotangent.astype(jnp.float32) + through_two
    grad_mid_rows = gather_rows(grad_mid.astype(jnp.bfloat16))
    grad_output_t = jnp.dot(grad_mid_rows.T, attn_low, preferred_element_type=jnp.float32)
    grad_attn = jnp.dot(grad_mid_rows, output_weight.T, preferred_element_type=jnp.float32).astype(
        jnp.bfloat16
    )
    grad_attn_blocks = grad_attn.reshape(2, seq_rows, kv_heads, group_size, head_dim)
    delta_rows = jnp.sum(grad_attn_blocks.astype(jnp.float32) * attn_rows, axis=-1)
    delta_rows = jnp.transpose(delta_rows, (0, 2, 3, 1))

    probs = jnp.where(allowed, jnp.exp(scores - log_total[..., None]), 0.0)
    grad_value_seq = jnp.einsum(
        "shgqk,sqhgd->skhd",
        probs.astype(jnp.bfloat16),
        grad_attn_blocks,
        preferred_element_type=jnp.float32,
    )
    grad_probs = jnp.einsum(
        "sqhgd,skhd->shgqk", grad_attn_blocks, value_heads, preferred_element_type=jnp.float32
    )
    grad_scores = (score_scale * probs * (grad_probs - delta_rows[..., None])).astype(jnp.bfloat16)
    query_acc = jnp.einsum(
        "shgqk,skhd->sqhgd", grad_scores, key_heads, preferred_element_type=jnp.float32
    )
    grad_key_seq = jnp.einsum(
        "shgqk,sqhgd->skhd", grad_scores, query_blocks, preferred_element_type=jnp.float32
    )
    grad_kv_seq = jnp.concatenate(
        [
            grad_key_seq.reshape(2, place_count, seq_rows, kv_width),
            grad_value_seq.reshape(2, place_count, seq_rows, kv_width),
        ],
        axis=-1,
    )
    grad_kv_all = jnp.transpose(grad_kv_seq, (1, 0, 2, 3)).reshape(
        place_count * rows_total, 2 * kv_width
    )
    grad_kv_flat = ctx_scatter(
        grad_kv_all.astype(jnp.bfloat16),
        place_count,
        1,
    )
    grad_keys_flat, grad_values_flat = grad_kv_flat[:, :kv_width], grad_kv_flat[:, kv_width:]
    grad_query_rot = query_acc.reshape(rows_total, query_heads, head_dim)
    grad_key_rot = grad_keys_flat.reshape(rows_total, kv_heads, head_dim)
    grad_query_raw, query_terms = rms_backward(
        query_raw, query_inverse, query_gain, rope_back(grad_query_rot, cosine, sine_table)
    )
    grad_key_raw, key_terms = rms_backward(
        key_raw, key_inverse, key_gain, rope_back(grad_key_rot, cosine, sine_table)
    )
    grad_query_low = grad_query_raw.reshape(rows_total, query_heads * head_dim).astype(jnp.bfloat16)
    grad_key_low = grad_key_raw.reshape(rows_total, kv_width).astype(jnp.bfloat16)
    grad_value_low = grad_values_flat.astype(jnp.bfloat16)
    grad_query = jnp.dot(rows_one.T, grad_query_low, preferred_element_type=jnp.float32)
    grad_key = jnp.dot(rows_one.T, grad_key_low, preferred_element_type=jnp.float32)
    grad_value = jnp.dot(rows_one.T, grad_value_low, preferred_element_type=jnp.float32)
    grad_normed_one = reduce_rows(
        jnp.dot(grad_query_low, query_weight.T, preferred_element_type=jnp.float32)
        + jnp.dot(grad_key_low, key_weight.T, preferred_element_type=jnp.float32)
        + jnp.dot(grad_value_low, value_weight.T, preferred_element_type=jnp.float32),
        6
    )
    through_one, attn_terms = rms_backward(residual_in, inverse_one, attn_gain, grad_normed_one)
    input_grad = grad_mid + through_one
    weight_parts = (grad_query, grad_key, grad_value, grad_output_t, grad_gate, grad_up, grad_down_t)
    widths = [part.shape[1] for part in weight_parts]
    gain_parts = (
        jnp.sum(attn_terms, axis=0),
        jnp.sum(query_terms, axis=(0, 1)),
        jnp.sum(key_terms, axis=(0, 1)),
        jnp.sum(ffn_terms, axis=0),
    )
    gain_sizes = [part.shape[0] for part in gain_parts]
    gain_local = jnp.concatenate(gain_parts)
    gain_pad = -gain_local.shape[0] % 1024
    tp_count = lax.axis_size("tp")
    gain_flat = ctx_scatter(
        jnp.tile(jnp.pad(gain_local, (0, gain_pad)).reshape(8, -1), (tp_count, 1)),
        tp_count,
        7,
        "tp",
    ).reshape(-1)[: gain_local.shape[0]]
    _, gains, summed = ctx_sum(
        jnp.concatenate([part.astype(jnp.bfloat16) for part in weight_parts], axis=1),
        jnp.pad(gain_flat, (0, gain_pad)).reshape(8, -1),
        place_count,
        2,
    )
    gains = gains.reshape(-1)
    offsets = [sum(widths[:k]) for k in range(len(widths) + 1)]
    shared_query, shared_key, shared_value, output_t, shared_gate, shared_up, down_t = (
        summed[:, offsets[k] : offsets[k + 1]] for k in range(len(widths))
    )
    shared_output = output_t.T
    shared_down = down_t.T
    gain_attn = gains[: gain_sizes[0]]
    gain_query = gains[gain_sizes[0] : gain_sizes[0] + gain_sizes[1]]
    gain_key = gains[gain_sizes[0] + gain_sizes[1] : gain_sizes[0] + gain_sizes[1] + gain_sizes[2]]
    gain_ffn = gains[gain_sizes[0] + gain_sizes[1] + gain_sizes[2] : sum(gain_sizes)]
    return (
        block_output,
        input_grad,
        gain_attn,
        shared_query,
        shared_key,
        shared_value,
        gain_query,
        gain_key,
        shared_output,
        gain_ffn,
        shared_gate,
        shared_up,
        shared_down,
    )


def solution(mesh):
    return jax.shard_map(
        per_device,
        mesh=mesh,
        in_specs=(
            P(("ctx", "tp"), None),
            P(),
            P(),
            P(None, "tp"),
            P(None, "tp"),
            P(None, "tp"),
            P(),
            P(),
            P("tp", None),
            P(),
            P(None, "tp"),
            P(None, "tp"),
            P("tp", None),
            P(("ctx", "tp"), None),
        ),
        out_specs=(
            P(("ctx", "tp"), None),
            P(("ctx", "tp"), None),
            P(),
            P(None, "tp"),
            P(None, "tp"),
            P(None, "tp"),
            P(),
            P(),
            P("tp", None),
            P(),
            P(None, "tp"),
            P(None, "tp"),
            P("tp", None),
        ),
        check_vma=False,
    )
```
